32 devices in a mesh: dp: 16 (over z, y, x), tensor: 2 (over core).
Axes of the slice: x: 2, y: 2, z: 4, core: 2. Of those that a mesh axis runs over, the one named last changes fastest.
Arguments:
- pixels: bfloat16 [32, 3, 240, 240], P('dp'), may hold values from -6 to 6
- patch_size: int32 [32], P('dp'), may hold values from 8 to 48, as said below
- counts: int32 [32], P('dp'), may hold values from 25 to 900, as said below
- offsets: int32 [32], P('dp'), may hold values from 0 to 900, as said below
- resize_table: bfloat16 [49, 48, 32], replicated, may hold values from -0.875 to 0.875
- pos_table: bfloat16 [31, 900, 49], replicated, may hold values from 0 to 0.29882812
- w_base: bfloat16 [768, 3072], replicated, may hold values from -0.109375 to 0.109375
- patch_bias: bfloat16 [768], replicated, may hold values from -1.75 to 1.75
- pos_base: bfloat16 [768, 49], replicated, may hold values from -3 to 3
- gain_one: bfloat16 [768], replicated, may hold values from 0.5 to 1.5
- shift_one: bfloat16 [768], replicated, may hold values from -1.75 to 1.75
- w_query: bfloat16 [768, 768], P(None, 'tensor'), may hold values from -0.21875 to 0.21875
- bias_query: bfloat16 [768], P('tensor'), may hold values from -1.75 to 1.75
- w_key: bfloat16 [768, 768], P(None, 'tensor'), may hold values from -0.21875 to 0.21875
- w_value: bfloat16 [768, 768], P(None, 'tensor'), may hold values from -0.21875 to 0.21875
- bias_value: bfloat16 [768], P('tensor'), may hold values from -1.75 to 1.75
- w_out: bfloat16 [768, 768], P('tensor'), may hold values from -0.875 to 0.875
- bias_out: bfloat16 [768], replicated, may hold values from -1.25 to 1.25
- gain_two: bfloat16 [768], replicated, may hold values from 0.5 to 1.5
- shift_two: bfloat16 [768], replicated, may hold values from -1.75 to 1.75
- w_up: bfloat16 [768, 3072], P(None, 'tensor'), may hold values from -0.21875 to 0.21875
- bias_up: bfloat16 [3072], P('tensor'), may hold values from -1.75 to 1.75
- w_down: bfloat16 [3072, 768], P('tensor'), may hold values from -0.109375 to 0.109375
- bias_down: bfloat16 [768], replicated, may hold values from -1.25 to 1.25
- cotangent: bfloat16 [16384, 768], P('dp'), may hold values from -6 to 6
Outputs:
- out: bfloat16 [16384, 768], P('dp')
- pixel_grad: float32 [32, 3, 240, 240], P('dp')
- grad_w_base: float32 [768, 3072], replicated
- grad_patch_bias: float32 [768], replicated
- grad_pos_base: float32 [768, 49], replicated
- grad_gain_one: float32 [768], replicated
- grad_shift_one: float32 [768], replicated
- grad_w_query: float32 [768, 768], P(None, 'tensor')
- grad_bias_query: float32 [768], P('tensor')
- grad_w_key: float32 [768, 768], P(None, 'tensor')
- grad_w_value: float32 [768, 768], P(None, 'tensor')
- grad_bias_value: float32 [768], P('tensor')
- grad_w_out: float32 [768, 768], P('tensor')
- grad_bias_out: float32 [768], replicated
- grad_gain_two: float32 [768], replicated
- grad_shift_two: float32 [768], replicated
- grad_w_up: float32 [768, 3072], P(None, 'tensor')
- grad_bias_up: float32 [3072], P('tensor')
- grad_w_down: float32 [3072, 768], P('tensor')
- grad_bias_down: float32 [768], replicated
The draws below stay inside these ranges and needn't reach their ends.
Inputs may be any that keep to these rules, and one draw needn't show every extreme that they name: `patch_size`: every patch size divides 240. Images 4 i to 4 i + 3 lie on two devices; on one of them the first image has patch size 8 and the second 24; every other image has a patch size from 24 to 48. counts is (240 / patch size) squared; the two images of a device hold at most 900 + 10^2 tokens together, and every pair of devices reaches that. `offsets`: A device's first image starts at row 0, its second right after the first.
All inputs are finite; a program needn't handle non-finite values.
Results may differ from the reference program's by a relative error of at most 0.015.
Values sent between devices are 32-bit elements; how exact they have to be, the bound alone decides.
A program may use at most 320 MiB of HBM per device.

```python
import math
import jax
import jax.numpy as jnp
from jax import lax

D = 768
HEADS = 12
HD = 64
FF = 3072
BASE = 32
POSG = 7
RES = 240
PMIN = 8
PLO = 24
PHI = 48
IMG_DEV = 2
GMAX = 30
TOK_DEV = 1024
IMAGES = 32
TOKENS = 16384
N_DP = 16


def image_plan(key):
    candidates = [candidate for candidate in range(PLO, PHI + 1) if RES % candidate == 0]
    light_table = jnp.array(candidates, dtype=jnp.int32)
    device_count = IMAGES // IMG_DEV
    pair_count = device_count // 2
    key_pick, key_light = jax.random.split(jax.random.fold_in(key, 11))
    heavy_slot = jax.random.randint(key_pick, (pair_count,), 0, 2)
    light_pick = jax.random.randint(key_light, (device_count, IMG_DEV), 0, len(candidates))
    light_sizes = jnp.take(light_table, light_pick)
    device_ids = jnp.arange(device_count, dtype=jnp.int32)
    heavy_dev = device_ids % 2 == jnp.repeat(heavy_slot, 2)
    heavy_sizes = jnp.array([PMIN, PLO], dtype=jnp.int32)
    patch_sides = jnp.where(heavy_dev[:, None], heavy_sizes[None, :], light_sizes)
    grid_sides = RES // patch_sides
    token_counts = grid_sides * grid_sides
    starts = jnp.concatenate([jnp.zeros((device_count, 1), jnp.int32), token_counts[:, :1]], axis=1)
    return (patch_sides.reshape(-1), token_counts.reshape(-1), starts.reshape(-1))


def draw_patch_size(key, part):
    return image_plan(key)[0]


def draw_counts(key, part):
    return image_plan(key)[1]


def draw_offsets(key, part):
    return image_plan(key)[2]


def steps_of(key, dims, shards, low, high):
    def one(dim, parts):
        draws = jax.random.uniform(jax.random.fold_in(jax.random.fold_in(key, 6), dim), (parts,), jnp.float32, low / len(shards), high / len(shards))
        return jnp.repeat(jnp.exp(draws), dims[dim] // parts).reshape((-1,) + (1,) * (len(dims) - dim - 1))

    gain = one(*shards[0])
    for cut in shards[1:]:
        gain = gain * one(*cut)
    return gain


def noise(own_key, dims, scale, limit, cuts=(), kind=jnp.bfloat16):
    drawn = scale * jax.random.normal(own_key, dims, jnp.float32)
    if cuts:
        drawn = drawn * steps_of(own_key, dims, cuts, -0.22, 0.18)
    return jnp.clip(drawn, -limit, limit).astype(kind)


def setup_inputs(seed: int = 0) -> dict:
    key_list = jax.random.split(jax.random.key(seed), 26)
    pixels = noise(key_list[0], (IMAGES, 3, RES, RES), 1.0, 6.0, ((0, 16),))
    patch_size = draw_patch_size(jax.random.fold_in(key_list[25], 71), 0)
    counts = draw_counts(jax.random.fold_in(key_list[25], 71), 0)
    offsets = draw_offsets(jax.random.fold_in(key_list[25], 71), 0)
    resize_table = noise(key_list[4], (PHI + 1, PHI, BASE), PHI ** -0.5, 0.875)
    pos_table = jnp.clip(jax.random.uniform(key_list[5], (GMAX + 1, GMAX * GMAX, POSG * POSG), jnp.float32, 0.0, 0.29882812), 0.0, 0.29882812).astype(jnp.bfloat16)
    w_base = noise(key_list[6], (D, 3 * BASE * BASE), (3 * BASE * BASE) ** -0.5, 0.109375)
    patch_bias = noise(key_list[7], (D,), 0.3, 1.75)
    pos_base = noise(key_list[8], (D, POSG * POSG), 0.5, 3.0)
    gain_one = jnp.clip(1.0 + 0.1 * jax.random.normal(key_list[9], (D,), jnp.float32), 0.5, 1.5).astype(jnp.bfloat16)
    shift_one = noise(key_list[10], (D,), 0.3, 1.75)
    w_query = noise(key_list[11], (D, D), D ** -0.5, 0.21875, ((1, 2),))
    bias_query = noise(key_list[12], (D,), 0.3, 1.75, ((0, 2),))
    w_key = noise(key_list[13], (D, D), D ** -0.5, 0.21875, ((1, 2),))
    w_value = noise(key_list[14], (D, D), D ** -0.5, 0.21875, ((1, 2),))
    bias_value = noise(key_list[15], (D,), 0.3, 1.75, ((0, 2),))
    w_out = noise(key_list[16], (D, D), (D // 16) ** -0.5, 0.875, ((0, 2),))
    bias_out = noise(key_list[17], (D,), 0.2, 1.25)
    gain_two = jnp.clip(1.0 + 0.1 * jax.random.normal(key_list[18], (D,), jnp.float32), 0.5, 1.5).astype(jnp.bfloat16)
    shift_two = noise(key_list[19], (D,), 0.3, 1.75)
    w_up = noise(key_list[20], (D, FF), D ** -0.5, 0.21875, ((1, 2),))
    bias_up = noise(key_list[21], (FF,), 0.3, 1.75, ((0, 2),))
    w_down = noise(key_list[22], (FF, D), FF ** -0.5, 0.109375, ((0, 2),))
    bias_down = noise(key_list[23], (D,), 0.2, 1.25)
    cotangent = noise(key_list[24], (TOKENS, D), 1.0, 6.0, ((0, 16),))
    return {"pixels": pixels, "patch_size": patch_size, "counts": counts, "offsets": offsets, "resize_table": resize_table, "pos_table": pos_table, "w_base": w_base, "patch_bias": patch_bias, "pos_base": pos_base, "gain_one": gain_one, "shift_one": shift_one, "w_query": w_query, "bias_query": bias_query, "w_key": w_key, "w_value": w_value, "bias_value": bias_value, "w_out": w_out, "bias_out": bias_out, "gain_two": gain_two, "shift_two": shift_two, "w_up": w_up, "bias_up": bias_up, "w_down": w_down, "bias_down": bias_down, "cotangent": cotangent}


@jax.custom_vjp
def low(v):
    return lax.optimization_barrier(v.astype(jnp.bfloat16)).astype(jnp.float32)

@jax.custom_vjp
def low_back(v):
    return v

def low_keep(v):
    return (low(v), None)

def low_pass(kept, grad):
    return (grad,)

def back_keep(v):
    return (v, None)

def back_low(kept, grad):
    return (low(grad),)
low.defvjp(low_keep, low_pass)
low_back.defvjp(back_keep, back_low)
highest = lax.Precision.HIGHEST

def product(left_side, right_side):
    return jnp.dot(left_side, right_side, precision=highest)

def rounded_both(operand):
    return low_back(low(operand))

def standardize(values):
    centered = values - lax.optimization_barrier(jnp.mean(values, axis=-1, keepdims=True))
    spread = lax.optimization_barrier(jnp.mean(centered * centered, axis=-1, keepdims=True))
    return centered * lax.rsqrt(spread + 1e-06)

def token_layout(patch_size, counts, offsets, rows_total):
    row_ids = jnp.arange(rows_total, dtype=jnp.int32)
    inside = (row_ids[:, None] >= offsets[None, :]) & (row_ids[:, None] < (offsets + counts)[None, :])
    inside_int = inside.astype(jnp.int32)
    valid_int = lax.optimization_barrier(jnp.sum(inside_int, axis=1))
    image_slots = jnp.arange(patch_size.shape[0], dtype=jnp.int32)
    image_index = lax.optimization_barrier(jnp.sum(inside_int * image_slots[None, :], axis=1))
    row_start = lax.optimization_barrier(jnp.sum(inside_int * offsets[None, :], axis=1))
    grid_sides = lax.optimization_barrier(jnp.sum(inside_int * (RES // patch_size)[None, :], axis=1)) + (1 - valid_int)
    within = (row_ids - row_start) * valid_int
    grid_row = within // grid_sides
    grid_col = within % grid_sides
    table_row = image_index * (GMAX * GMAX) + grid_row * GMAX + grid_col
    pos_row = grid_sides * (GMAX * GMAX) + within
    segment = image_index + (1 - valid_int) * patch_size.shape[0]
    return (table_row, pos_row, segment, valid_int)

def resize_matrix(kernel_table, patch_side):
    row_ids = jnp.arange(RES, dtype=jnp.int32)
    col_ids = jnp.arange(GMAX * BASE, dtype=jnp.int32)
    kernel = jnp.take(kernel_table, patch_side, axis=0)
    picked = jnp.take(kernel, row_ids % patch_side, axis=0)
    tiled_rows = jnp.tile(picked, (1, GMAX))
    same_block = (row_ids // patch_side)[:, None] == (col_ids // BASE)[None, :]
    return jnp.where(same_block, tiled_rows, jnp.zeros_like(tiled_rows))

def attend(queries, key_rows, value_rows, segment):
    row_count, head_count, head_size = queries.shape
    block_rows = min(512, row_count)
    block_count = row_count // block_rows
    score_scale = 1.0 / math.sqrt(head_size)

    def one_block(pieces):
        block_queries, block_segment = pieces
        scores = jnp.einsum('qhd,khd->hqk', block_queries, key_rows, precision=highest) * score_scale
        same_image = block_segment[:, None] == segment[None, :]
        scores = low_back(jnp.where(same_image[None, :, :], scores, -1000000000.0))
        row_max = lax.optimization_barrier(jnp.max(scores, axis=-1, keepdims=True))
        weights = jnp.exp(scores - row_max)
        attn_probs = low(weights / lax.optimization_barrier(jnp.sum(weights, axis=-1, keepdims=True)))
        return jnp.einsum('hqk,khd->qhd', attn_probs, value_rows, precision=highest)
    outputs = lax.map(jax.checkpoint(one_block), (queries.reshape(block_count, block_rows, head_count, head_size), segment.reshape(block_count, block_rows)))
    return outputs.reshape(row_count, head_count * head_size)

def layer_forward(params, pixels, layout, resize_wide, pos_wide):
    w_base, patch_bias, pos_base, gain_one, shift_one, w_query, bias_query, w_key, w_value, bias_value, w_out, bias_out, gain_two, shift_two, w_up, bias_up, w_down, bias_down = params
    patch_size, table_row, pos_row, segment, valid_rows = layout
    images = pixels.shape[0]
    row_count = table_row.shape[0]
    mixers = jax.vmap(resize_matrix, in_axes=(None, 0))(resize_wide, patch_size)
    halves = rounded_both(jnp.einsum('icrs,isg->icrg', pixels, mixers, precision=highest))
    grid_table = rounded_both(jnp.einsum('irxa,icryb->ixycab', mixers.reshape(images, RES, GMAX, BASE), halves.reshape(images, 3, RES, GMAX, BASE), precision=highest))
    grid_table = grid_table.reshape(images * GMAX * GMAX, 3 * BASE * BASE)
    base_tokens = jnp.take(grid_table, table_row, axis=0) * valid_rows[:, None]
    pos_rows = jnp.take(pos_wide.reshape(-1, POSG * POSG), pos_row, axis=0) * valid_rows[:, None]
    embedded = low_back(product(base_tokens, w_base.T) + patch_bias + product(pos_rows, pos_base.T))
    normed_one = low(standardize(embedded) * gain_one + shift_one)
    queries = rounded_both(product(normed_one, w_query) + bias_query)
    key_rows = rounded_both(product(normed_one, w_key))
    value_rows = rounded_both(product(normed_one, w_value) + bias_value)
    shaped = (row_count, HEADS, HD)
    mixed = rounded_both(attend(queries.reshape(shaped), key_rows.reshape(shaped), value_rows.reshape(shaped), segment))
    attended = low_back(product(mixed, w_out) + bias_out)
    middle = embedded + attended
    normed_two = low(standardize(middle) * gain_two + shift_two)
    hidden = low_back(product(normed_two, w_up) + bias_up)
    activated = low(jax.nn.gelu(hidden))
    branch = low_back(product(activated, w_down) + bias_down)
    return (middle + branch) * valid_rows[:, None]

def reference(pixels, patch_size, counts, offsets, resize_table, pos_table, w_base, patch_bias, pos_base, gain_one, shift_one, w_query, bias_query, w_key, w_value, bias_value, w_out, bias_out, gain_two, shift_two, w_up, bias_up, w_down, bias_down, cotangent):
    params = tuple((weight.astype(jnp.float32) for weight in (w_base, patch_bias, pos_base, gain_one, shift_one, w_query, bias_query, w_key, w_value, bias_value, w_out, bias_out, gain_two, shift_two, w_up, bias_up, w_down, bias_down)))
    resize_wide = resize_table.astype(jnp.float32)
    pos_wide = pos_table.astype(jnp.float32)
    stacked = (pixels.astype(jnp.float32).reshape(N_DP, IMG_DEV, 3, RES, RES), patch_size.reshape(N_DP, IMG_DEV), counts.reshape(N_DP, IMG_DEV), offsets.reshape(N_DP, IMG_DEV), cotangent.astype(jnp.float32).reshape(N_DP, TOK_DEV, D))

    def device_step(totals, pieces):
        device_pixels, device_patch, device_counts, device_offsets, device_cotangent = pieces
        table_row, pos_row, segment, valid_int = token_layout(device_patch, device_counts, device_offsets, TOK_DEV)
        layout = (device_patch, table_row, pos_row, segment, valid_int.astype(jnp.float32))

        def local_layer(weights, image_pixels):
            return layer_forward(weights, image_pixels, layout, resize_wide, pos_wide)
        result, pullback = jax.vjp(local_layer, params, device_pixels)
        weight_grads, image_grads = pullback(device_cotangent)
        totals = tuple((summed_grad + device_grad for summed_grad, device_grad in zip(totals, weight_grads)))
        return (totals, (result.astype(jnp.bfloat16), image_grads))
    zero_grads = tuple((jnp.zeros_like(weight) for weight in params))
    totals, (outputs, image_grads) = lax.scan(device_step, zero_grads, stacked)
    mean_grads = tuple((summed_grad / N_DP for summed_grad in totals))
    return (outputs.reshape(TOKENS, D), image_grads.reshape(IMAGES, 3, RES, RES), mean_grads[0], mean_grads[1], mean_grads[2], mean_grads[3], mean_grads[4], mean_grads[5], mean_grads[6], mean_grads[7], mean_grads[8], mean_grads[9], mean_grads[10], mean_grads[11], mean_grads[12], mean_grads[13], mean_grads[14], mean_grads[15], mean_grads[16], mean_grads[17])
```

```python
import functools
import math

import jax
import jax.numpy as jnp
from jax import lax
from jax.experimental import pallas as pl
from jax.experimental.pallas import tpu as pltpu
from jax.sharding import PartitionSpec as P

HD = 64
BASE = 32
RES = 240
GMAX = 30


def standardize(values):
    centered = values - jnp.mean(values, axis=-1, keepdims=True)
    spread = jnp.mean(centered * centered, axis=-1, keepdims=True)
    return centered * lax.rsqrt(spread + 1e-06)


def token_layout(patch_size, counts, offsets, rows_total):
    row_ids = jnp.arange(rows_total, dtype=jnp.int32)
    inside = (row_ids[:, None] >= offsets[None, :]) & (
        row_ids[:, None] < (offsets + counts)[None, :]
    )
    inside_int = inside.astype(jnp.int32)
    valid_int = jnp.sum(inside_int, axis=1)
    image_slots = jnp.arange(patch_size.shape[0], dtype=jnp.int32)
    image_index = jnp.sum(inside_int * image_slots[None, :], axis=1)
    row_start = jnp.sum(inside_int * offsets[None, :], axis=1)
    grid_sides = jnp.sum(inside_int * (RES // patch_size)[None, :], axis=1) + (1 - valid_int)
    within = (row_ids - row_start) * valid_int
    grid_row = within // grid_sides
    grid_col = within % grid_sides
    table_row = image_index * (GMAX * GMAX) + grid_row * GMAX + grid_col
    pos_row = grid_sides * (GMAX * GMAX) + within
    segment = image_index + (1 - valid_int) * patch_size.shape[0]
    return (table_row, pos_row, segment, valid_int)


def resize_matrix(kernel_table, patch_side):
    row_ids = jnp.arange(RES, dtype=jnp.int32)
    col_ids = jnp.arange(GMAX * BASE, dtype=jnp.int32)
    kernel = jnp.take(kernel_table, patch_side, axis=0)
    picked = jnp.take(kernel, row_ids % patch_side, axis=0)
    tiled_rows = jnp.tile(picked, (1, GMAX))
    same_block = (row_ids // patch_side)[:, None] == (col_ids // BASE)[None, :]
    return jnp.where(same_block, tiled_rows, jnp.zeros_like(tiled_rows))


LINE = 4
MESH_ID = pl.DeviceIdType.MESH


def sync_kernel(pieces, scale, in_count, out_count, *refs):
    grads = refs[:in_count]
    outs = refs[in_count : in_count + out_count]
    acc, land, land_right, land_left, land_last, sems = refs[in_count + out_count :]
    device = lax.axis_index("dp")
    core = lax.axis_index("tensor")
    place_x = lax.rem(device, 2)
    place_y = lax.rem(device // 2, 2)
    place_z = lax.rem(device // 4, LINE)
    beside = {"x": device + 1 - 2 * place_x, "y": device + 2 - 4 * place_y}
    bits = {"x": place_x, "y": place_y}
    up = device + 4
    down = device - 4

    barrier = pltpu.get_barrier_semaphore()
    for partner in (beside["x"], beside["y"]):
        pl.semaphore_signal(barrier, inc=1, device_id=(partner, core), device_id_type=MESH_ID)
    pl.semaphore_signal(barrier, inc=1, device_id=(device, 1 - core), device_id_type=MESH_ID)

    @pl.when(place_z < LINE - 1)
    def _():
        pl.semaphore_signal(barrier, inc=1, device_id=(up, core), device_id_type=MESH_ID)

    @pl.when(place_z > 0)
    def _():
        pl.semaphore_signal(barrier, inc=1, device_id=(down, core), device_id_type=MESH_ID)

    inner = (place_z + LINE - 1) // LINE + (2 * (LINE - 1) - place_z) // LINE
    pl.semaphore_wait(barrier, 3 + inner)

    def rows_at(ref, start, size, column, width):
        return ref.at[pl.ds(pl.multiple_of(start, 8), size), pl.ds(column, width)]

    def remote(src, dst, send, recv, where):
        return pltpu.make_async_remote_copy(
            src_ref=src,
            dst_ref=dst,
            send_sem=send,
            recv_sem=recv,
            device_id=where,
            device_id_type=MESH_ID,
        )

    def add_rows(total, start, extra, size, width, factor=None):
        step = 24 if size % 24 == 0 else 8

        @pl.loop(0, size // step)
        def _(i):
            here = pl.ds(pl.multiple_of(start + i * step, 8), step)
            there = pl.ds(pl.multiple_of(i * step, 8), step)
            value = total[here, :width] + extra[there, :width]
            total[here, :width] = value if factor is None else value * factor

    def build(number, piece):
        source, in_row, in_col, target, out_row, out_col, rows, width, first = piece
        second = "y" if first == "x" else "x"
        half, chunk, share = rows // 2, rows // 8, rows // 16
        grad, out = grads[source], outs[target]
        own, other = bits[first], bits[second]
        mine = acc.at[number]
        sem = lambda k: sems.at[number, k]
        base_row = out_row + core * rows if piece_swaps(piece) else out_row
        half_row = base_row + own * half

        def first_copy():
            return remote(
                rows_at(grad, in_row + (1 - own) * half, half, in_col, width),
                land.at[number, :half, :width],
                sem(0),
                sem(1),
                (beside[first], core),
            )

        def load():
            return pltpu.make_async_copy(
                rows_at(grad, in_row + own * half, half, in_col, width),
                mine.at[:half, :width],
                sem(2),
            )

        def right(k):
            return remote(
                rows_at(mine, (LINE - k + place_z) * chunk, chunk, 0, width),
                land_right.at[number, k - 1, :chunk, :width],
                sem(2 + k),
                sem(5 + k),
                (up, core),
            )

        def left(k):
            return remote(
                rows_at(mine, (k - 1 - (LINE - 1 - place_z)) * chunk, chunk, 0, width),
                land_left.at[number, k - 1, :chunk, :width],
                sem(8 + k),
                sem(11 + k),
                (down, core),
            )

        def got_right(k):
            return remote(
                land_right.at[number, k - 1, :chunk, :width],
                land_right.at[number, k - 1, :chunk, :width],
                sem(2 + k),
                sem(5 + k),
                (down, core),
            )

        def got_left(k):
            return remote(
                land_left.at[number, k - 1, :chunk, :width],
                land_left.at[number, k - 1, :chunk, :width],
                sem(8 + k),
                sem(11 + k),
                (up, core),
            )

        mirror = LINE - 1 - place_z

        def send_line(k):
            @pl.when((place_z <= k - 1) & (place_z < LINE - 1))
            def _():
                right(k).start()

            @pl.when((mirror <= k - 1) & (mirror < LINE - 1))
            def _():
                left(k).start()

        def wait_line(k):
            @pl.when((place_z >= 1) & (place_z <= k))
            def _():
                got_right(k).wait_recv()
                add_rows(
                    mine, (LINE - 1 - k + place_z) * chunk, land_right.at[number, k - 1], chunk, width
                )

            @pl.when((mirror >= 1) & (mirror <= k))
            def _():
                got_left(k).wait_recv()
                add_rows(mine, (k - mirror) * chunk, land_left.at[number, k - 1], chunk, width)

        def last_copy():
            return remote(
                rows_at(mine, place_z * chunk + (1 - other) * share, share, 0, width),
                land_last.at[number, :share, :width],
                sem(15),
                sem(16),
                (beside[second], core),
            )

        share_row = half_row + place_z * chunk + other * share

        def share_out():
            return remote(
                rows_at(mine, place_z * chunk + other * share, share, 0, width),
                rows_at(out, share_row, share, out_col, width),
                sem(17),
                sem(18),
                (beside[second], core),
            )

        def share_in():
            return remote(
                rows_at(mine, place_z * chunk + other * share, share, 0, width),
                rows_at(out, half_row + place_z * chunk + (1 - other) * share, share, out_col, width),
                sem(17),
                sem(18),
                (beside[second], core),
            )

        def share_store():
            return pltpu.make_async_copy(
                rows_at(mine, place_z * chunk + other * share, share, 0, width),
                rows_at(out, share_row, share, out_col, width),
                sem(19),
            )

        def chunk_out(position):
            return rows_at(out, half_row + position * chunk, chunk, out_col, width)

        def spread_right(k, position, where):
            return remote(
                chunk_out(position), chunk_out(position), sem(19 + k), sem(22 + k), (where, core)
            )

        def spread_left(k, position, where):
            return remote(
                chunk_out(position), chunk_out(position), sem(25 + k), sem(28 + k), (where, core)
            )

        def send_spread(k):
            @pl.when((place_z >= k - 1) & (place_z < LINE - 1))
            def _():
                spread_right(k, place_z - (k - 1), up).start()

            @pl.when((mirror >= k - 1) & (mirror < LINE - 1))
            def _():
                spread_left(k, place_z + (k - 1), down).start()

        def wait_spread(k):
            @pl.when(place_z >= k)
            def _():
                spread_right(k, place_z - k, down).wait_recv()

            @pl.when(mirror >= k)
            def _():
                spread_left(k, place_z + k, up).wait_recv()

        def half_out():
            here = rows_at(out, half_row, half, out_col, width)
            return remote(here, here, sem(32), sem(33), (beside[first], core))

        def half_in():
            there = rows_at(out, base_row + (1 - own) * half, half, out_col, width)
            return remote(there, there, sem(32), sem(33), (beside[first], core))

        def swap_out():
            here = rows_at(out, base_row, rows, out_col, width)
            return remote(here, here, sem(34), sem(35), (device, 1 - core))

        def swap_in():
            there = rows_at(out, out_row + (1 - core) * rows, rows, out_col, width)
            return remote(there, there, sem(34), sem(35), (device, 1 - core))

        def stage_0():
            first_copy().start()
            load().start()

        def stage_1():
            load().wait()
            first_copy().wait_recv()
            add_rows(mine, 0, land.at[number], half, width)
            send_line(1)

        def stage_2():
            wait_line(1)
            send_line(2)

        def stage_3():
            wait_line(2)
            send_line(3)

        def stage_4():
            wait_line(3)
            last_copy().start()

        def stage_5():
            last_copy().wait()
            add_rows(
                mine, place_z * chunk + other * share, land_last.at[number], share, width, scale
            )
            share_out().start()
            share_store().start()

        def stage_6():
            share_store().wait()
            share_in().wait_recv()
            send_spread(1)

        def stage_7():
            wait_spread(1)
            send_spread(2)

        def stage_8():
            wait_spread(2)
            send_spread(3)

        def stage_9():
            wait_spread(3)
            half_out().start()

        def stage_10():
            half_in().wait_recv()
            if piece_swaps(piece):
                swap_out().start()

        def stage_11():
            if piece_swaps(piece):
                swap_in().wait_recv()
                swap_out().wait_send()
            first_copy().wait_send()
            share_out().wait_send()
            half_out().wait_send()
            for k in range(1, LINE):

                @pl.when((place_z <= k - 1) & (place_z < LINE - 1))
                def _():
                    right(k).wait_send()

                @pl.when((mirror <= k - 1) & (mirror < LINE - 1))
                def _():
                    left(k).wait_send()

                @pl.when((place_z >= k - 1) & (place_z < LINE - 1))
                def _():
                    spread_right(k, place_z - (k - 1), up).wait_send()

                @pl.when((mirror >= k - 1) & (mirror < LINE - 1))
                def _():
                    spread_left(k, place_z + (k - 1), down).wait_send()

        return [
            stage_0,
            stage_1,
            stage_2,
            stage_3,
            stage_4,
            stage_5,
            stage_6,
            stage_7,
            stage_8,
            stage_9,
            stage_10,
            stage_11,
        ]

    lines = [build(number, piece) for number, piece in enumerate(pieces)]
    pairs = [lines[i : i + 2] for i in range(0, len(lines), 2)]
    depth = len(lines[0])
    ahead = 1
    for j in range(ahead):
        for line in pairs[j]:
            line[0]()
    for tick in range(len(pairs) + depth - 1):
        if tick + ahead < len(pairs):
            for line in pairs[tick + ahead]:
                line[0]()
        for j in range(max(0, tick - depth + 1), min(tick, len(pairs))):
            for line in pairs[j]:
                line[tick - j]()


def piece_swaps(piece):
    return piece[3] == SWAPPED


SWAPPED = 0
PIECE_ROWS = 384
PIECE_COLS = 768


def sync_plan(in_shapes, out_shapes, out_of):
    pieces = []
    for source, shape in enumerate(in_shapes):
        targets = out_of[source]
        col_of_source = 0
        for target in targets:
            cols = out_shapes[target][1]
            rows = shape[0]
            tall = min(PIECE_ROWS, rows)
            wide = min(PIECE_COLS, cols)
            for row in range(0, rows, tall):
                for col in range(0, cols, wide):
                    pieces.append([source, row, col_of_source + col, target, row, col, tall, wide])
            col_of_source += cols
    return [tuple(piece) + ("xy"[i % 2],) for i, piece in enumerate(pieces)]


def sync_grads(grads, out_shapes, out_of, replicas):
    pieces = sync_plan([g.shape for g in grads], out_shapes, out_of)
    count = len(pieces)
    high = max(p[6] for p in pieces)
    wide = max(p[7] for p in pieces)
    kernel = functools.partial(
        sync_kernel, pieces, 1.0 / replicas, len(grads), len(out_shapes)
    )
    vmem = lambda *dims: pltpu.VMEM(dims, jnp.float32)
    return pl.pallas_call(
        kernel,
        out_shape=[jax.ShapeDtypeStruct(s, jnp.float32) for s in out_shapes],
        in_specs=[pl.BlockSpec(memory_space=pl.ANY)] * len(grads),
        out_specs=[pl.BlockSpec(memory_space=pl.ANY)] * len(out_shapes),
        scratch_shapes=[
            vmem(count, high // 2, wide),
            vmem(count, high // 2, wide),
            vmem(count, LINE - 1, high // 8, wide),
            vmem(count, LINE - 1, high // 8, wide),
            vmem(count, high // 16, wide),
            pltpu.SemaphoreType.DMA((count, 36)),
        ],
        compiler_params=pltpu.CompilerParams(
            collective_id=0, has_side_effects=True, vmem_limit_bytes=56 << 20
        ),
        name="sync_grads",
    )(*grads)


def tensor_sum(partial):
    return partial + lax.ppermute(partial, "tensor", [(0, 1), (1, 0)])


def masked_scores(block_queries, block_segment, key_rows, segment):
    score_scale = 1.0 / math.sqrt(block_queries.shape[-1])
    scores = (
        jnp.einsum("qhd,khd->hqk", block_queries, key_rows, preferred_element_type=jnp.float32)
        * score_scale
    )
    same_image = block_segment[:, None] == segment[None, :]
    return jnp.where(same_image[None, :, :], scores, -1000000000.0)


def attention_forward(queries, key_rows, value_rows, segment, block_rows):
    row_count, head_count, head_size = queries.shape
    block_count = row_count // block_rows

    def one_block(pieces):
        block_queries, block_segment = pieces
        scores = masked_scores(block_queries, block_segment, key_rows, segment)
        row_max = jnp.max(scores, axis=-1, keepdims=True)
        weights = jnp.exp(scores - row_max)
        row_total = jnp.sum(weights, axis=-1, keepdims=True)
        probs_low = (weights / row_total).astype(jnp.bfloat16)
        output = jnp.einsum(
            "hqk,khd->qhd", probs_low, value_rows, preferred_element_type=jnp.float32
        )
        return (output, (row_max + jnp.log(row_total))[:, :, 0])

    outputs, log_totals = lax.map(
        one_block,
        (
            queries.reshape(block_count, block_rows, head_count, head_size),
            segment.reshape(block_count, block_rows),
        ),
    )
    return (outputs.reshape(row_count, head_count * head_size), log_totals)


def attention_backward(queries, key_rows, value_rows, segment, log_totals, grad_mixed, block_rows):
    row_count, head_count, head_size = queries.shape
    block_count = row_count // block_rows
    score_scale = 1.0 / math.sqrt(head_size)

    def one_block(carried, pieces):
        grad_keys, grad_values = carried
        block_queries, block_segment, block_grad, block_log = pieces
        scores = masked_scores(block_queries, block_segment, key_rows, segment)
        attn_probs = jnp.exp(scores - block_log[:, :, None])
        grad_probs = jnp.einsum(
            "qhd,khd->hqk", block_grad, value_rows, preferred_element_type=jnp.float32
        )
        inner_sum = jnp.sum(attn_probs * grad_probs, axis=-1, keepdims=True)
        grad_scores = (attn_probs * (grad_probs - inner_sum)).astype(jnp.bfloat16)
        grad_queries = (
            jnp.einsum("hqk,khd->qhd", grad_scores, key_rows, preferred_element_type=jnp.float32)
            * score_scale
        )
        grad_keys = (
            grad_keys
            + jnp.einsum(
                "hqk,qhd->khd", grad_scores, block_queries, preferred_element_type=jnp.float32
            )
            * score_scale
        )
        grad_values = grad_values + jnp.einsum(
            "hqk,qhd->khd",
            attn_probs.astype(jnp.bfloat16),
            block_grad,
            preferred_element_type=jnp.float32,
        )
        return ((grad_keys, grad_values), grad_queries)

    zero_rows = jnp.zeros((row_count, head_count, head_size), jnp.float32)
    shaped = (block_count, block_rows, head_count, head_size)
    (grad_keys, grad_values), grad_queries = lax.scan(
        one_block,
        (zero_rows, zero_rows),
        (
            queries.reshape(shaped),
            segment.reshape(block_count, block_rows),
            grad_mixed.reshape(shaped),
            log_totals,
        ),
    )
    return (
        grad_queries.reshape(row_count, head_count * head_size),
        grad_keys.reshape(row_count, head_count * head_size),
        grad_values.reshape(row_count, head_count * head_size),
    )


def local(
    pixels,
    patch_size,
    counts,
    offsets,
    resize_table,
    pos_table,
    w_base,
    patch_bias,
    pos_base,
    gain_one,
    shift_one,
    w_query,
    bias_query,
    w_key,
    w_value,
    bias_value,
    w_out,
    bias_out,
    gain_two,
    shift_two,
    w_up,
    bias_up,
    w_down,
    bias_down,
    cotangent,
):
    rows_total = cotangent.shape[0]
    images = pixels.shape[0]
    block_rows = min(512, rows_total)
    heads_local = w_query.shape[1] // HD
    table_row, pos_row, segment, valid_int = token_layout(patch_size, counts, offsets, rows_total)
    valid_rows = valid_int.astype(jnp.float32)[:, None]
    valid_low = valid_rows.astype(jnp.bfloat16)
    mixers = jax.vmap(resize_matrix, in_axes=(None, 0))(resize_table, patch_size)
    mixer_grid = mixers.reshape(images, RES, GMAX, BASE)
    halves = jnp.einsum(
        "icrs,isg->icrg", pixels, mixers, preferred_element_type=jnp.float32
    ).astype(jnp.bfloat16)
    grid_table = jnp.einsum(
        "irxa,icryb->ixycab",
        mixer_grid,
        halves.reshape(images, 3, RES, GMAX, BASE),
        preferred_element_type=jnp.float32,
    ).astype(jnp.bfloat16)
    grid_table = grid_table.reshape(images * GMAX * GMAX, 3 * BASE * BASE)
    base_tokens = jnp.take(grid_table, table_row, axis=0) * valid_low
    pos_rows = jnp.take(pos_table.reshape(-1, pos_table.shape[2]), pos_row, axis=0) * valid_low
    embedded = (
        jnp.einsum("tf,df->td", base_tokens, w_base, preferred_element_type=jnp.float32)
        + patch_bias.astype(jnp.float32)
        + jnp.einsum("tp,dp->td", pos_rows, pos_base, preferred_element_type=jnp.float32)
    )
    standard_one, standard_back_one = jax.vjp(standardize, embedded)
    normed_one = (
        standard_one * gain_one.astype(jnp.float32) + shift_one.astype(jnp.float32)
    ).astype(jnp.bfloat16)
    queries = (
        jnp.dot(normed_one, w_query, preferred_element_type=jnp.float32)
        + bias_query.astype(jnp.float32)
    ).astype(jnp.bfloat16)
    key_rows = jnp.dot(normed_one, w_key, preferred_element_type=jnp.float32).astype(jnp.bfloat16)
    value_rows = (
        jnp.dot(normed_one, w_value, preferred_element_type=jnp.float32)
        + bias_value.astype(jnp.float32)
    ).astype(jnp.bfloat16)
    shaped = (rows_total, heads_local, HD)
    mixed_wide, log_totals = attention_forward(
        queries.reshape(shaped),
        key_rows.reshape(shaped),
        value_rows.reshape(shaped),
        segment,
        block_rows,
    )
    mixed = mixed_wide.astype(jnp.bfloat16)
    attended = tensor_sum(
        jnp.dot(mixed, w_out, preferred_element_type=jnp.float32)
    ) + bias_out.astype(jnp.float32)
    middle = embedded + attended
    standard_two, standard_back_two = jax.vjp(standardize, middle)
    normed_two = (
        standard_two * gain_two.astype(jnp.float32) + shift_two.astype(jnp.float32)
    ).astype(jnp.bfloat16)
    hidden = jnp.dot(normed_two, w_up, preferred_element_type=jnp.float32) + bias_up.astype(
        jnp.float32
    )
    activated_wide, gelu_back = jax.vjp(jax.nn.gelu, hidden)
    activated = activated_wide.astype(jnp.bfloat16)
    branch = tensor_sum(
        jnp.dot(activated, w_down, preferred_element_type=jnp.float32)
    ) + bias_down.astype(jnp.float32)
    output = ((middle + branch) * valid_rows).astype(jnp.bfloat16)
    grad_out = cotangent.astype(jnp.float32) * valid_rows
    grad_branch = grad_out.astype(jnp.bfloat16)
    grad_w_down = jnp.einsum(
        "tf,td->fd", activated, grad_branch, preferred_element_type=jnp.float32
    )
    grad_activated = jnp.einsum(
        "td,fd->tf", grad_branch, w_down, preferred_element_type=jnp.float32
    )
    grad_hidden = gelu_back(grad_activated)[0].astype(jnp.bfloat16)
    grad_w_up = jnp.einsum("td,tf->df", normed_two, grad_hidden, preferred_element_type=jnp.float32)
    grad_bias_up = jnp.sum(grad_hidden, axis=0, dtype=jnp.float32)
    grad_normed_two = tensor_sum(
        jnp.einsum("tf,df->td", grad_hidden, w_up, preferred_element_type=jnp.float32)
    )
    grad_middle = grad_out + standard_back_two(grad_normed_two * gain_two.astype(jnp.float32))[0]
    grad_attended = grad_middle.astype(jnp.bfloat16)
    grad_w_out = jnp.einsum("te,td->ed", mixed, grad_attended, preferred_element_type=jnp.float32)
    grad_mixed = jnp.einsum(
        "td,ed->te", grad_attended, w_out, preferred_element_type=jnp.float32
    ).astype(jnp.bfloat16)
    grad_q_wide, grad_k_wide, grad_v_wide = attention_backward(
        queries.reshape(shaped),
        key_rows.reshape(shaped),
        value_rows.reshape(shaped),
        segment,
        log_totals,
        grad_mixed.reshape(shaped),
        block_rows,
    )
    grad_queries = grad_q_wide.astype(jnp.bfloat16)
    grad_keys = grad_k_wide.astype(jnp.bfloat16)
    grad_values = grad_v_wide.astype(jnp.bfloat16)
    grad_qkv = jnp.concatenate([grad_queries, grad_keys, grad_values], axis=1)
    grad_w_qkv = jnp.einsum("td,te->de", normed_one, grad_qkv, preferred_element_type=jnp.float32)
    grad_bias_query = jnp.sum(grad_queries, axis=0, dtype=jnp.float32)
    grad_bias_value = jnp.sum(grad_values, axis=0, dtype=jnp.float32)
    back_terms = (
        jnp.einsum("te,de->td", grad_queries, w_query, preferred_element_type=jnp.float32)
        + jnp.einsum("te,de->td", grad_keys, w_key, preferred_element_type=jnp.float32)
        + jnp.einsum("te,de->td", grad_values, w_value, preferred_element_type=jnp.float32)
    )
    grad_normed_one = tensor_sum(back_terms)
    grad_embedded = (
        grad_middle + standard_back_one(grad_normed_one * gain_one.astype(jnp.float32))[0]
    )
    grad_embedded_low = grad_embedded.astype(jnp.bfloat16)
    grad_tokens = (
        jnp.einsum("td,df->tf", grad_embedded_low, w_base, preferred_element_type=jnp.float32)
        * valid_rows
    )
    grad_table = (
        jnp.zeros((images * GMAX * GMAX, 3 * BASE * BASE), jnp.float32)
        .at[table_row]
        .add(grad_tokens)
        .astype(jnp.bfloat16)
    )
    grad_half = jnp.einsum(
        "irxa,ixycab->icryb",
        mixer_grid,
        grad_table.reshape(images, GMAX, GMAX, 3, BASE, BASE),
        preferred_element_type=jnp.float32,
    ).astype(jnp.bfloat16)
    pixel_grad = jnp.einsum(
        "icrg,isg->icrs",
        grad_half.reshape(images, 3, RES, GMAX * BASE),
        mixers,
        preferred_element_type=jnp.float32,
    )
    replicas = lax.axis_size("dp")
    core = lax.axis_index("tensor")
    half_width = grad_embedded_low.shape[1] // 2
    grad_embedded_half = lax.dynamic_slice_in_dim(
        grad_embedded_low, core * half_width, half_width, axis=1
    )
    grad_w_base = jnp.einsum(
        "td,tf->df", grad_embedded_half, base_tokens, preferred_element_type=jnp.float32
    )
    grad_patch_bias = jnp.sum(grad_embedded_low, axis=0, dtype=jnp.float32)
    grad_pos_base = jnp.einsum(
        "td,tp->pd", grad_embedded_low, pos_rows, preferred_element_type=jnp.float32
    )
    grad_gain_one = jnp.sum(grad_normed_one * standard_one, axis=0)
    grad_shift_one = jnp.sum(grad_normed_one, axis=0)
    grad_bias_out = jnp.sum(grad_attended, axis=0, dtype=jnp.float32)
    grad_gain_two = jnp.sum(grad_normed_two * standard_two, axis=0)
    grad_shift_two = jnp.sum(grad_normed_two, axis=0)
    grad_bias_down = jnp.sum(grad_branch, axis=0, dtype=jnp.float32)
    width = grad_patch_bias.shape[0]
    small_rows = [
        grad_pos_base,
        grad_patch_bias[None],
        grad_gain_one[None],
        grad_shift_one[None],
        grad_bias_out[None],
        grad_gain_two[None],
        grad_shift_two[None],
        grad_bias_down[None],
        jnp.concatenate([grad_bias_query, grad_bias_value])[None],
        grad_bias_up.reshape(-1, width),
    ]
    small = jnp.concatenate(small_rows, axis=0)
    used = small.shape[0]
    small = jnp.pad(small, ((0, -used % 128), (0, 0)))
    parts = [grad_w_down, grad_w_up, grad_w_qkv, grad_w_base, grad_w_out, small]
    beyond = replicas // 16
    step = 1
    while step < beyond:
        swap = [(i, (i // 16 ^ step) * 16 + i % 16) for i in range(replicas)]
        parts = [part + lax.ppermute(part, "dp", swap) for part in parts]
        step *= 2
    out_shapes = [
        (2 * grad_w_base.shape[0], grad_w_base.shape[1]),
        grad_w_down.shape,
        grad_w_up.shape,
        w_query.shape,
        w_key.shape,
        w_value.shape,
        grad_w_out.shape,
        small.shape,
    ]
    synced = sync_grads(parts, out_shapes, [[1], [2], [3, 4, 5], [0], [6], [7]], replicas)
    base_s, down_s, up_s, query_s, key_s, value_s, out_s, small_s = synced
    points = pos_rows.shape[1]
    row = lambda k: small_s[points + k]
    cut = grad_bias_query.shape[0]
    return (
        output,
        pixel_grad,
        base_s,
        row(0),
        small_s[:points].T,
        row(1),
        row(2),
        query_s,
        row(7)[:cut],
        key_s,
        value_s,
        row(7)[cut:],
        out_s,
        row(3),
        row(4),
        row(5),
        up_s,
        small_s[points + 8 : used].reshape(-1),
        down_s,
        row(6),
    )


def solution(mesh):
    in_specs = (
        P("dp", None, None, None),
        P("dp"),
        P("dp"),
        P("dp"),
        P(),
        P(),
        P(),
        P(),
        P(),
        P(),
        P(),
        P(None, "tensor"),
        P("tensor"),
        P(None, "tensor"),
        P(None, "tensor"),
        P("tensor"),
        P("tensor", None),
        P(),
        P(),
        P(),
        P(None, "tensor"),
        P("tensor"),
        P("tensor", None),
        P(),
        P("dp", None),
    )
    out_specs = (
        P("dp", None),
        P("dp", None, None, None),
        P(),
        P(),
        P(),
        P(),
        P(),
        P(None, "tensor"),
        P("tensor"),
        P(None, "tensor"),
        P(None, "tensor"),
        P("tensor"),
        P("tensor", None),
        P(),
        P(),
        P(),
        P(None, "tensor"),
        P("tensor"),
        P("tensor", None),
        P(),
    )
    return jax.shard_map(local, mesh=mesh, in_specs=in_specs, out_specs=out_specs, check_vma=False)
```

```python
import functools
import math

import jax
import jax.numpy as jnp
from jax import lax
from jax.experimental import pallas as pl
from jax.experimental.pallas import tpu as pltpu
from jax.sharding import PartitionSpec as P

HD = 64
VMEM = pl.BlockSpec(memory_space=pltpu.VMEM)
SMEM = pl.BlockSpec(memory_space=pltpu.SMEM)


def standardize(values):
    centered = values - jnp.mean(values, axis=-1, keepdims=True)
    spread = jnp.mean(centered * centered, axis=-1, keepdims=True)
    return centered * lax.rsqrt(spread + 1e-06)


def row_segments(counts, offsets, rows_total):
    row_ids = jnp.arange(rows_total, dtype=jnp.int32)
    inside = (row_ids[:, None] >= offsets[None, :]) & (
        row_ids[:, None] < (offsets + counts)[None, :]
    )
    inside_int = inside.astype(jnp.int32)
    valid_int = jnp.sum(inside_int, axis=1)
    image_slots = jnp.arange(counts.shape[0], dtype=jnp.int32)
    image_index = jnp.sum(inside_int * image_slots[None, :], axis=1)
    return image_index + (1 - valid_int) * counts.shape[0], valid_int


SIDES = (8, 24, 30, 40, 48)
FINE = 8


def spread_tables(table, side, base):
    entry = lax.broadcasted_iota(jnp.int32, (base, base * base), 0)
    place = lax.broadcasted_iota(jnp.int32, (base, base * base), 1)
    repeat = (place // base == entry).astype(jnp.bfloat16)
    tile = (place % base == entry).astype(jnp.bfloat16)
    wide = jnp.dot(table, repeat, preferred_element_type=jnp.float32)
    long = jnp.dot(table, tile, preferred_element_type=jnp.float32)
    return wide[:side], long[:side]


def fill_pairs(pair_ref, table, side, base):
    wide, long = spread_tables(table, side, base)
    for s in range(side):
        pair_ref[s * side : (s + 1) * side, :] = wide * long[s : s + 1]


def nt(left, right):
    return lax.dot_general(left, right, (((1,), (1,)), ((), ())), preferred_element_type=jnp.float32)


def tn(left, right):
    return lax.dot_general(left, right, (((0,), (0,)), ((), ())), preferred_element_type=jnp.float32)


def nn(left, right):
    return jnp.dot(left, right, preferred_element_type=jnp.float32)


def embed_kernel(
    sizes, pix, table, pos, weight, bias, pos_base, emb, tokens, patches, mixed_weight, line, pair, half_emb
):
    base = table.shape[2]
    area = base * base
    res = pix.shape[2]
    channels = pix.shape[1]

    @pl.loop(0, 2)
    def _(slot):
        for side in SIDES:
            grid = res // side
            count = grid * grid

            @pl.when(sizes[slot] == side)
            def _():
                fill_pairs(pair, table[slot], side, base)
                pairs = pair[: side * side, :].astype(jnp.bfloat16)
                total = nt(pos[slot, :count, :], pos_base[...]) + bias[...]
                for c in range(channels):
                    for x in range(grid):
                        block = pix[slot, c, x * side : (x + 1) * side, :]
                        line[x * res : (x + 1) * res, :side] = block.T[:res]
                    patch = jnp.concatenate(
                        [line[pl.ds(s, count, stride=side), :side] for s in range(side)], axis=1
                    ).astype(jnp.bfloat16)
                    columns = slice(c * area, (c + 1) * area)
                    if side == FINE:
                        span = slice(c * side * side, (c + 1) * side * side)
                        mixed = nt(pairs, weight[:, columns]).astype(jnp.bfloat16)
                        mixed_weight[span, :] = mixed
                        patches[:count, span] = patch
                        total += nn(patch, mixed)
                    else:
                        token = nn(patch, pairs).astype(jnp.bfloat16)
                        tokens[slot, :count, columns] = token
                        total += nt(token, weight[:, columns])
                half_emb[slot, :count, :] = total

    for side in SIDES:
        count = (res // side) ** 2

        @pl.when(sizes[0] == side)
        def _():
            tail = emb.shape[0] - count
            emb[:count, :] = half_emb[0, :count, :]
            emb[count:, :] = jnp.broadcast_to(bias[...], (tail, emb.shape[1]))
            for second in SIDES[1:]:
                more = (res // second) ** 2

                @pl.when(sizes[1] == second)
                def _():
                    emb[count : count + more, :] = half_emb[1, :more, :]


def pixel_kernel(
    sizes, grad, table, pos, weight, tokens, patches, mixed_weight, core_ref,
    pixel_grad, grad_weight, grad_pos, line, pair, rows_ref
):
    base = table.shape[2]
    area = base * base
    res = pixel_grad.shape[2]
    channels = pixel_grad.shape[1]
    half = grad_weight.shape[0]
    mine = pl.multiple_of(core_ref[0] * half, 128)
    low = jnp.bfloat16

    big = (res // FINE) ** 2
    rows_ref[0, :big, :] = grad[:big, :]
    most = (res // SIDES[1]) ** 2
    for side in SIDES:
        count = (res // side) ** 2

        @pl.when(sizes[0] == side)
        def _():
            rows_ref[1, :most, :] = grad[count : count + most, :]

    grad_weight[...] = jnp.zeros_like(grad_weight)
    grad_pos[...] = jnp.zeros_like(grad_pos)

    @pl.loop(0, 2)
    def _(slot):
        for side in SIDES:
            grid = res // side
            count = grid * grid

            @pl.when(sizes[slot] == side)
            def _():
                fill_pairs(pair, table[slot], side, base)
                pairs = pair[: side * side, :].astype(low)
                rows = rows_ref[slot, :count, :].astype(low)
                part = rows_ref[slot, :count, pl.ds(mine, half)].astype(low)
                grad_pos[...] += tn(pos[slot, :count, :], rows)
                for c in range(channels):
                    columns = slice(c * area, (c + 1) * area)
                    if side == FINE:
                        span = slice(c * side * side, (c + 1) * side * side)
                        patch = nt(rows, mixed_weight[span, :])
                        gathered = tn(patches[:count, span], part).astype(low)
                        grad_weight[:, columns] += tn(gathered, pairs)
                    else:
                        token = nn(rows, weight[:, columns]).astype(low)
                        patch = nt(token, pairs)
                        grad_weight[:, columns] += tn(part, tokens[slot, :count, columns])
                    for s in range(side):
                        line[pl.ds(s, count, stride=side), :side] = patch[
                            :, s * side : (s + 1) * side
                        ]
                    for x in range(grid):
                        block = line[x * res : (x + 1) * res, :side]
                        pixel_grad[slot, c, x * side : (x + 1) * side, :] = block.T

def embed(patch_size, pixels, table, pos, w_base, patch_bias, pos_base, rows_total):
    images, channels, res, _ = pixels.shape
    width, features = w_base.shape
    fine = (res // FINE) ** 2
    small = (res // SIDES[1]) ** 2
    side = table.shape[1]
    wide = jnp.pad(pixels.astype(jnp.float32), ((0, 0), (0, 0), (0, 0), (0, -res % 128)))
    return pl.pallas_call(
        embed_kernel,
        out_shape=[
            jax.ShapeDtypeStruct((rows_total, width), jnp.float32),
            jax.ShapeDtypeStruct((images, small + 4, features), jnp.bfloat16),
            jax.ShapeDtypeStruct((fine + 12, channels * FINE * FINE), jnp.bfloat16),
            jax.ShapeDtypeStruct((channels * FINE * FINE, width), jnp.bfloat16),
        ],
        in_specs=[SMEM] + [VMEM] * 6,
        out_specs=[VMEM] * 4,
        scratch_shapes=[
            pltpu.VMEM((res * res // FINE, 128), jnp.float32),
            pltpu.VMEM((side * side, features // channels), jnp.float32),
            pltpu.VMEM((images, fine + 4, width), jnp.float32),
        ],
        compiler_params=pltpu.CompilerParams(vmem_limit_bytes=60 << 20),
        name="embed",
    )(patch_size, wide, table, pos, w_base, patch_bias.astype(jnp.float32)[None], pos_base)


def pixel_back(patch_size, grad, table, pos, w_base, tokens, patches, mixed_weight, core, shape):
    images, channels, res, _ = shape
    width, features = w_base.shape
    fine = (res // FINE) ** 2
    side = table.shape[1]
    return pl.pallas_call(
        pixel_kernel,
        out_shape=[
            jax.ShapeDtypeStruct(shape, jnp.float32),
            jax.ShapeDtypeStruct((width // 2, features), jnp.float32),
            jax.ShapeDtypeStruct((pos.shape[2], width), jnp.float32),
        ],
        in_specs=[SMEM] + [VMEM] * 7 + [SMEM],
        out_specs=[VMEM] * 3,
        scratch_shapes=[
            pltpu.VMEM((res * res // FINE, 128), jnp.float32),
            pltpu.VMEM((side * side, features // channels), jnp.float32),
            pltpu.VMEM((images, fine + 4, width), jnp.float32),
        ],
        compiler_params=pltpu.CompilerParams(vmem_limit_bytes=60 << 20),
        name="pixel_back",
    )(patch_size, grad, table, pos, w_base, tokens, patches, mixed_weight, core)


PAIR = 2 * HD


def pair_halves(rows):
    lane = lax.broadcasted_iota(jnp.int32, (rows, PAIR), 1)
    return [lane < HD, lane >= HD]


def attend_kernel(scale, query, key, value, segment, segment_row, mixed):
    rows = query.shape[0]
    halves = pair_halves(rows)
    same = segment[...] == segment_row[...]
    both = []
    for h in range(2):
        own = jnp.where(halves[h], query[...], jnp.zeros_like(query))
        scores = jnp.where(same, nt(own, key[...]) * scale, -1000000000.0)
        weights = jnp.exp(scores - jnp.max(scores, axis=1, keepdims=True))
        inverse = 1.0 / jnp.sum(weights, axis=1, keepdims=True)
        both.append(nn((weights * inverse).astype(jnp.bfloat16), value[...]))
    mixed[...] = jnp.where(halves[0], both[0], both[1]).astype(jnp.bfloat16)


def attend(qkv, segment, block):
    rows, width = qkv.shape
    heads = width // 3 // PAIR
    kernel = functools.partial(attend_kernel, 1.0 / math.sqrt(HD))
    return pl.pallas_call(
        kernel,
        grid=(heads, rows // block),
        out_shape=jax.ShapeDtypeStruct((rows, width // 3), jnp.bfloat16),
        in_specs=[
            pl.BlockSpec((block, PAIR), lambda j, i: (i, j)),
            pl.BlockSpec((rows, PAIR), lambda j, i: (0, heads + j)),
            pl.BlockSpec((rows, PAIR), lambda j, i: (0, 2 * heads + j)),
            pl.BlockSpec((block, 1), lambda j, i: (i, 0)),
            pl.BlockSpec((1, rows), lambda j, i: (0, 0)),
        ],
        out_specs=pl.BlockSpec((block, PAIR), lambda j, i: (i, j)),
        compiler_params=pltpu.CompilerParams(vmem_limit_bytes=48 << 20),
        name="attend",
    )(qkv, qkv, qkv, segment[:, None], segment[None, :])


def attend_back_kernel(scale, query, key, value, grad_mixed, segment, segment_row, grad_qkv, grad_key, grad_value):
    block = query.shape[0]
    third = grad_qkv.shape[1] // 3
    pair = pl.program_id(0)
    step = pl.program_id(1)
    halves = pair_halves(block)
    same = segment[...] == segment_row[...]

    @pl.when(step == 0)
    def _():
        grad_key[...] = jnp.zeros_like(grad_key)
        grad_value[...] = jnp.zeros_like(grad_value)

    both = []
    for h in range(2):
        own = jnp.where(halves[h], query[...], jnp.zeros_like(query))
        grad = jnp.where(halves[h], grad_mixed[...], jnp.zeros_like(grad_mixed))
        scores = jnp.where(same, nt(key[...], own) * scale, -1000000000.0)
        weights = jnp.exp(scores - jnp.max(scores, axis=0, keepdims=True))
        probs = weights * (1.0 / jnp.sum(weights, axis=0, keepdims=True))
        grad_probs = nt(value[...], grad)
        inner = jnp.sum(probs * grad_probs, axis=0, keepdims=True)
        grad_scores = (probs * (grad_probs - inner)).astype(jnp.bfloat16)
        grad_value[...] += nn(probs.astype(jnp.bfloat16), grad)
        grad_key[...] += nn(grad_scores, own)
        both.append(tn(grad_scores, key[...]))
    here = pl.ds(pl.multiple_of(step * block, block), block)
    column = pl.multiple_of(pair * PAIR, PAIR)
    grad_query = jnp.where(halves[0], both[0], both[1]) * scale
    grad_qkv[here, pl.ds(column, PAIR)] = grad_query.astype(jnp.bfloat16)

    @pl.when(step == pl.num_programs(1) - 1)
    def _():
        grad_qkv[:, pl.ds(third + column, PAIR)] = (grad_key[...] * scale).astype(jnp.bfloat16)
        grad_qkv[:, pl.ds(2 * third + column, PAIR)] = grad_value[...].astype(jnp.bfloat16)


def attend_back(qkv, grad_mixed, segment, block):
    rows, width = qkv.shape
    heads = width // 3 // PAIR
    kernel = functools.partial(attend_back_kernel, 1.0 / math.sqrt(HD))
    return pl.pallas_call(
        kernel,
        grid=(heads, rows // block),
        out_shape=jax.ShapeDtypeStruct((rows, width), jnp.bfloat16),
        in_specs=[
            pl.BlockSpec((block, PAIR), lambda j, i: (i, j)),
            pl.BlockSpec((rows, PAIR), lambda j, i: (0, heads + j)),
            pl.BlockSpec((rows, PAIR), lambda j, i: (0, 2 * heads + j)),
            pl.BlockSpec((block, PAIR), lambda j, i: (i, j)),
            pl.BlockSpec((rows, 1), lambda j, i: (0, 0)),
            pl.BlockSpec((1, block), lambda j, i: (0, i)),
        ],
        out_specs=pl.BlockSpec((rows, width), lambda j, i: (0, 0)),
        scratch_shapes=[pltpu.VMEM((rows, PAIR), jnp.float32), pltpu.VMEM((rows, PAIR), jnp.float32)],
        compiler_params=pltpu.CompilerParams(vmem_limit_bytes=48 << 20),
        name="attend_back",
    )(qkv, qkv, qkv, grad_mixed, segment[:, None], segment[None, :])


LINE = 4
MESH_ID = pl.DeviceIdType.MESH


def sync_kernel(pieces, scale, in_count, out_count, *refs):
    grads = refs[:in_count]
    outs = refs[in_count : in_count + out_count]
    acc, land, land_right, land_left, land_last, sems = refs[in_count + out_count :]
    device = lax.axis_index("dp")
    core = lax.axis_index("tensor")
    place_x = lax.rem(device, 2)
    place_y = lax.rem(device // 2, 2)
    place_z = lax.rem(device // 4, LINE)
    beside = {"x": device + 1 - 2 * place_x, "y": device + 2 - 4 * place_y}
    bits = {"x": place_x, "y": place_y}
    up = device + 4
    down = device - 4

    barrier = pltpu.get_barrier_semaphore()
    for partner in (beside["x"], beside["y"]):
        pl.semaphore_signal(barrier, inc=1, device_id=(partner, core), device_id_type=MESH_ID)
    pl.semaphore_signal(barrier, inc=1, device_id=(device, 1 - core), device_id_type=MESH_ID)

    @pl.when(place_z < LINE - 1)
    def _():
        pl.semaphore_signal(barrier, inc=1, device_id=(up, core), device_id_type=MESH_ID)

    @pl.when(place_z > 0)
    def _():
        pl.semaphore_signal(barrier, inc=1, device_id=(down, core), device_id_type=MESH_ID)

    inner = (place_z + LINE - 1) // LINE + (2 * (LINE - 1) - place_z) // LINE
    pl.semaphore_wait(barrier, 3 + inner)

    def rows_at(ref, start, size, column, width):
        return ref.at[pl.ds(pl.multiple_of(start, 8), size), pl.ds(column, width)]

    def remote(src, dst, send, recv, where):
        return pltpu.make_async_remote_copy(
            src_ref=src,
            dst_ref=dst,
            send_sem=send,
            recv_sem=recv,
            device_id=where,
            device_id_type=MESH_ID,
        )

    def add_rows(total, start, extra, size, width, factor=None):
        step = 24 if size % 24 == 0 else 8

        @pl.loop(0, size // step)
        def _(i):
            here = pl.ds(pl.multiple_of(start + i * step, 8), step)
            there = pl.ds(pl.multiple_of(i * step, 8), step)
            value = total[here, :width] + extra[there, :width]
            total[here, :width] = value if factor is None else value * factor

    def build(number, piece):
        source, in_row, in_col, target, out_row, out_col, rows, width, first = piece
        second = "y" if first == "x" else "x"
        half, chunk, share = rows // 2, rows // 8, rows // 16
        grad, out = grads[source], outs[target]
        own, other = bits[first], bits[second]
        mine = acc.at[number]
        sem = lambda k: sems.at[number, k]
        base_row = out_row + core * rows if piece_swaps(piece) else out_row
        half_row = base_row + own * half

        def first_copy():
            return remote(
                rows_at(grad, in_row + (1 - own) * half, half, in_col, width),
                land.at[number, :half, :width],
                sem(0),
                sem(1),
                (beside[first], core),
            )

        def load():
            return pltpu.make_async_copy(
                rows_at(grad, in_row + own * half, half, in_col, width),
                mine.at[:half, :width],
                sem(2),
            )

        def right(k):
            return remote(
                rows_at(mine, (LINE - k + place_z) * chunk, chunk, 0, width),
                land_right.at[number, k - 1, :chunk, :width],
                sem(2 + k),
                sem(5 + k),
                (up, core),
            )

        def left(k):
            return remote(
                rows_at(mine, (k - 1 - (LINE - 1 - place_z)) * chunk, chunk, 0, width),
                land_left.at[number, k - 1, :chunk, :width],
                sem(8 + k),
                sem(11 + k),
                (down, core),
            )

        def got_right(k):
            return remote(
                land_right.at[number, k - 1, :chunk, :width],
                land_right.at[number, k - 1, :chunk, :width],
                sem(2 + k),
                sem(5 + k),
                (down, core),
            )

        def got_left(k):
            return remote(
                land_left.at[number, k - 1, :chunk, :width],
                land_left.at[number, k - 1, :chunk, :width],
                sem(8 + k),
                sem(11 + k),
                (up, core),
            )

        mirror = LINE - 1 - place_z

        def send_line(k):
            @pl.when((place_z <= k - 1) & (place_z < LINE - 1))
            def _():
                right(k).start()

            @pl.when((mirror <= k - 1) & (mirror < LINE - 1))
            def _():
                left(k).start()

        def wait_line(k):
            @pl.when((place_z >= 1) & (place_z <= k))
            def _():
                got_right(k).wait_recv()
                add_rows(
                    mine, (LINE - 1 - k + place_z) * chunk, land_right.at[number, k - 1], chunk, width
                )

            @pl.when((mirror >= 1) & (mirror <= k))
            def _():
                got_left(k).wait_recv()
                add_rows(mine, (k - mirror) * chunk, land_left.at[number, k - 1], chunk, width)

        def last_copy():
            return remote(
                rows_at(mine, place_z * chunk + (1 - other) * share, share, 0, width),
                land_last.at[number, :share, :width],
                sem(15),
                sem(16),
                (beside[second], core),
            )

        share_row = half_row + place_z * chunk + other * share

        def share_out():
            return remote(
                rows_at(mine, place_z * chunk + other * share, share, 0, width),
                rows_at(out, share_row, share, out_col, width),
                sem(17),
                sem(18),
                (beside[second], core),
            )

        def share_in():
            return remote(
                rows_at(mine, place_z * chunk + other * share, share, 0, width),
                rows_at(out, half_row + place_z * chunk + (1 - other) * share, share, out_col, width),
                sem(17),
                sem(18),
                (beside[second], core),
            )

        def share_store():
            return pltpu.make_async_copy(
                rows_at(mine, place_z * chunk + other * share, share, 0, width),
                rows_at(out, share_row, share, out_col, width),
                sem(19),
            )

        def chunk_out(position):
            return rows_at(out, half_row + position * chunk, chunk, out_col, width)

        def spread_right(k, position, where):
            return remote(
                chunk_out(position), chunk_out(position), sem(19 + k), sem(22 + k), (where, core)
            )

        def spread_left(k, position, where):
            return remote(
                chunk_out(position), chunk_out(position), sem(25 + k), sem(28 + k), (where, core)
            )

        def send_spread(k):
            @pl.when((place_z >= k - 1) & (place_z < LINE - 1))
            def _():
                spread_right(k, place_z - (k - 1), up).start()

            @pl.when((mirror >= k - 1) & (mirror < LINE - 1))
            def _():
                spread_left(k, place_z + (k - 1), down).start()

        def wait_spread(k):
            @pl.when(place_z >= k)
            def _():
                spread_right(k, place_z - k, down).wait_recv()

            @pl.when(mirror >= k)
            def _():
                spread_left(k, place_z + k, up).wait_recv()

        def half_out():
            here = rows_at(out, half_row, half, out_col, width)
            return remote(here, here, sem(32), sem(33), (beside[first], core))

        def half_in():
            there = rows_at(out, base_row + (1 - own) * half, half, out_col, width)
            return remote(there, there, sem(32), sem(33), (beside[first], core))

        def swap_out():
            here = rows_at(out, base_row, rows, out_col, width)
            return remote(here, here, sem(34), sem(35), (device, 1 - core))

        def swap_in():
            there = rows_at(out, out_row + (1 - core) * rows, rows, out_col, width)
            return remote(there, there, sem(34), sem(35), (device, 1 - core))

        def stage_0():
            first_copy().start()
            load().start()

        def stage_1():
            load().wait()
            first_copy().wait_recv()
            add_rows(mine, 0, land.at[number], half, width)
            send_line(1)

        def stage_2():
            wait_line(1)
            send_line(2)

        def stage_3():
            wait_line(2)
            send_line(3)

        def stage_4():
            wait_line(3)
            last_copy().start()

        def stage_5():
            last_copy().wait()
            add_rows(
                mine, place_z * chunk + other * share, land_last.at[number], share, width, scale
            )
            share_out().start()
            share_store().start()

        def stage_6():
            share_store().wait()
            share_in().wait_recv()
            send_spread(1)

        def stage_7():
            wait_spread(1)
            send_spread(2)

        def stage_8():
            wait_spread(2)
            send_spread(3)

        def stage_9():
            wait_spread(3)
            half_out().start()

        def stage_10():
            half_in().wait_recv()
            if piece_swaps(piece):
                swap_out().start()

        def stage_11():
            if piece_swaps(piece):
                swap_in().wait_recv()
                swap_out().wait_send()
            first_copy().wait_send()
            share_out().wait_send()
            half_out().wait_send()
            for k in range(1, LINE):

                @pl.when((place_z <= k - 1) & (place_z < LINE - 1))
                def _():
                    right(k).wait_send()

                @pl.when((mirror <= k - 1) & (mirror < LINE - 1))
                def _():
                    left(k).wait_send()

                @pl.when((place_z >= k - 1) & (place_z < LINE - 1))
                def _():
                    spread_right(k, place_z - (k - 1), up).wait_send()

                @pl.when((mirror >= k - 1) & (mirror < LINE - 1))
                def _():
                    spread_left(k, place_z + (k - 1), down).wait_send()

        return [
            stage_0,
            stage_1,
            stage_2,
            stage_3,
            stage_4,
            stage_5,
            stage_6,
            stage_7,
            stage_8,
            stage_9,
            stage_10,
            stage_11,
        ]

    lines = [build(number, piece) for number, piece in enumerate(pieces)]
    pairs = [lines[i : i + 2] for i in range(0, len(lines), 2)]
    depth = len(lines[0])
    ahead = 1
    for j in range(ahead):
        for line in pairs[j]:
            line[0]()
    for tick in range(len(pairs) + depth - 1):
        if tick + ahead < len(pairs):
            for line in pairs[tick + ahead]:
                line[0]()
        for j in range(max(0, tick - depth + 1), min(tick, len(pairs))):
            for line in pairs[j]:
                line[tick - j]()


def piece_swaps(piece):
    return piece[3] == SWAPPED


SWAPPED = 0
PIECE_ROWS = 384
PIECE_COLS = 768


def sync_plan(in_shapes, out_shapes, out_of):
    pieces = []
    for source, shape in enumerate(in_shapes):
        targets = out_of[source]
        col_of_source = 0
        for target in targets:
            cols = out_shapes[target][1]
            rows = shape[0]
            tall = min(PIECE_ROWS, rows)
            wide = min(PIECE_COLS, cols)
            for row in range(0, rows, tall):
                for col in range(0, cols, wide):
                    pieces.append([source, row, col_of_source + col, target, row, col, tall, wide])
            col_of_source += cols
    return [tuple(piece) + ("xy"[i % 2],) for i, piece in enumerate(pieces)]


def sync_grads(grads, out_shapes, out_of, replicas):
    pieces = sync_plan([g.shape for g in grads], out_shapes, out_of)
    count = len(pieces)
    high = max(p[6] for p in pieces)
    wide = max(p[7] for p in pieces)
    kernel = functools.partial(
        sync_kernel, pieces, 1.0 / replicas, len(grads), len(out_shapes)
    )
    vmem = lambda *dims: pltpu.VMEM(dims, jnp.float32)
    return pl.pallas_call(
        kernel,
        out_shape=[jax.ShapeDtypeStruct(s, jnp.float32) for s in out_shapes],
        in_specs=[pl.BlockSpec(memory_space=pl.ANY)] * len(grads),
        out_specs=[pl.BlockSpec(memory_space=pl.ANY)] * len(out_shapes),
        scratch_shapes=[
            vmem(count, high // 2, wide),
            vmem(count, high // 2, wide),
            vmem(count, LINE - 1, high // 8, wide),
            vmem(count, LINE - 1, high // 8, wide),
            vmem(count, high // 16, wide),
            pltpu.SemaphoreType.DMA((count, 36)),
        ],
        compiler_params=pltpu.CompilerParams(
            collective_id=0, has_side_effects=True, vmem_limit_bytes=56 << 20
        ),
        name="sync_grads",
    )(*grads)


def tensor_sum(partial):
    return partial + lax.ppermute(partial, "tensor", [(0, 1), (1, 0)])


def local(
    pixels,
    patch_size,
    counts,
    offsets,
    resize_table,
    pos_table,
    w_base,
    patch_bias,
    pos_base,
    gain_one,
    shift_one,
    w_query,
    bias_query,
    w_key,
    w_value,
    bias_value,
    w_out,
    bias_out,
    gain_two,
    shift_two,
    w_up,
    bias_up,
    w_down,
    bias_down,
    cotangent,
):
    wide = lambda value: value.astype(jnp.float32)
    rows_total = cotangent.shape[0]
    replicas = lax.axis_size("dp")
    core = lax.axis_index("tensor")
    segment, valid_int = row_segments(counts, offsets, rows_total)
    valid_rows = wide(valid_int)[:, None]
    table = jnp.take(resize_table, patch_size, axis=0)
    pos = jnp.take(pos_table, pixels.shape[2] // patch_size, axis=0)
    embedded, tokens, patches, mixed_weight = embed(
        patch_size, pixels, table, pos, w_base, patch_bias, pos_base, rows_total
    )
    w_qkv = jnp.concatenate([w_query, w_key, w_value], axis=1)
    bias_qkv = jnp.concatenate([bias_query, jnp.zeros_like(bias_query), bias_value])
    standard_one, standard_back_one = jax.vjp(standardize, embedded)
    normed_one = (standard_one * wide(gain_one) + wide(shift_one)).astype(jnp.bfloat16)
    qkv = (
        jnp.dot(normed_one, w_qkv, preferred_element_type=jnp.float32) + wide(bias_qkv)
    ).astype(jnp.bfloat16)
    mixed = attend(qkv, segment, rows_total)
    attended = tensor_sum(jnp.dot(mixed, w_out, preferred_element_type=jnp.float32)) + wide(
        bias_out
    )
    middle = embedded + attended
    standard_two, standard_back_two = jax.vjp(standardize, middle)
    normed_two = (standard_two * wide(gain_two) + wide(shift_two)).astype(jnp.bfloat16)
    hidden = jnp.dot(normed_two, w_up, preferred_element_type=jnp.float32) + wide(bias_up)
    activated_wide, gelu_back = jax.vjp(jax.nn.gelu, hidden)
    activated = activated_wide.astype(jnp.bfloat16)
    branch = tensor_sum(jnp.dot(activated, w_down, preferred_element_type=jnp.float32)) + wide(
        bias_down
    )
    output = ((middle + branch) * valid_rows).astype(jnp.bfloat16)
    grad_out = wide(cotangent) * valid_rows
    grad_branch = grad_out.astype(jnp.bfloat16)
    grad_w_down = jnp.einsum(
        "tf,td->fd", activated, grad_branch, preferred_element_type=jnp.float32
    )
    grad_activated = jnp.einsum(
        "td,fd->tf", grad_branch, w_down, preferred_element_type=jnp.float32
    )
    grad_hidden = gelu_back(grad_activated)[0].astype(jnp.bfloat16)
    grad_w_up = jnp.einsum("td,tf->df", normed_two, grad_hidden, preferred_element_type=jnp.float32)
    grad_bias_up = jnp.sum(grad_hidden, axis=0, dtype=jnp.float32)
    grad_normed_two = tensor_sum(
        jnp.einsum("tf,df->td", grad_hidden, w_up, preferred_element_type=jnp.float32)
    )
    grad_middle = grad_out + standard_back_two(grad_normed_two * wide(gain_two))[0]
    grad_attended = grad_middle.astype(jnp.bfloat16)
    grad_w_out = jnp.einsum("te,td->ed", mixed, grad_attended, preferred_element_type=jnp.float32)
    grad_mixed = jnp.einsum(
        "td,ed->te", grad_attended, w_out, preferred_element_type=jnp.float32
    ).astype(jnp.bfloat16)
    grad_qkv = attend_back(qkv, grad_mixed, segment, rows_total)
    grad_w_qkv = jnp.einsum("td,te->de", normed_one, grad_qkv, preferred_element_type=jnp.float32)
    grad_bias_qkv = jnp.sum(grad_qkv, axis=0, dtype=jnp.float32)
    cut = bias_query.shape[0]
    grad_bias_query, grad_bias_value = grad_bias_qkv[:cut], grad_bias_qkv[2 * cut :]
    grad_normed_one = tensor_sum(
        jnp.einsum("te,de->td", grad_qkv, w_qkv, preferred_element_type=jnp.float32)
    )
    grad_embedded = grad_middle + standard_back_one(grad_normed_one * wide(gain_one))[0]
    grad_embedded_low = grad_embedded.astype(jnp.bfloat16)
    pixel_grad, grad_w_base, grad_pos_base = pixel_back(
        patch_size,
        grad_embedded,
        table,
        pos,
        w_base,
        tokens,
        patches,
        mixed_weight,
        core[None],
        pixels.shape,
    )
    grad_patch_bias = jnp.sum(grad_embedded_low, axis=0, dtype=jnp.float32)
    grad_gain_one = jnp.sum(grad_normed_one * standard_one, axis=0)
    grad_shift_one = jnp.sum(grad_normed_one, axis=0)
    grad_bias_out = jnp.sum(grad_attended, axis=0, dtype=jnp.float32)
    grad_gain_two = jnp.sum(grad_normed_two * standard_two, axis=0)
    grad_shift_two = jnp.sum(grad_normed_two, axis=0)
    grad_bias_down = jnp.sum(grad_branch, axis=0, dtype=jnp.float32)
    width = grad_patch_bias.shape[0]
    small_rows = [
        grad_pos_base,
        grad_patch_bias[None],
        grad_gain_one[None],
        grad_shift_one[None],
        grad_bias_out[None],
        grad_gain_two[None],
        grad_shift_two[None],
        grad_bias_down[None],
        jnp.concatenate([grad_bias_query, grad_bias_value])[None],
        grad_bias_up.reshape(-1, width),
    ]
    small = jnp.concatenate(small_rows, axis=0)
    used = small.shape[0]
    small = jnp.pad(small, ((0, -used % 128), (0, 0)))
    parts = [grad_w_down, grad_w_up, grad_w_qkv, grad_w_base, grad_w_out, small]
    beyond = replicas // 16
    step = 1
    while step < beyond:
        swap = [(i, (i // 16 ^ step) * 16 + i % 16) for i in range(replicas)]
        parts = [part + lax.ppermute(part, "dp", swap) for part in parts]
        step *= 2
    out_shapes = [
        (2 * grad_w_base.shape[0], grad_w_base.shape[1]),
        grad_w_down.shape,
        grad_w_up.shape,
        w_query.shape,
        w_key.shape,
        w_value.shape,
        grad_w_out.shape,
        small.shape,
    ]
    synced = sync_grads(parts, out_shapes, [[1], [2], [3, 4, 5], [0], [6], [7]], replicas)
    base_s, down_s, up_s, query_s, key_s, value_s, out_s, small_s = synced
    points = pos.shape[2]
    row = lambda k: small_s[points + k]
    return (
        output,
        pixel_grad,
        base_s,
        row(0),
        small_s[:points].T,
        row(1),
        row(2),
        query_s,
        row(7)[:cut],
        key_s,
        value_s,
        row(7)[cut:],
        out_s,
        row(3),
        row(4),
        row(5),
        up_s,
        small_s[points + 8 : used].reshape(-1),
        down_s,
        row(6),
    )


def solution(mesh):
    in_specs = (
        P("dp", None, None, None),
        P("dp"),
        P("dp"),
        P("dp"),
        P(),
        P(),
        P(),
        P(),
        P(),
        P(),
        P(),
        P(None, "tensor"),
        P("tensor"),
        P(None, "tensor"),
        P(None, "tensor"),
        P("tensor"),
        P("tensor", None),
        P(),
        P(),
        P(),
        P(None, "tensor"),
        P("tensor"),
        P("tensor", None),
        P(),
        P("dp", None),
    )
    out_specs = (
        P("dp", None),
        P("dp", None, None, None),
        P(),
        P(),
        P(),
        P(),
        P(),
        P(None, "tensor"),
        P("tensor"),
        P(None, "tensor"),
        P(None, "tensor"),
        P("tensor"),
        P("tensor", None),
        P(),
        P(),
        P(),
        P(None, "tensor"),
        P("tensor"),
        P("tensor", None),
        P(),
    )
    return jax.shard_map(local, mesh=mesh, in_specs=in_specs, out_specs=out_specs, check_vma=False)
```

```python
import functools
import math

import jax
import jax.numpy as jnp
from jax import lax
from jax.experimental import pallas as pl
from jax.experimental.pallas import tpu as pltpu
from jax.sharding import PartitionSpec as P

HD = 64
VMEM = pl.BlockSpec(memory_space=pltpu.VMEM)
SMEM = pl.BlockSpec(memory_space=pltpu.SMEM)


def standardize(values):
    centered = values - jnp.mean(values, axis=-1, keepdims=True)
    spread = jnp.mean(centered * centered, axis=-1, keepdims=True)
    return centered * lax.rsqrt(spread + 1e-06)


FINE = 8
COARSE = (24, 30, 40, 48)


def nt(left, right):
    return lax.dot_general(left, right, (((1,), (1,)), ((), ())), preferred_element_type=jnp.float32)


def tn(left, right):
    return lax.dot_general(left, right, (((0,), (0,)), ((), ())), preferred_element_type=jnp.float32)


def nn(left, right):
    return jnp.dot(left, right, preferred_element_type=jnp.float32)


def up_to(value, step):
    return value + -value % step


def loop(count, body, unroll):
    if unroll:
        for i in range(count):
            body(i)
    else:
        pl.loop(0, count)(body)


def aligned(start, side):
    return pl.multiple_of(start, 8) if side % 8 == 0 and not isinstance(start, int) else start


def fill_pairs(pair, long, table, side):
    base = table.shape[1]
    entry = lax.broadcasted_iota(jnp.int32, (base, base * base), 0)
    place = lax.broadcasted_iota(jnp.int32, (base, base * base), 1)
    repeat = (place // base == entry).astype(jnp.bfloat16)
    tile = (place % base == entry).astype(jnp.bfloat16)
    wide = nn(table, repeat)[:side]
    long[...] = nn(table, tile)

    def one(s):
        pair[pl.ds(aligned(s * side, side), side), :] = wide * long[pl.ds(s, 1), :]

    loop(side, one, True)


def cut_patches(line, pix, image, channel, side, grid, res):
    def one(x):
        block = pix[image, channel, pl.ds(aligned(x * side, side), side), :]
        line[pl.ds(aligned(x * res, 8), res), :side] = block.T[:res]

    loop(grid, one, True)
    return jnp.concatenate(
        [line[pl.ds(s, grid * grid, stride=side), :side] for s in range(side)], axis=1
    ).astype(jnp.bfloat16)


def place_patches(line, pixel_grad, image, channel, patch, side, grid, res):
    for s in range(side):
        line[pl.ds(s, grid * grid, stride=side), :side] = patch[:, s * side : (s + 1) * side]

    def one(x):
        block = line[pl.ds(aligned(x * res, 8), res), :side]
        pixel_grad[image, channel, pl.ds(aligned(x * side, side), side), :] = block.T

    loop(grid, one, True)


def embed_kernel(
    sizes,
    order,
    pix,
    table,
    pos_fine,
    pos,
    weight,
    bias,
    pos_base,
    emb,
    tokens,
    patches,
    mixed_weight,
    line,
    pair,
    long,
):
    area = table.shape[2] ** 2
    channels, res = pix.shape[1:3]
    grid = res // FINE
    count = grid * grid
    start = up_to(count, 16)
    stride = tokens.shape[1]
    low = jnp.bfloat16
    emb[...] = jnp.broadcast_to(bias[...], emb.shape)

    fill_pairs(pair, long, table[0], FINE)
    fine_pairs = pair[: FINE * FINE, :].astype(low)
    emb[:count, :] += nt(pos_fine[...], pos_base[...])

    @functools.partial(loop, channels, unroll=True)
    def _(c):
        columns = pl.ds(c * area, area)
        patch = cut_patches(line, pix, order[0], c, FINE, grid, res)
        mixed = nt(fine_pairs, weight[:, columns]).astype(low)
        mixed_weight[c] = mixed
        patches[c, :count, :] = patch
        emb[:count, :] += nn(patch, mixed)

    @pl.loop(1, 4)
    def _(slot):
        row = pl.multiple_of(start + (slot - 1) * stride, 8)
        for side in COARSE:
            grid = res // side
            count = grid * grid

            @pl.when(sizes[slot] == side)
            def _():
                fill_pairs(pair, long, table[slot], side)
                here = pl.ds(row, count)
                emb[here, :] += nt(pos[slot - 1, :count, :], pos_base[...])

                @functools.partial(loop, channels, unroll=True)
                def _(c):
                    columns = pl.ds(c * area, area)
                    patch = cut_patches(line, pix, order[slot], c, side, grid, res)
                    token = nn(patch, pair[: side * side, :].astype(low)).astype(low)
                    tokens[slot - 1, :count, columns] = token
                    emb[here, :] += nt(token, weight[:, columns])


def embed(sizes, order, pix, table, pos_fine, pos, w_base, patch_bias, pos_base, rows):
    _, channels, res, _ = pix.shape
    width, features = w_base.shape
    fine = (res // FINE) ** 2
    side = table.shape[1]
    area = features // channels
    return pl.pallas_call(
        embed_kernel,
        out_shape=[
            jax.ShapeDtypeStruct((rows, width), jnp.float32),
            jax.ShapeDtypeStruct((3, up_to(pos.shape[1], 8), features), jnp.bfloat16),
            jax.ShapeDtypeStruct((channels, up_to(fine, 16), FINE * FINE), jnp.bfloat16),
            jax.ShapeDtypeStruct((channels, FINE * FINE, width), jnp.bfloat16),
        ],
        in_specs=[SMEM] * 2 + [VMEM] * 7,
        out_specs=[VMEM] * 4,
        scratch_shapes=[
            pltpu.VMEM((res * res // FINE, 128), jnp.float32),
            pltpu.VMEM((side * side, area), jnp.float32),
            pltpu.VMEM((side, area), jnp.float32),
        ],
        compiler_params=pltpu.CompilerParams(vmem_limit_bytes=48 << 20),
        name="embed",
    )(
        sizes,
        order,
        pix,
        table,
        pos_fine,
        pos,
        w_base,
        patch_bias.astype(jnp.float32)[None],
        pos_base,
    )


def pixel_kernel(
    sizes,
    place,
    grad,
    table,
    pos_fine,
    pos,
    weight,
    tokens,
    patches,
    mixed_weight,
    pixel_grad,
    grad_weight,
    grad_pos,
    line,
    pair,
    long,
):
    area = table.shape[2] ** 2
    channels, res = pixel_grad.shape[1:3]
    half = grad_weight.shape[0]
    part = grad_weight.shape[1] // channels
    core_columns = pl.ds(pl.multiple_of(place[0] * half, 128), half)
    side_start = place[1] * part
    is_fine = place[2]
    grid = res // FINE
    count = grid * grid
    start = up_to(count, 16)
    stride = tokens.shape[1]
    low = jnp.bfloat16

    fill_pairs(pair, long, table[0], FINE)
    some_pairs = pair[: FINE * FINE, pl.ds(pl.multiple_of(side_start, 128), part)].astype(low)
    rows = grad[:count, :].astype(low)
    some = grad[:count, core_columns].astype(low)
    grad_pos[...] = tn(pos_fine[...], rows)

    @pl.loop(0, channels)
    def _(c):
        gathered = tn(patches[c, :count, :], some).astype(low)
        grad_weight[:, pl.ds(pl.multiple_of(c * part, 128), part)] = tn(gathered, some_pairs)

        @pl.when(is_fine == 1)
        def _():
            patch = nt(grad[:count, :].astype(low), mixed_weight[c])
            place_patches(line, pixel_grad, 0, c, patch, FINE, grid, res)

    @pl.loop(1, 4)
    def _(slot):
        row = pl.multiple_of(start + (slot - 1) * stride, 8)
        wanted = jnp.where(slot == 1, is_fine, 1 - is_fine)
        image = jnp.where(slot == 1, 1, slot - 2)
        for side in COARSE:
            grid = res // side
            count = grid * grid

            @pl.when(sizes[slot] == side)
            def _():
                here = pl.ds(row, count)
                rows = grad[here, :].astype(low)
                some = grad[here, core_columns].astype(low)
                grad_pos[...] += tn(pos[slot - 1, :count, :], rows)

                @pl.loop(0, channels)
                def _(c):
                    columns = pl.ds(pl.multiple_of(c * area + side_start, 128), part)
                    grad_weight[:, pl.ds(pl.multiple_of(c * part, 128), part)] += tn(
                        some, tokens[slot - 1, :count, columns]
                    )

                @pl.when(wanted == 1)
                def _():
                    fill_pairs(pair, long, table[slot], side)

                    @pl.loop(0, channels)
                    def _(c):
                        columns = pl.ds(pl.multiple_of(c * area, area), area)
                        token = nn(grad[here, :].astype(low), weight[:, columns]).astype(low)
                        patch = nt(token, pair[: side * side, :].astype(low))
                        place_patches(line, pixel_grad, image, c, patch, side, grid, res)


def pixel_back(
    sizes, place, grad, table, pos_fine, pos, w_base, tokens, patches, mixed_weight, shape
):
    _, channels, res, _ = shape
    width, features = w_base.shape
    side = table.shape[1]
    return pl.pallas_call(
        pixel_kernel,
        out_shape=[
            jax.ShapeDtypeStruct(shape, jnp.float32),
            jax.ShapeDtypeStruct((width // 2, features // 2), jnp.float32),
            jax.ShapeDtypeStruct((pos.shape[2], width), jnp.float32),
        ],
        in_specs=[SMEM] * 2 + [VMEM] * 8,
        out_specs=[VMEM] * 3,
        scratch_shapes=[
            pltpu.VMEM((res * res // FINE, 128), jnp.float32),
            pltpu.VMEM((side * side, features // channels), jnp.float32),
            pltpu.VMEM((side, features // channels), jnp.float32),
        ],
        compiler_params=pltpu.CompilerParams(vmem_limit_bytes=48 << 20),
        name="pixel_back",
    )(sizes, place, grad, table, pos_fine, pos, w_base, tokens, patches, mixed_weight)


PAIR = 2 * HD


def pair_halves(rows):
    lane = lax.broadcasted_iota(jnp.int32, (rows, PAIR), 1)
    return [lane < HD, lane >= HD]


def attend_block(scale, query, key, value, mask):
    halves = pair_halves(query.shape[0])
    both = []
    for h in range(2):
        own = jnp.where(halves[h], query, jnp.zeros_like(query))
        scores = jnp.where(mask, nt(own, key) * scale, -1000000000.0)
        weights = jnp.exp(scores - jnp.max(scores, axis=1, keepdims=True))
        inverse = 1.0 / jnp.sum(weights, axis=1, keepdims=True)
        both.append(nn((weights * inverse).astype(jnp.bfloat16), value))
    return jnp.where(halves[0], both[0], both[1]).astype(jnp.bfloat16)


def block_masks(fine, start, rows, segment, segment_row, axis):
    inside = lax.broadcasted_iota(jnp.int32, (start, start), axis) < fine
    same = segment[start:rows, :] == segment_row[:, : rows - start]
    return inside, same


def attend_kernel(scale, fine, start, query, key, value, segment, segment_row, mixed):
    rows = query.shape[0]
    masks = block_masks(fine, start, rows, segment, segment_row, 1)
    for here, mask in zip((slice(0, start), slice(start, rows)), masks):
        mixed[here, :] = attend_block(scale, query[here, :], key[here, :], value[here, :], mask)


def attend(qkv, segment, fine, start):
    rows, width = qkv.shape
    heads = width // 3 // PAIR
    kernel = functools.partial(attend_kernel, 1.0 / math.sqrt(HD), fine, start)
    column = lambda k: pl.BlockSpec((rows, PAIR), lambda j: (0, k * heads + j))
    return pl.pallas_call(
        kernel,
        grid=(heads,),
        out_shape=jax.ShapeDtypeStruct((rows, width // 3), jnp.bfloat16),
        in_specs=[
            column(0),
            column(1),
            column(2),
            pl.BlockSpec((rows, 1), lambda j: (0, 0)),
            pl.BlockSpec((1, rows - start), lambda j: (0, 0)),
        ],
        out_specs=column(0),
        compiler_params=pltpu.CompilerParams(vmem_limit_bytes=48 << 20),
        name="attend",
    )(qkv, qkv, qkv, segment[:, None], segment[None, start:])


def attend_back_block(scale, query, key, value, grad_mixed, mask):
    halves = pair_halves(query.shape[0])
    grad_query, grad_key, grad_value = [], 0.0, 0.0
    for h in range(2):
        own = jnp.where(halves[h], query, jnp.zeros_like(query))
        grad = jnp.where(halves[h], grad_mixed, jnp.zeros_like(grad_mixed))
        scores = jnp.where(mask, nt(key, own) * scale, -1000000000.0)
        weights = jnp.exp(scores - jnp.max(scores, axis=0, keepdims=True))
        probs = weights * (1.0 / jnp.sum(weights, axis=0, keepdims=True))
        grad_probs = nt(value, grad)
        inner = jnp.sum(probs * grad_probs, axis=0, keepdims=True)
        grad_scores = (probs * (grad_probs - inner)).astype(jnp.bfloat16)
        grad_value = grad_value + nn(probs.astype(jnp.bfloat16), grad)
        grad_key = grad_key + nn(grad_scores, own)
        grad_query.append(tn(grad_scores, key))
    grad_query = jnp.where(halves[0], grad_query[0], grad_query[1])
    low = lambda value: value.astype(jnp.bfloat16)
    return low(grad_query * scale), low(grad_key * scale), low(grad_value)


def attend_back_kernel(
    scale, fine, start, query, key, value, grad_mixed, segment, segment_row, grad_qkv
):
    rows = query.shape[0]
    third = grad_qkv.shape[1] // 3
    column = pl.multiple_of(pl.program_id(0) * PAIR, PAIR)
    masks = block_masks(fine, start, rows, segment, segment_row, 0)
    for here, mask in zip((slice(0, start), slice(start, rows)), masks):
        grads = attend_back_block(
            scale, query[here, :], key[here, :], value[here, :], grad_mixed[here, :], mask
        )
        for k in range(3):
            grad_qkv[here, pl.ds(k * third + column, PAIR)] = grads[k]


def attend_back(qkv, grad_mixed, segment, fine, start):
    rows, width = qkv.shape
    heads = width // 3 // PAIR
    kernel = functools.partial(attend_back_kernel, 1.0 / math.sqrt(HD), fine, start)
    column = lambda k: pl.BlockSpec((rows, PAIR), lambda j: (0, k * heads + j))
    return pl.pallas_call(
        kernel,
        grid=(heads,),
        out_shape=jax.ShapeDtypeStruct((rows, width), jnp.bfloat16),
        in_specs=[
            column(0),
            column(1),
            column(2),
            column(0),
            pl.BlockSpec((rows, 1), lambda j: (0, 0)),
            pl.BlockSpec((1, rows - start), lambda j: (0, 0)),
        ],
        out_specs=pl.BlockSpec((rows, width), lambda j: (0, 0)),
        compiler_params=pltpu.CompilerParams(vmem_limit_bytes=48 << 20),
        name="attend_back",
    )(qkv, qkv, qkv, grad_mixed, segment[:, None], segment[None, start:])


LINE = 4
MESH_ID = pl.DeviceIdType.MESH
PIECE_ROWS = 192
PIECE_COLS = 384
CROSS_EVERY = 4
SEMS = 48


class Piece:
    def __init__(self, source, row, col, rows, cols, target, out_row, out_col, swap, cross):
        self.source, self.row, self.col, self.rows, self.cols = source, row, col, rows, cols
        self.target, self.out_row, self.out_col = target, out_row, out_col
        self.swap, self.cross = swap, cross


def sync_kernel(pieces, scale, in_count, out_count, *refs):
    grads = refs[:in_count]
    outs = refs[in_count : in_count + out_count]
    acc, land, land_right, land_left, sems = refs[in_count + out_count :]
    device = lax.axis_index("dp")
    core = lax.axis_index("tensor")
    place_x = lax.rem(device, 2)
    place_y = lax.rem(device // 2, 2)
    place_z = lax.rem(device // 4, LINE)
    mirror = LINE - 1 - place_z
    beside_x = (device + 1 - 2 * place_x, core)
    beside_y = (device + 2 - 4 * place_y, core)
    sibling = (device, 1 - core)
    up = (device + 4, core)
    down = (device - 4, core)

    barrier = pltpu.get_barrier_semaphore()
    for partner in (beside_x, beside_y, sibling):
        pl.semaphore_signal(barrier, inc=1, device_id=partner, device_id_type=MESH_ID)

    @pl.when(place_z < LINE - 1)
    def _():
        pl.semaphore_signal(barrier, inc=1, device_id=up, device_id_type=MESH_ID)

    @pl.when(place_z > 0)
    def _():
        pl.semaphore_signal(barrier, inc=1, device_id=down, device_id_type=MESH_ID)

    inner = (place_z + LINE - 1) // LINE + (2 * (LINE - 1) - place_z) // LINE
    pl.semaphore_wait(barrier, 3 + inner)

    def rows_at(ref, start, size, column, width):
        return ref.at[pl.ds(pl.multiple_of(start, 8), size), pl.ds(pl.multiple_of(column, 128), width)]

    def remote(src, dst, send, recv, where):
        return pltpu.make_async_remote_copy(
            src_ref=src,
            dst_ref=dst,
            send_sem=send,
            recv_sem=recv,
            device_id=where,
            device_id_type=MESH_ID,
        )

    def add_rows(total, start, extra, size, width, factor=None):
        step = 24 if size % 24 == 0 else 8

        @pl.loop(0, size // step)
        def _(i):
            here = pl.ds(pl.multiple_of(start + i * step, 8), step)
            there = pl.ds(pl.multiple_of(i * step, 8), step)
            value = total[here, :width] + extra[there, :width]
            total[here, :width] = value if factor is None else value * factor

    def build(number, piece):
        half, chunk, width = piece.rows // 2, piece.rows // 8, piece.cols
        grad, out = grads[piece.source], outs[piece.target]
        mine = acc.at[number]
        sem = lambda k: sems.at[number, k]

        def out_at(x, owner, row, size):
            return rows_at(out, piece.out_row(x, owner) + row, size, piece.out_col(x), width)

        def y_copy():
            return remote(
                rows_at(grad, piece.row + (1 - place_y) * half, half, piece.col, width),
                land.at[number, :half, :width],
                sem(0),
                sem(1),
                beside_y,
            )

        def load():
            return pltpu.make_async_copy(
                rows_at(grad, piece.row + place_y * half, half, piece.col, width),
                mine.at[:half, :width],
                sem(2),
            )

        def right(k):
            return remote(
                rows_at(mine, (LINE - k + place_z) * chunk, chunk, 0, width),
                land_right.at[number, k - 1, :chunk, :width],
                sem(2 + k),
                sem(5 + k),
                up,
            )

        def left(k):
            return remote(
                rows_at(mine, (k - 1 - mirror) * chunk, chunk, 0, width),
                land_left.at[number, k - 1, :chunk, :width],
                sem(8 + k),
                sem(11 + k),
                down,
            )

        def got(slots, k, first, where):
            here = slots.at[number, k - 1, :chunk, :width]
            return remote(here, here, sem(first + k), sem(first + 3 + k), where)

        def send_line(k):
            @pl.when((place_z <= k - 1) & (place_z < LINE - 1))
            def _():
                right(k).start()

            @pl.when((mirror <= k - 1) & (mirror < LINE - 1))
            def _():
                left(k).start()

        def wait_line(k):
            @pl.when((place_z >= 1) & (place_z <= k))
            def _():
                got(land_right, k, 2, down).wait_recv()
                add_rows(
                    mine, (LINE - 1 - k + place_z) * chunk, land_right.at[number, k - 1], chunk, width
                )

            @pl.when((mirror >= 1) & (mirror <= k))
            def _():
                got(land_left, k, 8, up).wait_recv()
                add_rows(mine, (k - mirror) * chunk, land_left.at[number, k - 1], chunk, width)

        def own_chunk():
            return rows_at(mine, place_z * chunk, chunk, 0, width)

        def store():
            return pltpu.make_async_copy(
                own_chunk(), out_at(place_x, core, place_y * half + place_z * chunk, chunk), sem(17)
            )

        def share_out():
            return remote(
                own_chunk(),
                out_at(place_x, core, place_y * half + place_z * chunk, chunk),
                sem(15),
                sem(16),
                beside_x if piece.cross else beside_y,
            )

        def share_in():
            if piece.cross:
                there = out_at(1 - place_x, core, place_y * half + place_z * chunk, chunk)
                return remote(there, there, sem(15), sem(16), beside_x)
            there = out_at(place_x, core, (1 - place_y) * half + place_z * chunk, chunk)
            return remote(there, there, sem(15), sem(16), beside_y)

        def spread(k, position, where, first):
            copies = []
            for b in range(2):
                if piece.cross:
                    here = out_at(b, core, place_y * half + position * chunk, chunk)
                else:
                    here = out_at(place_x, core, b * half + position * chunk, chunk)
                at = first + 2 * (k - 1) + b
                copies.append(remote(here, here, sem(at), sem(at + 6), where))
            return copies

        def send_spread(k):
            @pl.when((place_z >= k - 1) & (place_z < LINE - 1))
            def _():
                for copy in spread(k, place_z - (k - 1), up, 18):
                    copy.start()

            @pl.when((mirror >= k - 1) & (mirror < LINE - 1))
            def _():
                for copy in spread(k, place_z + (k - 1), down, 30):
                    copy.start()

        def wait_spread(k):
            @pl.when(place_z >= k)
            def _():
                for copy in spread(k, place_z - k, down, 18):
                    copy.wait_recv()

            @pl.when(mirror >= k)
            def _():
                for copy in spread(k, place_z + k, up, 30):
                    copy.wait_recv()

        def last(outgoing):
            if piece.cross:
                row = (place_y if outgoing else 1 - place_y) * half
                views = [out_at(b, core, row, half) for b in range(2)]
                return [
                    remote(v, v, sem(42 + b), sem(44 + b), beside_y) for b, v in enumerate(views)
                ]
            view = out_at(place_x if outgoing else 1 - place_x, core, 0, piece.rows)
            return [remote(view, view, sem(42), sem(44), beside_x)]

        def swap(owner):
            views = [out_at(b, owner, 0, piece.rows) for b in range(2)]
            return [remote(v, v, sem(46 + b), sem(48 + b), sibling) for b, v in enumerate(views)]

        def stage_0():
            y_copy().start()
            load().start()

        def stage_1():
            load().wait()
            y_copy().wait_recv()
            add_rows(mine, 0, land.at[number], half, width)
            send_line(1)

        def stage_2():
            wait_line(1)
            send_line(2)

        def stage_3():
            wait_line(2)
            send_line(3)

        def stage_4():
            wait_line(3)

            @pl.loop(0, chunk // 8)
            def _(i):
                here = pl.ds(pl.multiple_of(place_z * chunk + i * 8, 8), 8)
                mine[here, :width] = mine[here, :width] * scale

            share_out().start()
            store().start()

        def stage_5():
            store().wait()
            share_in().wait_recv()
            send_spread(1)

        def stage_6():
            wait_spread(1)
            send_spread(2)

        def stage_7():
            wait_spread(2)
            send_spread(3)

        def stage_8():
            wait_spread(3)
            for copy in last(True):
                copy.start()

        def stage_9():
            for copy in last(False):
                copy.wait_recv()
            if piece.swap:
                for copy in swap(core):
                    copy.start()

        def stage_10():
            if piece.swap:
                for copy in swap(1 - core):
                    copy.wait_recv()
                for copy in swap(core):
                    copy.wait_send()
            y_copy().wait_send()
            share_out().wait_send()
            for copy in last(True):
                copy.wait_send()
            for k in range(1, LINE):

                @pl.when((place_z <= k - 1) & (place_z < LINE - 1))
                def _():
                    right(k).wait_send()

                @pl.when((mirror <= k - 1) & (mirror < LINE - 1))
                def _():
                    left(k).wait_send()

                @pl.when((place_z >= k - 1) & (place_z < LINE - 1))
                def _():
                    for copy in spread(k, place_z - (k - 1), up, 18):
                        copy.wait_send()

                @pl.when((mirror >= k - 1) & (mirror < LINE - 1))
                def _():
                    for copy in spread(k, place_z + (k - 1), down, 30):
                        copy.wait_send()

        return [
            stage_0,
            stage_1,
            stage_2,
            stage_3,
            stage_4,
            stage_5,
            stage_6,
            stage_7,
            stage_8,
            stage_9,
            stage_10,
        ]

    lines = [build(number, piece) for number, piece in enumerate(pieces)]
    groups = [lines[i : i + GROUP] for i in range(0, len(lines), GROUP)]
    depth = len(lines[0])
    for j in range(min(AHEAD, len(groups))):
        for line in groups[j]:
            line[0]()
    late = depth - 2
    for tick in range(len(groups) + depth - 1):
        if tick + AHEAD < len(groups):
            for line in groups[tick + AHEAD]:
                line[0]()
        active = range(max(0, tick - depth + 1), min(tick, len(groups)))
        for j in [j for j in active if tick - j < late] + [j for j in active if tick - j >= late]:
            for line in groups[j]:
                line[tick - j]()


GROUP = 1
AHEAD = 1


def sync_plan(grads, outs):
    pieces = []
    for source, (rows, cols) in enumerate(grads):
        start = 0
        for target, width, row_x, row_core, col_x, block in outs[source]:
            tall = min(PIECE_ROWS, rows)
            wide = min(PIECE_COLS, width) if block is None else width
            for row in range(0, rows, tall):
                for col in range(0, width, wide) if block is None else range(1):
                    out_col = col if block is None else block
                    pieces.append(
                        Piece(
                            source,
                            row,
                            start + col,
                            tall,
                            wide,
                            target,
                            lambda x, core, row=row, a=row_x, b=row_core: row + x * a + core * b,
                            lambda x, c=out_col, a=col_x: c + x * a,
                            row_core != 0,
                            len(pieces) % CROSS_EVERY == CROSS_EVERY - 1,
                        )
                    )
            start += width
    return pieces


def sync_grads(grads, out_shapes, outs, replicas):
    pieces = sync_plan([g.shape for g in grads], outs)
    count = len(pieces)
    high = max(p.rows for p in pieces)
    wide = max(p.cols for p in pieces)
    kernel = functools.partial(sync_kernel, pieces, 1.0 / replicas, len(grads), len(out_shapes))
    vmem = lambda *dims: pltpu.VMEM(dims, jnp.float32)
    return pl.pallas_call(
        kernel,
        out_shape=[jax.ShapeDtypeStruct(s, jnp.float32) for s in out_shapes],
        in_specs=[pl.BlockSpec(memory_space=pl.ANY)] * len(grads),
        out_specs=[pl.BlockSpec(memory_space=pl.ANY)] * len(out_shapes),
        scratch_shapes=[
            vmem(count, high // 2, wide),
            vmem(count, high // 2, wide),
            vmem(count, LINE - 1, high // 8, wide),
            vmem(count, LINE - 1, high // 8, wide),
            pltpu.SemaphoreType.DMA((count, SEMS + 2)),
        ],
        compiler_params=pltpu.CompilerParams(
            collective_id=0, has_side_effects=True, vmem_limit_bytes=56 << 20
        ),
        name="sync_grads",
    )(*grads)


def tensor_sum(partial):
    return partial + lax.ppermute(partial, "tensor", [(0, 1), (1, 0)])


def from_partner(mine, core, replicas):
    there = [(i, i ^ 1) for i in range(replicas)]
    direct = lax.ppermute(mine, "dp", there)
    across = lax.ppermute(direct, "tensor", [(0, 1), (1, 0)])
    return direct, across


def merged_rows(fine_rows, light_rows, second, counts, start, stride, rows):
    width = fine_rows.shape[1]
    small = stride - stride % 4
    keep = jnp.arange(stride, dtype=jnp.int32)[:, None]
    fine = fine_rows.shape[0]
    padded = jnp.pad(light_rows, ((0, stride), (0, 0)))
    third = padded[:stride]
    fourth = lax.dynamic_slice_in_dim(padded, counts[2], stride, axis=0)
    blocks = [
        jnp.pad(fine_rows, ((0, start - fine), (0, 0))),
        jnp.pad(second, ((0, stride - second.shape[0]), (0, 0))),
        jnp.where(keep < counts[2], third, 0.0),
        jnp.where(keep < counts[3], fourth, 0.0),
        jnp.zeros((rows - start - 3 * stride, width), fine_rows.dtype),
    ]
    return jnp.concatenate(blocks, axis=0)


def own_rows(merged, is_fine, counts, fine, start, stride, rows):
    width = merged.shape[1]
    coarse = counts[1]
    heavy = jnp.concatenate(
        [
            merged[:fine],
            merged[start : start + stride],
            jnp.zeros((rows - fine - stride, width), merged.dtype),
        ],
        axis=0,
    )
    row = jnp.arange(rows, dtype=jnp.int32)[:, None]
    third = jnp.pad(merged[start + stride : start + 2 * stride], ((0, rows - stride), (0, 0)))
    fourth = jnp.pad(merged[start + 2 * stride : start + 3 * stride], ((stride, rows), (0, 0)))
    fourth = lax.dynamic_slice_in_dim(fourth, stride - counts[2], rows, axis=0)
    light = jnp.where(row < counts[2], third, fourth)
    used = jnp.where(is_fine, fine + coarse, counts[2] + counts[3])
    return jnp.where(row < used, jnp.where(is_fine, heavy, light), jnp.zeros_like(heavy))


def local(
    pixels,
    patch_size,
    counts,
    offsets,
    resize_table,
    pos_table,
    w_base,
    patch_bias,
    pos_base,
    gain_one,
    shift_one,
    w_query,
    bias_query,
    w_key,
    w_value,
    bias_value,
    w_out,
    bias_out,
    gain_two,
    shift_two,
    w_up,
    bias_up,
    w_down,
    bias_down,
    cotangent,
):
    wide = lambda value: value.astype(jnp.float32)
    images, channels, res, _ = pixels.shape
    rows_total = cotangent.shape[0]
    replicas = lax.axis_size("dp")
    core = lax.axis_index("tensor")
    side_x = lax.rem(lax.axis_index("dp"), 2)
    fine = (res // FINE) ** 2
    small = (res // COARSE[0]) ** 2
    start = up_to(fine, 16)
    stride = up_to(small, 8)
    rows = up_to(start + 3 * stride, 16)

    lane = jnp.arange(up_to(res, 128), dtype=jnp.int32)
    own_pix = jnp.pad(wide(pixels), ((0, 0), (0, 0), (0, 0), (0, -res % 128)))
    own_pix = jnp.where(lane == res, wide(patch_size)[:, None, None, None], own_pix)
    direct, across = from_partner(
        lax.dynamic_index_in_dim(own_pix, core, 0, keepdims=False), core, replicas
    )
    pix = jnp.concatenate([own_pix, direct[None], across[None]], axis=0)
    half_rows = rows_total // 2
    own_cotangent = wide(cotangent)
    cot_direct, cot_across = from_partner(
        lax.dynamic_slice_in_dim(own_cotangent, core * half_rows, half_rows, axis=0),
        core,
        replicas,
    )
    is_fine = patch_size[0] == FINE
    other = jnp.where(core == 0, jnp.array([2, 3], jnp.int32), jnp.array([3, 2], jnp.int32))
    order = jnp.where(
        is_fine,
        jnp.concatenate([jnp.array([0, 1], jnp.int32), other]),
        jnp.concatenate([other, jnp.array([0, 1], jnp.int32)]),
    )
    found = jnp.concatenate([patch_size, jnp.stack([direct[0, 0, res], across[0, 0, res]]).astype(jnp.int32)])
    sizes = jnp.take(found, order)
    counts4 = (res // sizes) ** 2
    table = jnp.take(resize_table, sizes, axis=0)
    pos_fine = pos_table[res // FINE, :fine]
    pos = jnp.take(pos_table[:, :small], res // sizes[1:], axis=0)

    row = jnp.arange(rows, dtype=jnp.int32)
    slot = jnp.where(row < start, 0, (row - start) // stride + 1)
    first = jnp.where(slot == 0, 0, start + (slot - 1) * stride)
    limit = jnp.where(
        slot == 0,
        counts4[0],
        jnp.where(slot == 1, counts4[1], jnp.where(slot == 2, counts4[2], counts4[3])),
    )
    valid = (slot < 4) & (row - first < limit)
    segment = jnp.where(valid, slot, 4)
    valid_rows = wide(valid)[:, None]

    embedded, tokens, patches, mixed_weight = embed(
        sizes, order, pix, table, pos_fine, pos, w_base, patch_bias, pos_base, rows
    )
    w_qkv = jnp.concatenate([w_query, w_key, w_value], axis=1)
    bias_qkv = jnp.concatenate([bias_query, jnp.zeros_like(bias_query), bias_value])
    standard_one, standard_back_one = jax.vjp(standardize, embedded)
    normed_one = (standard_one * wide(gain_one) + wide(shift_one)).astype(jnp.bfloat16)
    qkv = (
        jnp.dot(normed_one, w_qkv, preferred_element_type=jnp.float32) + wide(bias_qkv)
    ).astype(jnp.bfloat16)
    mixed = attend(qkv, segment, fine, start)
    attended = tensor_sum(jnp.dot(mixed, w_out, preferred_element_type=jnp.float32)) + wide(
        bias_out
    )
    middle = embedded + attended
    standard_two, standard_back_two = jax.vjp(standardize, middle)
    normed_two = (standard_two * wide(gain_two) + wide(shift_two)).astype(jnp.bfloat16)
    hidden = jnp.dot(normed_two, w_up, preferred_element_type=jnp.float32) + wide(bias_up)
    activated_wide, gelu_back = jax.vjp(jax.nn.gelu, hidden)
    activated = activated_wide.astype(jnp.bfloat16)
    branch = tensor_sum(jnp.dot(activated, w_down, preferred_element_type=jnp.float32)) + wide(
        bias_down
    )
    output = own_rows(
        (middle + branch).astype(jnp.bfloat16), is_fine, counts4, fine, start, stride, rows_total
    )
    other_cotangent = jnp.where(
        core == 0,
        jnp.concatenate([cot_direct, cot_across]),
        jnp.concatenate([cot_across, cot_direct]),
    )
    fine_cotangent = jnp.where(is_fine, own_cotangent, other_cotangent)
    light_cotangent = jnp.where(
        is_fine, other_cotangent[: 2 * stride], own_cotangent[: 2 * stride]
    )
    grad_out = (
        merged_rows(
            fine_cotangent[:fine],
            light_cotangent,
            fine_cotangent[fine : fine + small],
            counts4,
            start,
            stride,
            rows,
        )
        * valid_rows
    )
    grad_branch = grad_out.astype(jnp.bfloat16)
    own_part = lambda value: lax.dynamic_slice_in_dim(
        value, side_x * (value.shape[1] // 2), value.shape[1] // 2, axis=1
    )
    grad_w_down = jnp.einsum(
        "tf,td->fd", own_part(activated), grad_branch, preferred_element_type=jnp.float32
    )
    grad_activated = jnp.einsum(
        "td,fd->tf", grad_branch, w_down, preferred_element_type=jnp.float32
    )
    grad_hidden = gelu_back(grad_activated)[0].astype(jnp.bfloat16)
    grad_w_up = jnp.einsum(
        "td,tf->df", own_part(normed_two), grad_hidden, preferred_element_type=jnp.float32
    )
    grad_bias_up = jnp.sum(grad_hidden, axis=0, dtype=jnp.float32)
    grad_normed_two = tensor_sum(
        jnp.einsum("tf,df->td", grad_hidden, w_up, preferred_element_type=jnp.float32)
    )
    grad_middle = grad_out + standard_back_two(grad_normed_two * wide(gain_two))[0]
    grad_attended = grad_middle.astype(jnp.bfloat16)
    grad_w_out = jnp.einsum(
        "te,td->ed", own_part(mixed), grad_attended, preferred_element_type=jnp.float32
    )
    grad_mixed = jnp.einsum(
        "td,ed->te", grad_attended, w_out, preferred_element_type=jnp.float32
    ).astype(jnp.bfloat16)
    grad_qkv = attend_back(qkv, grad_mixed, segment, fine, start)
    grad_w_qkv = jnp.einsum(
        "td,te->de", own_part(normed_one), grad_qkv, preferred_element_type=jnp.float32
    )
    grad_bias_qkv = jnp.sum(grad_qkv, axis=0, dtype=jnp.float32)
    cut = bias_query.shape[0]
    grad_bias_query, grad_bias_value = grad_bias_qkv[:cut], grad_bias_qkv[2 * cut :]
    grad_normed_one = tensor_sum(
        jnp.einsum("te,de->td", grad_qkv, w_qkv, preferred_element_type=jnp.float32)
    )
    grad_embedded = grad_middle + standard_back_one(grad_normed_one * wide(gain_one))[0]
    grad_embedded_low = grad_embedded.astype(jnp.bfloat16)
    pixel_grad, grad_w_base, grad_pos_base = pixel_back(
        sizes,
        jnp.stack([core, side_x, is_fine.astype(jnp.int32)]),
        grad_embedded,
        table,
        pos_fine,
        pos,
        w_base,
        tokens,
        patches,
        mixed_weight,
        pixels.shape,
    )
    grad_patch_bias = jnp.sum(grad_embedded_low, axis=0, dtype=jnp.float32)
    grad_gain_one = jnp.sum(grad_normed_one * standard_one, axis=0)
    grad_shift_one = jnp.sum(grad_normed_one, axis=0)
    grad_bias_out = jnp.sum(grad_attended, axis=0, dtype=jnp.float32)
    grad_gain_two = jnp.sum(grad_normed_two * standard_two, axis=0)
    grad_shift_two = jnp.sum(grad_normed_two, axis=0)
    grad_bias_down = jnp.sum(grad_branch, axis=0, dtype=jnp.float32)
    width = grad_patch_bias.shape[0]
    small_rows = [
        grad_pos_base,
        grad_patch_bias[None],
        grad_gain_one[None],
        grad_shift_one[None],
        grad_bias_out[None],
        grad_gain_two[None],
        grad_shift_two[None],
        grad_bias_down[None],
        jnp.concatenate([grad_bias_query, grad_bias_value])[None],
        grad_bias_up.reshape(-1, width),
    ]
    bundle = jnp.concatenate(small_rows, axis=0)
    used = bundle.shape[0]
    bundle = jnp.pad(bundle, ((0, -used % 128), (0, 0)))
    bundle_part = lax.dynamic_slice_in_dim(
        bundle, side_x * (bundle.shape[0] // 2), bundle.shape[0] // 2, axis=0
    )
    parts = [grad_w_down, grad_w_up, grad_w_qkv, grad_w_base, grad_w_out, bundle_part]
    beyond = replicas // 16
    step = 1
    while step < beyond:
        swap = [(i, (i // 16 ^ step) * 16 + i % 16) for i in range(replicas)]
        parts = [part + lax.ppermute(part, "dp", swap) for part in parts]
        step *= 2
    area = w_base.shape[1] // channels
    base_shape = (2 * grad_w_base.shape[0], w_base.shape[1])
    ff = w_down.shape[0]
    deep = w_up.shape[0]
    out_shapes = [
        base_shape,
        w_down.shape,
        w_up.shape,
        w_query.shape,
        w_key.shape,
        w_value.shape,
        w_out.shape,
        bundle.shape,
    ]
    outs = [
        [(1, width, ff // 2, 0, 0, None)],
        [(2, ff, deep // 2, 0, 0, None)],
        [(3 + k, cut, deep // 2, 0, 0, None) for k in range(3)],
        [(0, area // 2, 0, width // 2, area // 2, area * c) for c in range(channels)],
        [(6, width, cut // 2, 0, 0, None)],
        [(7, width, bundle.shape[0] // 2, 0, 0, None)],
    ]
    synced = sync_grads(parts, out_shapes, outs, replicas)
    base_s, down_s, up_s, query_s, key_s, value_s, out_s, small_s = synced
    points = pos.shape[2]
    line = lambda k: small_s[points + k]
    return (
        output,
        pixel_grad,
        base_s,
        line(0),
        small_s[:points].T,
        line(1),
        line(2),
        query_s,
        line(7)[:cut],
        key_s,
        value_s,
        line(7)[cut:],
        out_s,
        line(3),
        line(4),
        line(5),
        up_s,
        small_s[points + 8 : used].reshape(-1),
        down_s,
        line(6),
    )


def solution(mesh):
    in_specs = (
        P("dp", None, None, None),
        P("dp"),
        P("dp"),
        P("dp"),
        P(),
        P(),
        P(),
        P(),
        P(),
        P(),
        P(),
        P(None, "tensor"),
        P("tensor"),
        P(None, "tensor"),
        P(None, "tensor"),
        P("tensor"),
        P("tensor", None),
        P(),
        P(),
        P(),
        P(None, "tensor"),
        P("tensor"),
        P("tensor", None),
        P(),
        P("dp", None),
    )
    out_specs = (
        P("dp", None),
        P("dp", None, None, None),
        P(),
        P(),
        P(),
        P(),
        P(),
        P(None, "tensor"),
        P("tensor"),
        P(None, "tensor"),
        P(None, "tensor"),
        P("tensor"),
        P("tensor", None),
        P(),
        P(),
        P(),
        P(None, "tensor"),
        P("tensor"),
        P("tensor", None),
        P(),
    )
    return jax.shard_map(local, mesh=mesh, in_specs=in_specs, out_specs=out_specs, check_vma=False)
```

```python
import functools
import math

import jax
import jax.numpy as jnp
from jax import lax
from jax.experimental import pallas as pl
from jax.experimental.pallas import tpu as pltpu
from jax.sharding import PartitionSpec as P

HD = 64
VMEM = pl.BlockSpec(memory_space=pltpu.VMEM)
SMEM = pl.BlockSpec(memory_space=pltpu.SMEM)


def standardize(values):
    centered = values - jnp.mean(values, axis=-1, keepdims=True)
    spread = jnp.mean(centered * centered, axis=-1, keepdims=True)
    return centered * lax.rsqrt(spread + 1e-06)


FINE = 8
COARSE = (24, 30, 40, 48)


def nt(left, right):
    return lax.dot_general(left, right, (((1,), (1,)), ((), ())), preferred_element_type=jnp.float32)


def tn(left, right):
    return lax.dot_general(left, right, (((0,), (0,)), ((), ())), preferred_element_type=jnp.float32)


def nn(left, right):
    return jnp.dot(left, right, preferred_element_type=jnp.float32)


def up_to(value, step):
    return value + -value % step


def loop(count, body, unroll):
    if unroll:
        for i in range(count):
            body(i)
    else:
        pl.loop(0, count)(body)


def aligned(start, side):
    return pl.multiple_of(start, 8) if side % 8 == 0 and not isinstance(start, int) else start


def fill_pairs(pair, long, table, side):
    base = table.shape[1]
    entry = lax.broadcasted_iota(jnp.int32, (base, base * base), 0)
    place = lax.broadcasted_iota(jnp.int32, (base, base * base), 1)
    repeat = (place // base == entry).astype(jnp.bfloat16)
    tile = (place % base == entry).astype(jnp.bfloat16)
    wide = nn(table, repeat)[:side]
    long[...] = nn(table, tile)

    def one(s):
        pair[pl.ds(aligned(s * side, side), side), :] = wide * long[pl.ds(s, 1), :]

    loop(side, one, True)


def cut_patches(line, pix, image, channel, side, grid, res):
    def one(x):
        block = pix[image, channel, pl.ds(aligned(x * side, side), side), :]
        line[pl.ds(aligned(x * res, 8), res), :side] = block.T[:res]

    loop(grid, one, True)
    return jnp.concatenate(
        [line[pl.ds(s, grid * grid, stride=side), :side] for s in range(side)], axis=1
    ).astype(jnp.bfloat16)


def place_patches(line, pixel_grad, image, channel, patch, side, grid, res):
    for s in range(side):
        line[pl.ds(s, grid * grid, stride=side), :side] = patch[:, s * side : (s + 1) * side]

    def one(x):
        block = line[pl.ds(aligned(x * res, 8), res), :side]
        pixel_grad[image, channel, pl.ds(aligned(x * side, side), side), :] = block.T

    loop(grid, one, True)


def embed_kernel(
    sizes,
    order,
    pix,
    table,
    pos_fine,
    pos,
    weight,
    bias,
    pos_base,
    emb,
    tokens,
    patches,
    mixed_weight,
    fine_pairs,
    line,
    pair,
    long,
):
    area = table.shape[2] ** 2
    channels, res = pix.shape[1:3]
    grid = res // FINE
    count = grid * grid
    start = up_to(count, 16)
    stride = tokens.shape[1]
    low = jnp.bfloat16
    emb[...] = jnp.broadcast_to(bias[...], emb.shape)
    tokens[...] = jnp.zeros_like(tokens)

    fill_pairs(pair, long, table[0], FINE)
    fine_pairs[...] = pair[: FINE * FINE, :].astype(low)
    emb[:count, :] += nt(pos_fine[...], pos_base[...])

    @functools.partial(loop, channels, unroll=True)
    def _(c):
        columns = pl.ds(c * area, area)
        patch = cut_patches(line, pix, order[0], c, FINE, grid, res)
        mixed = nt(fine_pairs[...], weight[:, columns]).astype(low)
        mixed_weight[c] = mixed
        patches[c, :count, :] = patch
        emb[:count, :] += nn(patch, mixed)

    @pl.loop(1, 4)
    def _(slot):
        row = pl.multiple_of(start + (slot - 1) * stride, 8)
        for side in COARSE:
            grid = res // side
            count = grid * grid

            @pl.when(sizes[slot] == side)
            def _():
                fill_pairs(pair, long, table[slot], side)
                here = pl.ds(row, count)
                emb[here, :] += nt(pos[slot - 1, :count, :], pos_base[...])

                @functools.partial(loop, channels, unroll=True)
                def _(c):
                    columns = pl.ds(c * area, area)
                    patch = cut_patches(line, pix, order[slot], c, side, grid, res)
                    token = nn(patch, pair[: side * side, :].astype(low)).astype(low)
                    tokens[slot - 1, :count, columns] = token
                    emb[here, :] += nt(token, weight[:, columns])


def embed(sizes, order, pix, table, pos_fine, pos, w_base, patch_bias, pos_base, rows):
    _, channels, res, _ = pix.shape
    width, features = w_base.shape
    fine = (res // FINE) ** 2
    side = table.shape[1]
    area = features // channels
    return pl.pallas_call(
        embed_kernel,
        out_shape=[
            jax.ShapeDtypeStruct((rows, width), jnp.float32),
            jax.ShapeDtypeStruct((3, up_to(pos.shape[1], 8), features), jnp.bfloat16),
            jax.ShapeDtypeStruct((channels, up_to(fine, 16), FINE * FINE), jnp.bfloat16),
            jax.ShapeDtypeStruct((channels, FINE * FINE, width), jnp.bfloat16),
            jax.ShapeDtypeStruct((FINE * FINE, area), jnp.bfloat16),
        ],
        in_specs=[SMEM] * 2 + [VMEM] * 7,
        out_specs=[VMEM] * 5,
        scratch_shapes=[
            pltpu.VMEM((res * res // FINE, 128), jnp.float32),
            pltpu.VMEM((side * side, area), jnp.float32),
            pltpu.VMEM((side, area), jnp.float32),
        ],
        compiler_params=pltpu.CompilerParams(vmem_limit_bytes=48 << 20),
        name="embed",
    )(
        sizes,
        order,
        pix,
        table,
        pos_fine,
        pos,
        w_base,
        patch_bias.astype(jnp.float32)[None],
        pos_base,
    )


def pixel_kernel(sizes, is_fine, grad, table, weight, mixed_weight, pixel_grad, line, pair, long):
    area = table.shape[2] ** 2
    channels, res = pixel_grad.shape[1:3]
    start = up_to((res // FINE) ** 2, 16)
    stride = up_to((res // COARSE[0]) ** 2, 8)
    low = jnp.bfloat16

    @pl.when(is_fine[0] == 1)
    def _():
        grid = res // FINE
        count = grid * grid
        for c in range(channels):
            patch = nt(grad[:count, :].astype(low), mixed_weight[c])
            place_patches(line, pixel_grad, 0, c, patch, FINE, grid, res)

    @pl.loop(1, 4)
    def _(slot):
        row = pl.multiple_of(start + (slot - 1) * stride, 8)
        wanted = jnp.where(slot == 1, is_fine[0], 1 - is_fine[0])
        image = jnp.where(slot == 1, 1, slot - 2)
        for side in COARSE:
            grid = res // side
            count = grid * grid

            @pl.when((sizes[slot] == side) & (wanted == 1))
            def _():
                fill_pairs(pair, long, table[slot], side)
                rows = grad[pl.ds(row, count), :].astype(low)

                @pl.loop(0, channels)
                def _(c):
                    columns = pl.ds(pl.multiple_of(c * area, area), area)
                    token = nn(rows, weight[:, columns]).astype(low)
                    patch = nt(token, pair[: side * side, :].astype(low))
                    place_patches(line, pixel_grad, image, c, patch, side, grid, res)


def pixel_back(sizes, is_fine, grad, table, w_base, mixed_weight, shape):
    _, channels, res, _ = shape
    width, features = w_base.shape
    side = table.shape[1]
    return pl.pallas_call(
        pixel_kernel,
        out_shape=jax.ShapeDtypeStruct(shape, jnp.float32),
        in_specs=[SMEM] * 2 + [VMEM] * 4,
        out_specs=VMEM,
        scratch_shapes=[
            pltpu.VMEM((res * res // FINE, 128), jnp.float32),
            pltpu.VMEM((side * side, features // channels), jnp.float32),
            pltpu.VMEM((side, features // channels), jnp.float32),
        ],
        compiler_params=pltpu.CompilerParams(vmem_limit_bytes=40 << 20),
        name="pixel_back",
    )(sizes, is_fine, grad, table, w_base, mixed_weight)


PAIR = 2 * HD


def pair_halves(rows):
    lane = lax.broadcasted_iota(jnp.int32, (rows, PAIR), 1)
    return [lane < HD, lane >= HD]


def attend_block(scale, query, key, value, mask):
    halves = pair_halves(query.shape[0])
    both = []
    for h in range(2):
        own = jnp.where(halves[h], query, jnp.zeros_like(query))
        scores = jnp.where(mask, nt(own, key) * scale, -1000000000.0)
        weights = jnp.exp(scores - jnp.max(scores, axis=1, keepdims=True))
        inverse = 1.0 / jnp.sum(weights, axis=1, keepdims=True)
        both.append(nn((weights * inverse).astype(jnp.bfloat16), value))
    return jnp.where(halves[0], both[0], both[1]).astype(jnp.bfloat16)


def block_masks(fine, start, rows, segment, segment_row, axis):
    inside = lax.broadcasted_iota(jnp.int32, (start, start), axis) < fine
    same = segment[start:rows, :] == segment_row[:, : rows - start]
    return inside, same


def attend_kernel(scale, fine, start, query, key, value, segment, segment_row, mixed):
    rows = query.shape[0]
    masks = block_masks(fine, start, rows, segment, segment_row, 1)
    for here, mask in zip((slice(0, start), slice(start, rows)), masks):
        mixed[here, :] = attend_block(scale, query[here, :], key[here, :], value[here, :], mask)


def attend(qkv, segment, fine, start):
    rows, width = qkv.shape
    heads = width // 3 // PAIR
    kernel = functools.partial(attend_kernel, 1.0 / math.sqrt(HD), fine, start)
    column = lambda k: pl.BlockSpec((rows, PAIR), lambda j: (0, k * heads + j))
    return pl.pallas_call(
        kernel,
        grid=(heads,),
        out_shape=jax.ShapeDtypeStruct((rows, width // 3), jnp.bfloat16),
        in_specs=[
            column(0),
            column(1),
            column(2),
            pl.BlockSpec((rows, 1), lambda j: (0, 0)),
            pl.BlockSpec((1, rows - start), lambda j: (0, 0)),
        ],
        out_specs=column(0),
        compiler_params=pltpu.CompilerParams(vmem_limit_bytes=48 << 20),
        name="attend",
    )(qkv, qkv, qkv, segment[:, None], segment[None, start:])


def attend_back_block(scale, query, key, value, grad_mixed, mask):
    halves = pair_halves(query.shape[0])
    grad_query, grad_key, grad_value = [], 0.0, 0.0
    for h in range(2):
        own = jnp.where(halves[h], query, jnp.zeros_like(query))
        grad = jnp.where(halves[h], grad_mixed, jnp.zeros_like(grad_mixed))
        scores = jnp.where(mask, nt(key, own) * scale, -1000000000.0)
        weights = jnp.exp(scores - jnp.max(scores, axis=0, keepdims=True))
        probs = weights * (1.0 / jnp.sum(weights, axis=0, keepdims=True))
        grad_probs = nt(value, grad)
        inner = jnp.sum(probs * grad_probs, axis=0, keepdims=True)
        grad_scores = (probs * (grad_probs - inner)).astype(jnp.bfloat16)
        grad_value = grad_value + nn(probs.astype(jnp.bfloat16), grad)
        grad_key = grad_key + nn(grad_scores, own)
        grad_query.append(tn(grad_scores, key))
    grad_query = jnp.where(halves[0], grad_query[0], grad_query[1])
    return grad_query * scale, grad_key * scale, grad_value


LINE = 4
MESH_ID = pl.DeviceIdType.MESH
PIECE_ROWS = 192
PIECE_COLS = 384
CROSS_EVERY = 4
SEMS = 48


class Piece:
    def __init__(self, source, row, col, rows, cols, target, out_row, out_col, swap, cross):
        self.source, self.row, self.col, self.rows, self.cols = source, row, col, rows, cols
        self.target, self.out_row, self.out_col = target, out_row, out_col
        self.swap, self.cross = swap, cross


def move_pieces(pieces, scale, grads, outs, acc, land, land_right, land_left, sems, prepare):
    device = lax.axis_index("dp")
    core = lax.axis_index("tensor")
    place_x = lax.rem(device, 2)
    place_y = lax.rem(device // 2, 2)
    place_z = lax.rem(device // 4, LINE)
    mirror = LINE - 1 - place_z
    beside_x = (device + 1 - 2 * place_x, core)
    beside_y = (device + 2 - 4 * place_y, core)
    sibling = (device, 1 - core)
    up = (device + 4, core)
    down = (device - 4, core)

    barrier = pltpu.get_barrier_semaphore()
    for partner in (beside_x, beside_y, sibling):
        pl.semaphore_signal(barrier, inc=1, device_id=partner, device_id_type=MESH_ID)

    @pl.when(place_z < LINE - 1)
    def _():
        pl.semaphore_signal(barrier, inc=1, device_id=up, device_id_type=MESH_ID)

    @pl.when(place_z > 0)
    def _():
        pl.semaphore_signal(barrier, inc=1, device_id=down, device_id_type=MESH_ID)

    inner = (place_z + LINE - 1) // LINE + (2 * (LINE - 1) - place_z) // LINE
    pl.semaphore_wait(barrier, 3 + inner)

    def remote(src, dst, send, recv, where):
        return pltpu.make_async_remote_copy(
            src_ref=src,
            dst_ref=dst,
            send_sem=send,
            recv_sem=recv,
            device_id=where,
            device_id_type=MESH_ID,
        )

    work = prepare(core, place_x, sibling, remote)

    def rows_at(ref, start, size, column, width):
        return ref.at[pl.ds(pl.multiple_of(start, 8), size), pl.ds(pl.multiple_of(column, 128), width)]

    def add_rows(total, start, extra, size, width, factor=None):
        step = 24 if size % 24 == 0 else 8

        @pl.loop(0, size // step)
        def _(i):
            here = pl.ds(pl.multiple_of(start + i * step, 8), step)
            there = pl.ds(pl.multiple_of(i * step, 8), step)
            value = total[here, :width] + extra[there, :width]
            total[here, :width] = value if factor is None else value * factor

    def build(number, piece):
        half, chunk, width = piece.rows // 2, piece.rows // 8, piece.cols
        grad, out = grads[piece.source], outs[piece.target]
        mine = acc.at[number]
        sem = lambda k: sems.at[number, k]

        def out_at(x, owner, row, size):
            return rows_at(out, piece.out_row(x, owner) + row, size, piece.out_col(x), width)

        def y_copy():
            return remote(
                rows_at(grad, piece.row(place_x) + (1 - place_y) * half, half, piece.col, width),
                land.at[number, :half, :width],
                sem(0),
                sem(1),
                beside_y,
            )

        def load():
            return pltpu.make_async_copy(
                rows_at(grad, piece.row(place_x) + place_y * half, half, piece.col, width),
                mine.at[:half, :width],
                sem(2),
            )

        def right(k):
            return remote(
                rows_at(mine, (LINE - k + place_z) * chunk, chunk, 0, width),
                land_right.at[number, k - 1, :chunk, :width],
                sem(2 + k),
                sem(5 + k),
                up,
            )

        def left(k):
            return remote(
                rows_at(mine, (k - 1 - mirror) * chunk, chunk, 0, width),
                land_left.at[number, k - 1, :chunk, :width],
                sem(8 + k),
                sem(11 + k),
                down,
            )

        def got(slots, k, first, where):
            here = slots.at[number, k - 1, :chunk, :width]
            return remote(here, here, sem(first + k), sem(first + 3 + k), where)

        def send_line(k):
            @pl.when((place_z <= k - 1) & (place_z < LINE - 1))
            def _():
                right(k).start()

            @pl.when((mirror <= k - 1) & (mirror < LINE - 1))
            def _():
                left(k).start()

        def wait_line(k):
            @pl.when((place_z >= 1) & (place_z <= k))
            def _():
                got(land_right, k, 2, down).wait_recv()
                add_rows(
                    mine, (LINE - 1 - k + place_z) * chunk, land_right.at[number, k - 1], chunk, width
                )

            @pl.when((mirror >= 1) & (mirror <= k))
            def _():
                got(land_left, k, 8, up).wait_recv()
                add_rows(mine, (k - mirror) * chunk, land_left.at[number, k - 1], chunk, width)

        def own_chunk():
            return rows_at(mine, place_z * chunk, chunk, 0, width)

        def store():
            return pltpu.make_async_copy(
                own_chunk(), out_at(place_x, core, place_y * half + place_z * chunk, chunk), sem(17)
            )

        def share_out():
            return remote(
                own_chunk(),
                out_at(place_x, core, place_y * half + place_z * chunk, chunk),
                sem(15),
                sem(16),
                beside_x if piece.cross else beside_y,
            )

        def share_in():
            if piece.cross:
                there = out_at(1 - place_x, core, place_y * half + place_z * chunk, chunk)
                return remote(there, there, sem(15), sem(16), beside_x)
            there = out_at(place_x, core, (1 - place_y) * half + place_z * chunk, chunk)
            return remote(there, there, sem(15), sem(16), beside_y)

        def spread(k, position, where, first):
            copies = []
            for b in range(2):
                if piece.cross:
                    here = out_at(b, core, place_y * half + position * chunk, chunk)
                else:
                    here = out_at(place_x, core, b * half + position * chunk, chunk)
                at = first + 2 * (k - 1) + b
                copies.append(remote(here, here, sem(at), sem(at + 6), where))
            return copies

        def send_spread(k):
            @pl.when((place_z >= k - 1) & (place_z < LINE - 1))
            def _():
                for copy in spread(k, place_z - (k - 1), up, 18):
                    copy.start()

            @pl.when((mirror >= k - 1) & (mirror < LINE - 1))
            def _():
                for copy in spread(k, place_z + (k - 1), down, 30):
                    copy.start()

        def wait_spread(k):
            @pl.when(place_z >= k)
            def _():
                for copy in spread(k, place_z - k, down, 18):
                    copy.wait_recv()

            @pl.when(mirror >= k)
            def _():
                for copy in spread(k, place_z + k, up, 30):
                    copy.wait_recv()

        def last(outgoing):
            if piece.cross:
                row = (place_y if outgoing else 1 - place_y) * half
                views = [out_at(b, core, row, half) for b in range(2)]
                return [
                    remote(v, v, sem(42 + b), sem(44 + b), beside_y) for b, v in enumerate(views)
                ]
            view = out_at(place_x if outgoing else 1 - place_x, core, 0, piece.rows)
            return [remote(view, view, sem(42), sem(44), beside_x)]

        def swap(owner):
            views = [out_at(b, owner, 0, piece.rows) for b in range(2)]
            return [remote(v, v, sem(46 + b), sem(48 + b), sibling) for b, v in enumerate(views)]

        def stage_0():
            y_copy().start()
            load().start()

        def stage_1():
            load().wait()
            y_copy().wait_recv()
            add_rows(mine, 0, land.at[number], half, width)
            send_line(1)

        def stage_2():
            wait_line(1)
            send_line(2)

        def stage_3():
            wait_line(2)
            send_line(3)

        def stage_4():
            wait_line(3)

            @pl.loop(0, chunk // 8)
            def _(i):
                here = pl.ds(pl.multiple_of(place_z * chunk + i * 8, 8), 8)
                mine[here, :width] = mine[here, :width] * scale

            share_out().start()
            store().start()

        def stage_5():
            store().wait()
            share_in().wait_recv()
            send_spread(1)

        def stage_6():
            wait_spread(1)
            send_spread(2)

        def stage_7():
            wait_spread(2)
            send_spread(3)

        def stage_8():
            wait_spread(3)
            for copy in last(True):
                copy.start()

        def stage_9():
            for copy in last(False):
                copy.wait_recv()
            if piece.swap:
                for copy in swap(core):
                    copy.start()

        def stage_10():
            if piece.swap:
                for copy in swap(1 - core):
                    copy.wait_recv()
                for copy in swap(core):
                    copy.wait_send()
            y_copy().wait_send()
            share_out().wait_send()
            for copy in last(True):
                copy.wait_send()
            for k in range(1, LINE):

                @pl.when((place_z <= k - 1) & (place_z < LINE - 1))
                def _():
                    right(k).wait_send()

                @pl.when((mirror <= k - 1) & (mirror < LINE - 1))
                def _():
                    left(k).wait_send()

                @pl.when((place_z >= k - 1) & (place_z < LINE - 1))
                def _():
                    for copy in spread(k, place_z - (k - 1), up, 18):
                        copy.wait_send()

                @pl.when((mirror >= k - 1) & (mirror < LINE - 1))
                def _():
                    for copy in spread(k, place_z + (k - 1), down, 30):
                        copy.wait_send()

        return [
            stage_0,
            stage_1,
            stage_2,
            stage_3,
            stage_4,
            stage_5,
            stage_6,
            stage_7,
            stage_8,
            stage_9,
            stage_10,
        ]

    lines = [build(number, piece) for number, piece in enumerate(pieces)]
    groups = [lines[i : i + GROUP] for i in range(0, len(lines), GROUP)]
    depth = len(lines[0])
    for j in range(min(AHEAD, len(groups))):
        for line in groups[j]:
            line[0]()
    late = depth - 2
    for tick in range(len(groups) + depth - 1):
        if tick + AHEAD < len(groups):
            for line in groups[tick + AHEAD]:
                line[0]()
        for job in work.pop(0) if work else ():
            job()
        active = range(max(0, tick - depth + 1), min(tick, len(groups)))
        for j in [j for j in active if tick - j < late] + [j for j in active if tick - j >= late]:
            for line in groups[j]:
                line[tick - j]()


GROUP = 1
AHEAD = 1


def sync_plan(grads, outs):
    pieces = []
    for source, (rows, cols, step_x) in enumerate(grads):
        start = 0
        for target, width, row_x, row_core, col_x, out_start in outs[source]:
            tall = min(PIECE_ROWS, rows)
            wide = min(PIECE_COLS, width)
            if width % wide:
                wide = width // 2
            for row in range(0, rows, tall):
                for col in range(0, width, wide):
                    pieces.append(
                        Piece(
                            source,
                            lambda x, row=row, a=step_x: row + x * a,
                            start + col,
                            tall,
                            wide,
                            target,
                            lambda x, core, row=row, a=row_x, b=row_core: row + x * a + core * b,
                            lambda x, c=out_start + col, a=col_x: c + x * a,
                            row_core != 0,
                            len(pieces) % CROSS_EVERY == CROSS_EVERY - 1,
                        )
                    )
            start += width
    return pieces


QUERY_BLOCK = 384
LN_ROWS = 112
POINT_ROWS = 64


def back_kernel(pieces, sizes, fine, start, points, counts, *refs):
    replicas, given = counts
    (
        qkv,
        grad_mixed,
        segment,
        segment_row,
        normed_part,
        w_qkv,
        standard,
        inverse,
        grad_middle,
        gain,
        tokens,
        patches,
        fine_pairs,
        pos_fine,
        pos,
        rest,
    ) = refs[:16]
    early = refs[16 : 16 + given]
    refs = refs[16 + given :]
    outs, grad_embedded, refs = refs[:sizes], refs[sizes], refs[sizes + 1 :]
    (
        grad_qkv,
        grad_key,
        grad_value,
        partial,
        arrived,
        grad_w_qkv,
        grad_w_base,
        bundle,
        acc,
        land,
        land_right,
        land_left,
        sems,
        swap_sems,
        chunk_standard,
        chunk_middle,
        chunk_sems,
    ) = refs
    rows, width = standard.shape
    third = qkv.shape[1] // 3
    scale = 1.0 / math.sqrt(HD)
    low = lambda value: value.astype(jnp.bfloat16)
    blocks = range(0, rows, LN_ROWS)

    def prepare(core, place_x, sibling, remote):
        def back_rows(pair, here, keys, mask):
            column = lambda k: slice(k * third + pair * PAIR, k * third + (pair + 1) * PAIR)
            return attend_back_block(
                scale,
                qkv[here, column(0)],
                qkv[keys, column(1)],
                qkv[keys, column(2)],
                grad_mixed[here, column(0)],
                mask,
            )

        def store_qkv(pair, k, here, value):
            grad_qkv[here, k * third + pair * PAIR : k * third + (pair + 1) * PAIR] = low(value)

        def fine_job(pair, begin):
            def job():
                here = slice(begin, min(begin + QUERY_BLOCK, start))
                keys = slice(0, start)
                inside = lax.broadcasted_iota(jnp.int32, (start, here.stop - begin), 0) < fine
                grad_q, grad_k, grad_v = back_rows(pair, here, keys, inside)
                store_qkv(pair, 0, here, grad_q)
                if begin == 0:
                    grad_key[...] = grad_k
                    grad_value[...] = grad_v
                else:
                    grad_key[...] += grad_k
                    grad_value[...] += grad_v
                if here.stop == start:
                    store_qkv(pair, 1, keys, grad_key[...])
                    store_qkv(pair, 2, keys, grad_value[...])

            return job

        def coarse_job(pair):
            def job():
                here = slice(start, rows)
                same = segment[here, :] == segment_row[...]
                for k, value in enumerate(back_rows(pair, here, here, same)):
                    store_qkv(pair, k, here, value)

            return job

        def weight_job():
            grad_w_qkv[...] = tn(normed_part[...], grad_qkv[...])

        def partial_job():
            partial[...] = nt(grad_qkv[...], w_qkv[...])
            swap().start()

        def swap():
            return remote(partial, arrived, swap_sems.at[0], swap_sems.at[1], sibling)

        def chunk_copies(number):
            here = pl.ds(pl.multiple_of(number * LN_ROWS, 8), LN_ROWS)
            at = lax.rem(number, 2)
            return [
                pltpu.make_async_copy(standard.at[here], chunk_standard.at[at], chunk_sems.at[0, at]),
                pltpu.make_async_copy(
                    grad_middle.at[here], chunk_middle.at[at], chunk_sems.at[1, at]
                ),
            ]

        def norm_job():
            swap().wait()
            for copy in chunk_copies(0):
                copy.start()
            for k in range(3):
                bundle[points + k : points + k + 1, :] = jnp.zeros((1, width), jnp.float32)

            @pl.loop(0, len(blocks))
            def _(number):
                @pl.when(number + 1 < len(blocks))
                def _():
                    for copy in chunk_copies(number + 1):
                        copy.start()

                for copy in chunk_copies(number):
                    copy.wait()
                at = lax.rem(number, 2)

                @pl.loop(0, LN_ROWS // 16)
                def _(i):
                    inner = pl.ds(pl.multiple_of(i * 16, 8), 16)
                    here = pl.ds(pl.multiple_of(number * LN_ROWS + i * 16, 8), 16)
                    grad = partial[here, :] + arrived[here, :]
                    z = chunk_standard[at, inner, :]
                    up = grad * gain[...]
                    mean = jnp.mean(up, axis=1, keepdims=True)
                    along = jnp.mean(up * z, axis=1, keepdims=True)
                    value = (
                        chunk_middle[at, inner, :] + (up - mean - z * along) * inverse[here, :]
                    )
                    grad_embedded[here, :] = value
                    column = lambda v: jnp.sum(v, axis=0, keepdims=True)
                    bundle[points : points + 1, :] += column(low(value).astype(jnp.float32))
                    bundle[points + 1 : points + 2, :] += column(grad * z)
                    bundle[points + 2 : points + 3, :] += column(grad)

        def base_job():
            half = grad_w_base.shape[0]
            channels = patches.shape[0]
            part = grad_w_base.shape[1] // channels
            area = 2 * part
            columns = pl.ds(pl.multiple_of(core * half, 128), half)
            stride = tokens.shape[1]
            some = low(grad_embedded[:fine, columns])
            wanted = fine_pairs[:, pl.ds(pl.multiple_of(place_x * part, 128), part)]
            for c in range(channels):
                gathered = low(tn(patches[c, :fine, :], some))
                total = tn(gathered, wanted)
                for k in range(3):
                    begin = start + k * stride
                    here = pl.ds(pl.multiple_of(c * area + place_x * part, 128), part)
                    total += tn(low(grad_embedded[begin : begin + stride, columns]), tokens[k, :, here])
                grad_w_base[:, c * part : (c + 1) * part] = total

        def bundle_job():
            gathered = tn(pos_fine[...], low(grad_embedded[:fine, :]))
            count = pos.shape[1]
            for k in range(3):
                begin = start + k * tokens.shape[1]
                gathered += tn(pos[k], low(grad_embedded[begin : begin + count, :]))
            bundle[:points, :] = gathered
            bundle[points + 3 : 2 * POINT_ROWS, :] = rest[points + 3 : 2 * POINT_ROWS, :]
            sums = jnp.sum(grad_qkv[...].astype(jnp.float32), axis=0, keepdims=True)
            bundle[points + 7 : points + 8, :third] = sums[:, :third]
            bundle[points + 7 : points + 8, third : 2 * third] = sums[:, 2 * third :]

        jobs = []
        for pair in range(third // PAIR):
            jobs += [[fine_job(pair, begin)] for begin in range(0, start, QUERY_BLOCK)]
            jobs[-1].append(coarse_job(pair))
        return jobs + [[partial_job], [weight_job], [norm_job], [base_job], [bundle_job]]

    move_pieces(
        pieces,
        1.0 / replicas,
        list(early) + [grad_w_qkv, grad_w_base, bundle],
        outs,
        acc,
        land,
        land_right,
        land_left,
        sems,
        prepare,
    )


def back_and_sync(
    qkv,
    grad_mixed,
    segment,
    normed_part,
    w_qkv,
    standard,
    inverse,
    grad_middle,
    gain,
    tokens,
    patches,
    fine_pairs,
    pos_fine,
    pos,
    rest,
    early,
    out_shapes,
    grads,
    outs,
    fine,
    start,
    replicas,
):
    rows, width = standard.shape
    channels = patches.shape[0]
    pieces = sync_plan(grads, outs)
    count = len(pieces)
    high = max(p.rows for p in pieces)
    wide = max(p.cols for p in pieces)
    points = pos.shape[2]
    kernel = functools.partial(
        back_kernel, pieces, len(out_shapes), fine, start, points, (replicas, len(early))
    )
    f32 = lambda *dims: pltpu.VMEM(dims, jnp.float32)
    anywhere = pl.BlockSpec(memory_space=pl.ANY)
    results = pl.pallas_call(
        kernel,
        out_shape=[jax.ShapeDtypeStruct(s, jnp.float32) for s in out_shapes]
        + [jax.ShapeDtypeStruct((rows, width), jnp.float32)],
        in_specs=[VMEM] * 6
        + [anywhere, VMEM, anywhere]
        + [VMEM] * 7
        + [anywhere] * len(early),
        out_specs=[anywhere] * len(out_shapes) + [VMEM],
        scratch_shapes=[
            pltpu.VMEM(qkv.shape, jnp.bfloat16),
            f32(start, PAIR),
            f32(start, PAIR),
            f32(rows, width),
            f32(rows, width),
            f32(width // 2, qkv.shape[1]),
            f32(width // 2, channels * fine_pairs.shape[1] // 2),
            f32(2 * POINT_ROWS, width),
            f32(count, high // 2, wide),
            f32(count, high // 2, wide),
            f32(count, LINE - 1, high // 8, wide),
            f32(count, LINE - 1, high // 8, wide),
            pltpu.SemaphoreType.DMA((count, SEMS + 2)),
            pltpu.SemaphoreType.DMA((2,)),
            f32(2, LN_ROWS, width),
            f32(2, LN_ROWS, width),
            pltpu.SemaphoreType.DMA((2, 2)),
        ],
        compiler_params=pltpu.CompilerParams(
            collective_id=0, has_side_effects=True, vmem_limit_bytes=63 << 20
        ),
        name="back_and_sync",
    )(
        qkv,
        grad_mixed,
        segment[:, None],
        segment[None, start:],
        normed_part,
        w_qkv,
        standard,
        inverse,
        grad_middle,
        gain,
        tokens,
        patches,
        fine_pairs,
        pos_fine,
        pos,
        rest,
        *early,
    )
    return results[:-1], results[-1]


def tensor_sum(partial):
    return partial + lax.ppermute(partial, "tensor", [(0, 1), (1, 0)])


def from_partner(mine, core, replicas):
    there = [(i, i ^ 1) for i in range(replicas)]
    direct = lax.ppermute(mine, "dp", there)
    across = lax.ppermute(direct, "tensor", [(0, 1), (1, 0)])
    return direct, across


def merged_rows(fine_rows, light_rows, second, counts, start, stride, rows):
    width = fine_rows.shape[1]
    small = stride - stride % 4
    keep = jnp.arange(stride, dtype=jnp.int32)[:, None]
    fine = fine_rows.shape[0]
    padded = jnp.pad(light_rows, ((0, stride), (0, 0)))
    third = padded[:stride]
    fourth = lax.dynamic_slice_in_dim(padded, counts[2], stride, axis=0)
    blocks = [
        jnp.pad(fine_rows, ((0, start - fine), (0, 0))),
        jnp.pad(second, ((0, stride - second.shape[0]), (0, 0))),
        jnp.where(keep < counts[2], third, 0.0),
        jnp.where(keep < counts[3], fourth, 0.0),
        jnp.zeros((rows - start - 3 * stride, width), fine_rows.dtype),
    ]
    return jnp.concatenate(blocks, axis=0)


def own_rows(merged, is_fine, counts, fine, start, stride, rows):
    width = merged.shape[1]
    coarse = counts[1]
    heavy = jnp.concatenate(
        [
            merged[:fine],
            merged[start : start + stride],
            jnp.zeros((rows - fine - stride, width), merged.dtype),
        ],
        axis=0,
    )
    row = jnp.arange(rows, dtype=jnp.int32)[:, None]
    third = jnp.pad(merged[start + stride : start + 2 * stride], ((0, rows - stride), (0, 0)))
    fourth = jnp.pad(merged[start + 2 * stride : start + 3 * stride], ((stride, rows), (0, 0)))
    fourth = lax.dynamic_slice_in_dim(fourth, stride - counts[2], rows, axis=0)
    light = jnp.where(row < counts[2], third, fourth)
    used = jnp.where(is_fine, fine + coarse, counts[2] + counts[3])
    return jnp.where(row < used, jnp.where(is_fine, heavy, light), jnp.zeros_like(heavy))


def local(
    pixels,
    patch_size,
    counts,
    offsets,
    resize_table,
    pos_table,
    w_base,
    patch_bias,
    pos_base,
    gain_one,
    shift_one,
    w_query,
    bias_query,
    w_key,
    w_value,
    bias_value,
    w_out,
    bias_out,
    gain_two,
    shift_two,
    w_up,
    bias_up,
    w_down,
    bias_down,
    cotangent,
):
    wide = lambda value: value.astype(jnp.float32)
    images, channels, res, _ = pixels.shape
    rows_total = cotangent.shape[0]
    replicas = lax.axis_size("dp")
    core = lax.axis_index("tensor")
    side_x = lax.rem(lax.axis_index("dp"), 2)
    fine = (res // FINE) ** 2
    small = (res // COARSE[0]) ** 2
    start = up_to(fine, 16)
    stride = up_to(small, 8)
    rows = up_to(start + 3 * stride, 16)

    lane = jnp.arange(up_to(res, 128), dtype=jnp.int32)
    own_pix = jnp.pad(wide(pixels), ((0, 0), (0, 0), (0, 0), (0, -res % 128)))
    own_pix = jnp.where(lane == res, wide(patch_size)[:, None, None, None], own_pix)
    direct, across = from_partner(
        lax.dynamic_index_in_dim(own_pix, core, 0, keepdims=False), core, replicas
    )
    pix = jnp.concatenate([own_pix, direct[None], across[None]], axis=0)
    half_rows = rows_total // 2
    own_cotangent = wide(cotangent)
    cot_direct, cot_across = from_partner(
        lax.dynamic_slice_in_dim(own_cotangent, core * half_rows, half_rows, axis=0),
        core,
        replicas,
    )
    is_fine = patch_size[0] == FINE
    other = jnp.where(core == 0, jnp.array([2, 3], jnp.int32), jnp.array([3, 2], jnp.int32))
    order = jnp.where(
        is_fine,
        jnp.concatenate([jnp.array([0, 1], jnp.int32), other]),
        jnp.concatenate([other, jnp.array([0, 1], jnp.int32)]),
    )
    found = jnp.concatenate([patch_size, jnp.stack([direct[0, 0, res], across[0, 0, res]]).astype(jnp.int32)])
    sizes = jnp.take(found, order)
    counts4 = (res // sizes) ** 2
    table = jnp.take(resize_table, sizes, axis=0)
    pos_fine = pos_table[res // FINE, :fine]
    pos = jnp.take(pos_table[:, :small], res // sizes[1:], axis=0)

    row = jnp.arange(rows, dtype=jnp.int32)
    slot = jnp.where(row < start, 0, (row - start) // stride + 1)
    first = jnp.where(slot == 0, 0, start + (slot - 1) * stride)
    limit = jnp.where(
        slot == 0,
        counts4[0],
        jnp.where(slot == 1, counts4[1], jnp.where(slot == 2, counts4[2], counts4[3])),
    )
    valid = (slot < 4) & (row - first < limit)
    segment = jnp.where(valid, slot, 4)
    valid_rows = wide(valid)[:, None]

    embedded, tokens, patches, mixed_weight, fine_pairs = embed(
        sizes, order, pix, table, pos_fine, pos, w_base, patch_bias, pos_base, rows
    )
    w_qkv = jnp.concatenate([w_query, w_key, w_value], axis=1)
    bias_qkv = jnp.concatenate([bias_query, jnp.zeros_like(bias_query), bias_value])
    centered = embedded - jnp.mean(embedded, axis=-1, keepdims=True)
    inverse_one = lax.rsqrt(jnp.mean(centered * centered, axis=-1, keepdims=True) + 1e-06)
    standard_one = centered * inverse_one
    normed_one = (standard_one * wide(gain_one) + wide(shift_one)).astype(jnp.bfloat16)
    qkv = (
        jnp.dot(normed_one, w_qkv, preferred_element_type=jnp.float32) + wide(bias_qkv)
    ).astype(jnp.bfloat16)
    mixed = attend(qkv, segment, fine, start)
    attended = tensor_sum(jnp.dot(mixed, w_out, preferred_element_type=jnp.float32)) + wide(
        bias_out
    )
    middle = embedded + attended
    standard_two, standard_back_two = jax.vjp(standardize, middle)
    normed_two = (standard_two * wide(gain_two) + wide(shift_two)).astype(jnp.bfloat16)
    hidden = jnp.dot(normed_two, w_up, preferred_element_type=jnp.float32) + wide(bias_up)
    activated_wide, gelu_back = jax.vjp(jax.nn.gelu, hidden)
    activated = activated_wide.astype(jnp.bfloat16)
    branch = tensor_sum(jnp.dot(activated, w_down, preferred_element_type=jnp.float32)) + wide(
        bias_down
    )
    output = own_rows(
        (middle + branch).astype(jnp.bfloat16), is_fine, counts4, fine, start, stride, rows_total
    )
    other_cotangent = jnp.where(
        core == 0,
        jnp.concatenate([cot_direct, cot_across]),
        jnp.concatenate([cot_across, cot_direct]),
    )
    fine_cotangent = jnp.where(is_fine, own_cotangent, other_cotangent)
    light_cotangent = jnp.where(
        is_fine, other_cotangent[: 2 * stride], own_cotangent[: 2 * stride]
    )
    grad_out = (
        merged_rows(
            fine_cotangent[:fine],
            light_cotangent,
            fine_cotangent[fine : fine + small],
            counts4,
            start,
            stride,
            rows,
        )
        * valid_rows
    )
    grad_branch = grad_out.astype(jnp.bfloat16)
    own_part = lambda value: lax.dynamic_slice_in_dim(
        value, side_x * (value.shape[1] // 2), value.shape[1] // 2, axis=1
    )
    grad_w_down = jnp.einsum(
        "tf,td->fd", own_part(activated), grad_branch, preferred_element_type=jnp.float32
    )
    grad_activated = jnp.einsum(
        "td,fd->tf", grad_branch, w_down, preferred_element_type=jnp.float32
    )
    grad_hidden = gelu_back(grad_activated)[0].astype(jnp.bfloat16)
    grad_w_up = jnp.einsum(
        "td,tf->df", own_part(normed_two), grad_hidden, preferred_element_type=jnp.float32
    )
    grad_bias_up = jnp.sum(grad_hidden, axis=0, dtype=jnp.float32)
    grad_normed_two = tensor_sum(
        jnp.einsum("tf,df->td", grad_hidden, w_up, preferred_element_type=jnp.float32)
    )
    grad_middle = grad_out + standard_back_two(grad_normed_two * wide(gain_two))[0]
    grad_attended = grad_middle.astype(jnp.bfloat16)
    grad_w_out = jnp.einsum(
        "te,td->ed", own_part(mixed), grad_attended, preferred_element_type=jnp.float32
    )
    grad_mixed = jnp.einsum(
        "td,ed->te", grad_attended, w_out, preferred_element_type=jnp.float32
    ).astype(jnp.bfloat16)
    points = pos.shape[2]
    width = grad_attended.shape[1]
    bundle = jnp.concatenate(
        [
            jnp.zeros((points + 3, width), jnp.float32),
            jnp.sum(grad_attended, axis=0, dtype=jnp.float32)[None],
            jnp.sum(grad_normed_two * standard_two, axis=0)[None],
            jnp.sum(grad_normed_two, axis=0)[None],
            jnp.sum(grad_branch, axis=0, dtype=jnp.float32)[None],
            jnp.zeros((1, width), jnp.float32),
            grad_bias_up.reshape(-1, width),
        ],
        axis=0,
    )
    used = bundle.shape[0]
    bundle = jnp.pad(bundle, ((0, 2 * POINT_ROWS - used), (0, 0)))
    early = [grad_w_down, grad_w_up, grad_w_out]
    area = w_base.shape[1] // channels
    ff = w_down.shape[0]
    deep = w_up.shape[0]
    cut = bias_query.shape[0]
    out_shapes = [
        w_base.shape,
        w_down.shape,
        w_up.shape,
        w_query.shape,
        w_key.shape,
        w_value.shape,
        w_out.shape,
        bundle.shape,
    ]
    grads = [
        (ff // 2, width, 0),
        (deep // 2, ff, 0),
        (cut // 2, width, 0),
        (deep // 2, 3 * cut, 0),
        (width // 2, w_base.shape[1] // 2, 0),
        (POINT_ROWS, width, POINT_ROWS),
    ]
    outs = [
        [(1, width, ff // 2, 0, 0, 0)],
        [(2, ff, deep // 2, 0, 0, 0)],
        [(6, width, cut // 2, 0, 0, 0)],
        [(3 + k, cut, deep // 2, 0, 0, 0) for k in range(3)],
        [(0, area // 2, 0, width // 2, area // 2, area * c) for c in range(channels)],
        [(7, width, POINT_ROWS, 0, 0, 0)],
    ]
    synced, grad_embedded = back_and_sync(
        qkv,
        grad_mixed,
        segment,
        own_part(normed_one),
        w_qkv,
        standard_one,
        inverse_one,
        grad_middle,
        wide(gain_one)[None],
        tokens,
        patches,
        fine_pairs,
        pos_fine,
        pos,
        bundle,
        early,
        out_shapes,
        grads,
        outs,
        fine,
        start,
        replicas,
    )
    beyond = replicas // 16
    step = 1
    while step < beyond:
        swap = [(i, (i // 16 ^ step) * 16 + i % 16) for i in range(replicas)]
        synced = [part + lax.ppermute(part, "dp", swap) for part in synced]
        step *= 2
    pixel_grad = pixel_back(
        sizes,
        is_fine.astype(jnp.int32)[None],
        grad_embedded,
        table,
        w_base,
        mixed_weight,
        pixels.shape,
    )
    base_s, down_s, up_s, query_s, key_s, value_s, out_s, small_s = synced
    line = lambda k: small_s[points + k]
    return (
        output,
        pixel_grad,
        base_s,
        line(0),
        small_s[:points].T,
        line(1),
        line(2),
        query_s,
        line(7)[:cut],
        key_s,
        value_s,
        line(7)[cut:],
        out_s,
        line(3),
        line(4),
        line(5),
        up_s,
        small_s[points + 8 : used].reshape(-1),
        down_s,
        line(6),
    )


def solution(mesh):
    in_specs = (
        P("dp", None, None, None),
        P("dp"),
        P("dp"),
        P("dp"),
        P(),
        P(),
        P(),
        P(),
        P(),
        P(),
        P(),
        P(None, "tensor"),
        P("tensor"),
        P(None, "tensor"),
        P(None, "tensor"),
        P("tensor"),
        P("tensor", None),
        P(),
        P(),
        P(),
        P(None, "tensor"),
        P("tensor"),
        P("tensor", None),
        P(),
        P("dp", None),
    )
    out_specs = (
        P("dp", None),
        P("dp", None, None, None),
        P(),
        P(),
        P(),
        P(),
        P(),
        P(None, "tensor"),
        P("tensor"),
        P(None, "tensor"),
        P(None, "tensor"),
        P("tensor"),
        P("tensor", None),
        P(),
        P(),
        P(),
        P(None, "tensor"),
        P("tensor"),
        P("tensor", None),
        P(),
    )
    return jax.shard_map(local, mesh=mesh, in_specs=in_specs, out_specs=out_specs, check_vma=False)
```

```python
import functools
import math

import jax
import jax.numpy as jnp
from jax import lax
from jax.experimental import pallas as pl
from jax.experimental.pallas import tpu as pltpu
from jax.sharding import PartitionSpec as P

HD = 64
VMEM = pl.BlockSpec(memory_space=pltpu.VMEM)
SMEM = pl.BlockSpec(memory_space=pltpu.SMEM)


def standardize(values):
    centered = values - jnp.mean(values, axis=-1, keepdims=True)
    spread = jnp.mean(centered * centered, axis=-1, keepdims=True)
    return centered * lax.rsqrt(spread + 1e-06)


FINE = 8
COARSE = (24, 30, 40, 48)


def nt(left, right):
    return lax.dot_general(left, right, (((1,), (1,)), ((), ())), preferred_element_type=jnp.float32)


def tn(left, right):
    return lax.dot_general(left, right, (((0,), (0,)), ((), ())), preferred_element_type=jnp.float32)


def nn(left, right):
    return jnp.dot(left, right, preferred_element_type=jnp.float32)


def up_to(value, step):
    return value + -value % step


def loop(count, body, unroll):
    if unroll:
        for i in range(count):
            body(i)
    else:
        pl.loop(0, count)(body)


def aligned(start, side):
    return pl.multiple_of(start, 8) if side % 8 == 0 and not isinstance(start, int) else start


def fill_pairs(pair, long, table, side):
    base = table.shape[1]
    entry = lax.broadcasted_iota(jnp.int32, (base, base * base), 0)
    place = lax.broadcasted_iota(jnp.int32, (base, base * base), 1)
    repeat = (place // base == entry).astype(jnp.bfloat16)
    tile = (place % base == entry).astype(jnp.bfloat16)
    wide = nn(table, repeat)[:side]
    long[...] = nn(table, tile)

    def one(s):
        pair[pl.ds(aligned(s * side, side), side), :] = wide * long[pl.ds(s, 1), :]

    loop(side, one, True)


def cut_patches(line, pix, image, channel, side, grid, res):
    def one(x):
        block = pix[image, channel, pl.ds(aligned(x * side, side), side), :]
        line[pl.ds(aligned(x * res, 8), res), :side] = block.T[:res]

    loop(grid, one, True)
    return jnp.concatenate(
        [line[pl.ds(s, grid * grid, stride=side), :side] for s in range(side)], axis=1
    ).astype(jnp.bfloat16)


def place_patches(line, pixel_grad, image, channel, patch, side, grid, res):
    for s in range(side):
        line[pl.ds(s, grid * grid, stride=side), :side] = patch[:, s * side : (s + 1) * side]

    def one(x):
        block = line[pl.ds(aligned(x * res, 8), res), :side]
        pixel_grad[image, channel, pl.ds(aligned(x * side, side), side), :] = block.T

    loop(grid, one, True)


def embed_kernel(
    sizes,
    order,
    pix,
    table,
    pos_fine,
    pos,
    weight,
    bias,
    pos_base,
    emb,
    tokens,
    patches,
    mixed_weight,
    fine_pairs,
    line,
    pair,
    long,
):
    area = table.shape[2] ** 2
    channels, res = pix.shape[1:3]
    grid = res // FINE
    count = grid * grid
    start = up_to(count, 16)
    stride = tokens.shape[1]
    low = jnp.bfloat16
    emb[...] = jnp.broadcast_to(bias[...], emb.shape)
    tokens[...] = jnp.zeros_like(tokens)

    fill_pairs(pair, long, table[0], FINE)
    fine_pairs[...] = pair[: FINE * FINE, :].astype(low)
    emb[:count, :] += nt(pos_fine[...], pos_base[...])

    @functools.partial(loop, channels, unroll=True)
    def _(c):
        columns = pl.ds(c * area, area)
        patch = cut_patches(line, pix, order[0], c, FINE, grid, res)
        mixed = nt(fine_pairs[...], weight[:, columns]).astype(low)
        mixed_weight[c] = mixed
        patches[c, :count, :] = patch
        emb[:count, :] += nn(patch, mixed)

    @pl.loop(1, 4)
    def _(slot):
        row = pl.multiple_of(start + (slot - 1) * stride, 8)
        for side in COARSE:
            grid = res // side
            count = grid * grid

            @pl.when(sizes[slot] == side)
            def _():
                fill_pairs(pair, long, table[slot], side)
                here = pl.ds(row, count)
                emb[here, :] += nt(pos[slot - 1, :count, :], pos_base[...])

                @functools.partial(loop, channels, unroll=True)
                def _(c):
                    columns = pl.ds(c * area, area)
                    patch = cut_patches(line, pix, order[slot], c, side, grid, res)
                    token = nn(patch, pair[: side * side, :].astype(low)).astype(low)
                    tokens[slot - 1, :count, columns] = token
                    emb[here, :] += nt(token, weight[:, columns])


def embed(sizes, order, pix, table, pos_fine, pos, w_base, patch_bias, pos_base, rows):
    _, channels, res, _ = pix.shape
    width, features = w_base.shape
    fine = (res // FINE) ** 2
    side = table.shape[1]
    area = features // channels
    return pl.pallas_call(
        embed_kernel,
        out_shape=[
            jax.ShapeDtypeStruct((rows, width), jnp.float32),
            jax.ShapeDtypeStruct((3, up_to(pos.shape[1], 8), features), jnp.bfloat16),
            jax.ShapeDtypeStruct((channels, up_to(fine, 16), FINE * FINE), jnp.bfloat16),
            jax.ShapeDtypeStruct((channels, FINE * FINE, width), jnp.bfloat16),
            jax.ShapeDtypeStruct((FINE * FINE, area), jnp.bfloat16),
        ],
        in_specs=[SMEM] * 2 + [VMEM] * 7,
        out_specs=[VMEM] * 5,
        scratch_shapes=[
            pltpu.VMEM((res * res // FINE, 128), jnp.float32),
            pltpu.VMEM((side * side, area), jnp.float32),
            pltpu.VMEM((side, area), jnp.float32),
        ],
        compiler_params=pltpu.CompilerParams(vmem_limit_bytes=48 << 20),
        name="embed",
    )(
        sizes,
        order,
        pix,
        table,
        pos_fine,
        pos,
        w_base,
        patch_bias.astype(jnp.float32)[None],
        pos_base,
    )


def pixel_kernel(sizes, is_fine, grad, table, weight, mixed_weight, pixel_grad, line, pair, long):
    area = table.shape[2] ** 2
    channels, res = pixel_grad.shape[1:3]
    start = up_to((res // FINE) ** 2, 16)
    stride = up_to((res // COARSE[0]) ** 2, 8)
    low = jnp.bfloat16

    @pl.when(is_fine[0] == 1)
    def _():
        grid = res // FINE
        count = grid * grid
        for c in range(channels):
            patch = nt(grad[:count, :].astype(low), mixed_weight[c])
            place_patches(line, pixel_grad, 0, c, patch, FINE, grid, res)

    @pl.loop(1, 4)
    def _(slot):
        row = pl.multiple_of(start + (slot - 1) * stride, 8)
        wanted = jnp.where(slot == 1, is_fine[0], 1 - is_fine[0])
        image = jnp.where(slot == 1, 1, slot - 2)
        for side in COARSE:
            grid = res // side
            count = grid * grid

            @pl.when((sizes[slot] == side) & (wanted == 1))
            def _():
                fill_pairs(pair, long, table[slot], side)
                rows = grad[pl.ds(row, count), :].astype(low)

                @pl.loop(0, channels)
                def _(c):
                    columns = pl.ds(pl.multiple_of(c * area, area), area)
                    token = nn(rows, weight[:, columns]).astype(low)
                    patch = nt(token, pair[: side * side, :].astype(low))
                    place_patches(line, pixel_grad, image, c, patch, side, grid, res)


def pixel_back(sizes, is_fine, grad, table, w_base, mixed_weight, shape):
    _, channels, res, _ = shape
    width, features = w_base.shape
    side = table.shape[1]
    return pl.pallas_call(
        pixel_kernel,
        out_shape=jax.ShapeDtypeStruct(shape, jnp.float32),
        in_specs=[SMEM] * 2 + [VMEM] * 4,
        out_specs=VMEM,
        scratch_shapes=[
            pltpu.VMEM((res * res // FINE, 128), jnp.float32),
            pltpu.VMEM((side * side, features // channels), jnp.float32),
            pltpu.VMEM((side, features // channels), jnp.float32),
        ],
        compiler_params=pltpu.CompilerParams(vmem_limit_bytes=40 << 20),
        name="pixel_back",
    )(sizes, is_fine, grad, table, w_base, mixed_weight)


PAIR = 2 * HD


def pair_halves(rows):
    lane = lax.broadcasted_iota(jnp.int32, (rows, PAIR), 1)
    return [lane < HD, lane >= HD]


def attend_block(scale, query, key, value, mask):
    halves = pair_halves(query.shape[0])
    both = []
    for h in range(2):
        own = jnp.where(halves[h], query, jnp.zeros_like(query))
        scores = jnp.where(mask, nt(own, key) * scale, -1000000000.0)
        weights = jnp.exp(scores - jnp.max(scores, axis=1, keepdims=True))
        inverse = 1.0 / jnp.sum(weights, axis=1, keepdims=True)
        both.append(nn((weights * inverse).astype(jnp.bfloat16), value))
    return jnp.where(halves[0], both[0], both[1]).astype(jnp.bfloat16)


def block_masks(fine, start, rows, segment, segment_row, axis):
    inside = lax.broadcasted_iota(jnp.int32, (start, start), axis) < fine
    same = segment[start:rows, :] == segment_row[:, : rows - start]
    return inside, same


def attend_kernel(scale, fine, start, query, key, value, segment, segment_row, mixed):
    rows = query.shape[0]
    masks = block_masks(fine, start, rows, segment, segment_row, 1)
    for here, mask in zip((slice(0, start), slice(start, rows)), masks):
        mixed[here, :] = attend_block(scale, query[here, :], key[here, :], value[here, :], mask)


def attend(qkv, segment, fine, start):
    rows, width = qkv.shape
    heads = width // 3 // PAIR
    kernel = functools.partial(attend_kernel, 1.0 / math.sqrt(HD), fine, start)
    column = lambda k: pl.BlockSpec((rows, PAIR), lambda j: (0, k * heads + j))
    return pl.pallas_call(
        kernel,
        grid=(heads,),
        out_shape=jax.ShapeDtypeStruct((rows, width // 3), jnp.bfloat16),
        in_specs=[
            column(0),
            column(1),
            column(2),
            pl.BlockSpec((rows, 1), lambda j: (0, 0)),
            pl.BlockSpec((1, rows - start), lambda j: (0, 0)),
        ],
        out_specs=column(0),
        compiler_params=pltpu.CompilerParams(vmem_limit_bytes=48 << 20),
        name="attend",
    )(qkv, qkv, qkv, segment[:, None], segment[None, start:])


def attend_back_block(scale, query, key, value, grad_mixed, mask):
    halves = pair_halves(query.shape[0])
    grad_query, grad_key, grad_value = [], 0.0, 0.0
    for h in range(2):
        own = jnp.where(halves[h], query, jnp.zeros_like(query))
        grad = jnp.where(halves[h], grad_mixed, jnp.zeros_like(grad_mixed))
        scores = jnp.where(mask, nt(key, own) * scale, -1000000000.0)
        weights = jnp.exp(scores - jnp.max(scores, axis=0, keepdims=True))
        probs = weights * (1.0 / jnp.sum(weights, axis=0, keepdims=True))
        grad_probs = nt(value, grad)
        inner = jnp.sum(probs * grad_probs, axis=0, keepdims=True)
        grad_scores = (probs * (grad_probs - inner)).astype(jnp.bfloat16)
        grad_value = grad_value + nn(probs.astype(jnp.bfloat16), grad)
        grad_key = grad_key + nn(grad_scores, own)
        grad_query.append(tn(grad_scores, key))
    grad_query = jnp.where(halves[0], grad_query[0], grad_query[1])
    return grad_query * scale, grad_key * scale, grad_value


LINE = 4
MESH_ID = pl.DeviceIdType.MESH
PIECE_ROWS = 192
PIECE_COLS = 384
CROSS_EVERY = 3
SEMS = 48


class Piece:
    def __init__(self, source, row, col, rows, cols, target, out_row, out_col, swap, cross):
        self.source, self.row, self.col, self.rows, self.cols = source, row, col, rows, cols
        self.target, self.out_row, self.out_col = target, out_row, out_col
        self.swap, self.cross = swap, cross


def move_pieces(pieces, scale, grads, outs, acc, land, land_right, land_left, sems, prepare):
    device = lax.axis_index("dp")
    core = lax.axis_index("tensor")
    place_x = lax.rem(device, 2)
    place_y = lax.rem(device // 2, 2)
    place_z = lax.rem(device // 4, LINE)
    mirror = LINE - 1 - place_z
    beside_x = (device + 1 - 2 * place_x, core)
    beside_y = (device + 2 - 4 * place_y, core)
    sibling = (device, 1 - core)
    up = (device + 4, core)
    down = (device - 4, core)

    barrier = pltpu.get_barrier_semaphore()
    for partner in (beside_x, beside_y, sibling):
        pl.semaphore_signal(barrier, inc=1, device_id=partner, device_id_type=MESH_ID)

    @pl.when(place_z < LINE - 1)
    def _():
        pl.semaphore_signal(barrier, inc=1, device_id=up, device_id_type=MESH_ID)

    @pl.when(place_z > 0)
    def _():
        pl.semaphore_signal(barrier, inc=1, device_id=down, device_id_type=MESH_ID)

    inner = (place_z + LINE - 1) // LINE + (2 * (LINE - 1) - place_z) // LINE
    pl.semaphore_wait(barrier, 3 + inner)

    def remote(src, dst, send, recv, where):
        return pltpu.make_async_remote_copy(
            src_ref=src,
            dst_ref=dst,
            send_sem=send,
            recv_sem=recv,
            device_id=where,
            device_id_type=MESH_ID,
        )

    work = prepare(core, place_x, sibling, remote)

    def rows_at(ref, start, size, column, width):
        return ref.at[pl.ds(pl.multiple_of(start, 8), size), pl.ds(pl.multiple_of(column, 128), width)]

    def add_rows(total, start, extra, size, width, factor=None):
        step = 24 if size % 24 == 0 else 8

        @pl.loop(0, size // step)
        def _(i):
            here = pl.ds(pl.multiple_of(start + i * step, 8), step)
            there = pl.ds(pl.multiple_of(i * step, 8), step)
            value = total[here, :width] + extra[there, :width]
            total[here, :width] = value if factor is None else value * factor

    def build(number, piece):
        half, chunk, width = piece.rows // 2, piece.rows // 8, piece.cols
        grad, out = grads[piece.source], outs[piece.target]
        mine = acc.at[number]
        sem = lambda k: sems.at[number, k]

        def out_at(x, owner, row, size):
            return rows_at(out, piece.out_row(x, owner) + row, size, piece.out_col(x), width)

        def y_copy():
            return remote(
                rows_at(grad, piece.row(place_x) + (1 - place_y) * half, half, piece.col, width),
                land.at[number, :half, :width],
                sem(0),
                sem(1),
                beside_y,
            )

        def load():
            return pltpu.make_async_copy(
                rows_at(grad, piece.row(place_x) + place_y * half, half, piece.col, width),
                mine.at[:half, :width],
                sem(2),
            )

        def right(k):
            return remote(
                rows_at(mine, (LINE - k + place_z) * chunk, chunk, 0, width),
                land_right.at[number, k - 1, :chunk, :width],
                sem(2 + k),
                sem(5 + k),
                up,
            )

        def left(k):
            return remote(
                rows_at(mine, (k - 1 - mirror) * chunk, chunk, 0, width),
                land_left.at[number, k - 1, :chunk, :width],
                sem(8 + k),
                sem(11 + k),
                down,
            )

        def got(slots, k, first, where):
            here = slots.at[number, k - 1, :chunk, :width]
            return remote(here, here, sem(first + k), sem(first + 3 + k), where)

        def send_line(k):
            @pl.when((place_z <= k - 1) & (place_z < LINE - 1))
            def _():
                right(k).start()

            @pl.when((mirror <= k - 1) & (mirror < LINE - 1))
            def _():
                left(k).start()

        def wait_line(k):
            @pl.when((place_z >= 1) & (place_z <= k))
            def _():
                got(land_right, k, 2, down).wait_recv()
                add_rows(
                    mine, (LINE - 1 - k + place_z) * chunk, land_right.at[number, k - 1], chunk, width
                )

            @pl.when((mirror >= 1) & (mirror <= k))
            def _():
                got(land_left, k, 8, up).wait_recv()
                add_rows(mine, (k - mirror) * chunk, land_left.at[number, k - 1], chunk, width)

        def own_chunk():
            return rows_at(mine, place_z * chunk, chunk, 0, width)

        def store():
            return pltpu.make_async_copy(
                own_chunk(), out_at(place_x, core, place_y * half + place_z * chunk, chunk), sem(17)
            )

        def share_out():
            return remote(
                own_chunk(),
                out_at(place_x, core, place_y * half + place_z * chunk, chunk),
                sem(15),
                sem(16),
                beside_x if piece.cross else beside_y,
            )

        def share_in():
            if piece.cross:
                there = out_at(1 - place_x, core, place_y * half + place_z * chunk, chunk)
                return remote(there, there, sem(15), sem(16), beside_x)
            there = out_at(place_x, core, (1 - place_y) * half + place_z * chunk, chunk)
            return remote(there, there, sem(15), sem(16), beside_y)

        def spread(k, position, where, first):
            copies = []
            for b in range(2):
                if piece.cross:
                    here = out_at(b, core, place_y * half + position * chunk, chunk)
                else:
                    here = out_at(place_x, core, b * half + position * chunk, chunk)
                at = first + 2 * (k - 1) + b
                copies.append(remote(here, here, sem(at), sem(at + 6), where))
            return copies

        def send_spread(k):
            @pl.when((place_z >= k - 1) & (place_z < LINE - 1))
            def _():
                for copy in spread(k, place_z - (k - 1), up, 18):
                    copy.start()

            @pl.when((mirror >= k - 1) & (mirror < LINE - 1))
            def _():
                for copy in spread(k, place_z + (k - 1), down, 30):
                    copy.start()

        def wait_spread(k):
            @pl.when(place_z >= k)
            def _():
                for copy in spread(k, place_z - k, down, 18):
                    copy.wait_recv()

            @pl.when(mirror >= k)
            def _():
                for copy in spread(k, place_z + k, up, 30):
                    copy.wait_recv()

        def last(outgoing):
            if piece.cross:
                row = (place_y if outgoing else 1 - place_y) * half
                views = [out_at(b, core, row, half) for b in range(2)]
                return [
                    remote(v, v, sem(42 + b), sem(44 + b), beside_y) for b, v in enumerate(views)
                ]
            view = out_at(place_x if outgoing else 1 - place_x, core, 0, piece.rows)
            return [remote(view, view, sem(42), sem(44), beside_x)]

        def swap(owner):
            views = [out_at(b, owner, 0, piece.rows) for b in range(2)]
            return [remote(v, v, sem(46 + b), sem(48 + b), sibling) for b, v in enumerate(views)]

        def stage_0():
            y_copy().start()
            load().start()

        def stage_1():
            load().wait()
            y_copy().wait_recv()
            add_rows(mine, 0, land.at[number], half, width)
            send_line(1)

        def stage_2():
            wait_line(1)
            send_line(2)

        def stage_3():
            wait_line(2)
            send_line(3)

        def stage_4():
            wait_line(3)

            @pl.loop(0, chunk // 8)
            def _(i):
                here = pl.ds(pl.multiple_of(place_z * chunk + i * 8, 8), 8)
                mine[here, :width] = mine[here, :width] * scale

            share_out().start()
            store().start()

        def stage_5():
            store().wait()
            share_in().wait_recv()
            send_spread(1)

        def stage_6():
            wait_spread(1)
            send_spread(2)

        def stage_7():
            wait_spread(2)
            send_spread(3)

        def stage_8():
            wait_spread(3)
            for copy in last(True):
                copy.start()

        def stage_9():
            for copy in last(False):
                copy.wait_recv()
            if piece.swap:
                for copy in swap(core):
                    copy.start()

        def stage_10():
            if piece.swap:
                for copy in swap(1 - core):
                    copy.wait_recv()
                for copy in swap(core):
                    copy.wait_send()
            y_copy().wait_send()
            share_out().wait_send()
            for copy in last(True):
                copy.wait_send()
            for k in range(1, LINE):

                @pl.when((place_z <= k - 1) & (place_z < LINE - 1))
                def _():
                    right(k).wait_send()

                @pl.when((mirror <= k - 1) & (mirror < LINE - 1))
                def _():
                    left(k).wait_send()

                @pl.when((place_z >= k - 1) & (place_z < LINE - 1))
                def _():
                    for copy in spread(k, place_z - (k - 1), up, 18):
                        copy.wait_send()

                @pl.when((mirror >= k - 1) & (mirror < LINE - 1))
                def _():
                    for copy in spread(k, place_z + (k - 1), down, 30):
                        copy.wait_send()

        return [
            stage_0,
            stage_1,
            stage_2,
            stage_3,
            stage_4,
            stage_5,
            stage_6,
            stage_7,
            stage_8,
            stage_9,
            stage_10,
        ]

    lines = [build(number, piece) for number, piece in enumerate(pieces)]
    groups = [lines[i : i + GROUP] for i in range(0, len(lines), GROUP)]
    depth = len(lines[0])
    for j in range(min(AHEAD, len(groups))):
        for line in groups[j]:
            line[0]()
    late = depth - 2
    for tick in range(len(groups) + depth - 1):
        if tick + AHEAD < len(groups):
            for line in groups[tick + AHEAD]:
                line[0]()
        for job in work.pop(0) if work else ():
            job()
        active = range(max(0, tick - depth + 1), min(tick, len(groups)))
        for j in [j for j in active if tick - j < late] + [j for j in active if tick - j >= late]:
            for line in groups[j]:
                line[tick - j]()


GROUP = 1
AHEAD = 1


def sync_plan(grads, outs):
    pieces = []
    for source, (rows, cols, step_x) in enumerate(grads):
        start = 0
        for target, width, row_x, row_core, col_x, out_start in outs[source]:
            tall = min(PIECE_ROWS, rows)
            wide = min(PIECE_COLS, width)
            if width % wide:
                wide = width // 2
            for row in range(0, rows, tall):
                for col in range(0, width, wide):
                    pieces.append(
                        Piece(
                            source,
                            lambda x, row=row, a=step_x: row + x * a,
                            start + col,
                            tall,
                            wide,
                            target,
                            lambda x, core, row=row, a=row_x, b=row_core: row + x * a + core * b,
                            lambda x, c=out_start + col, a=col_x: c + x * a,
                            row_core != 0,
                            len(pieces) % CROSS_EVERY == CROSS_EVERY - 1,
                        )
                    )
            start += width
    return pieces


QUERY_BLOCK = 384
CHUNK = 112
POINT_ROWS = 64


def gelu_slope(value):
    root = math.sqrt(2.0 / math.pi)
    square = value * value
    bend = jnp.tanh(root * value * (1.0 + 0.044715 * square))
    return 0.5 * (1.0 + bend) + (0.5 * root) * value * (1.0 - bend * bend) * (
        1.0 + (3 * 0.044715) * square
    )


def back_kernel(pieces, sizes, fine, start, points, replicas, *refs):
    (
        qkv,
        segment,
        segment_row,
        normed_part,
        normed_two_part,
        mixed_part,
        w_qkv,
        w_out,
        w_up,
        w_down,
        bias_up,
        inverse,
        gain_one,
        gain_two,
        tokens,
        patches,
        fine_pairs,
        pos_fine,
        pos,
        rest,
        standard_one,
        standard_two,
        normed_two,
        grad_branch,
        grad_w_down,
    ) = refs[:25]
    refs = refs[25:]
    outs, grad_embedded, middle, refs = refs[:sizes], refs[sizes], refs[sizes + 1], refs[sizes + 2 :]
    (
        shared,
        grad_mixed,
        grad_key,
        grad_value,
        partial,
        arrived,
        grad_w_qkv,
        grad_w_base,
        grad_w_up,
        grad_w_out,
        bundle,
        acc,
        land,
        land_right,
        land_left,
        sems,
        swap_sems,
        free_sem,
        chunk_one,
        chunk_two,
        chunk_branch,
        chunk_low,
        chunk_sems,
        out_sem,
    ) = refs
    rows, width = standard_one.shape
    third = qkv.shape[1] // 3
    hidden_width = w_up.shape[1]
    scale = 1.0 / math.sqrt(HD)
    low = lambda value: value.astype(jnp.bfloat16)
    column_sum = lambda value: jnp.sum(value, axis=0, keepdims=True)
    count = rows // CHUNK

    def prepare(core, place_x, sibling, remote):
        def rows_of(ref, number):
            return ref.at[pl.ds(pl.multiple_of(number * CHUNK, 16), CHUNK)]

        def stream(ref, slots, kind, number):
            at = lax.rem(number, 2)
            return pltpu.make_async_copy(rows_of(ref, number), slots.at[at], chunk_sems.at[kind, at])

        def over_chunks(begin, end, streams, body):
            for ref, slots, kind in streams:
                stream(ref, slots, kind, begin).start()

            @pl.loop(begin, end)
            def _(number):
                @pl.when(number + 1 < end)
                def _():
                    for ref, slots, kind in streams:
                        stream(ref, slots, kind, number + 1).start()

                for ref, slots, kind in streams:
                    stream(ref, slots, kind, number).wait()
                body(number, lax.rem(number, 2))

        def swap(turn):
            return remote(
                partial, arrived, swap_sems.at[2 * turn], swap_sems.at[2 * turn + 1], sibling
            )

        def ffn_job(begin, end):
            def body(number, at):
                here = pl.ds(pl.multiple_of(number * CHUNK, 16), CHUNK)
                hidden = nn(chunk_low[at], w_up[...]) + bias_up[...]
                grad_hidden = low(nt(chunk_branch[at], w_down[...]) * gelu_slope(hidden))
                shared[here, :] = grad_hidden
                partial[here, :] = nt(grad_hidden, w_up[...])
                total = column_sum(grad_hidden.astype(jnp.float32))
                for k in range(hidden_width // width):
                    bundle[points + 8 + k : points + 9 + k, :] += total[
                        :, k * width : (k + 1) * width
                    ]

            def job():
                if begin == 0:
                    bundle[...] = rest[...]
                over_chunks(
                    begin, end, [(normed_two, chunk_low, 0), (grad_branch, chunk_branch, 1)], body
                )
                if end == count:
                    swap(0).start()

            return job

        def up_job():
            grad_w_up[...] = tn(normed_two_part[...], shared[...])

        def norm_rows(number, at, slots, gain, scale_column, row, before, after):
            @pl.loop(0, CHUNK // 16)
            def _(i):
                inner = pl.ds(pl.multiple_of(i * 16, 16), 16)
                here = pl.ds(pl.multiple_of(number * CHUNK + i * 16, 16), 16)
                grad = partial[here, :] + arrived[here, :]
                z = slots[at, inner, :]
                up = grad * gain[...]
                mean = jnp.mean(up, axis=1, keepdims=True)
                along = jnp.mean(up * z, axis=1, keepdims=True)
                back = (up - mean - z * along) * inverse[here, scale_column : scale_column + 1]
                value = before(inner) + back
                bundle[row : row + 1, :] += column_sum(grad * z)
                bundle[row + 1 : row + 2, :] += column_sum(grad)
                after(here, inner, value)

        def two_job(begin, end):
            def body(number, at):
                @pl.when(number >= 2)
                def _():
                    store_middle(number - 2).wait()

                def before(inner):
                    return chunk_branch[at, inner, :].astype(jnp.float32)

                def after(here, inner, value):
                    chunk_two[at, inner, :] = value
                    chunk_low[0, inner, :] = low(value)
                    bundle[points + 3 : points + 4, :] += column_sum(
                        low(value).astype(jnp.float32)
                    )

                norm_rows(number, at, chunk_one, gain_two, 1, points + 4, before, after)
                store_middle(number).start()
                here = pl.ds(pl.multiple_of(number * CHUNK, 16), CHUNK)
                grad_mixed[here, :] = low(nt(chunk_low[0], w_out[...]))
                grad_w_out[...] += tn(mixed_part[here, :], chunk_low[0])

            def job():
                if begin == 0:
                    swap(0).wait()
                    grad_w_out[...] = jnp.zeros_like(grad_w_out)
                over_chunks(
                    begin, end, [(standard_two, chunk_one, 0), (grad_branch, chunk_branch, 1)], body
                )
                if end == count:
                    store_middle(count - 2).wait()
                    store_middle(count - 1).wait()
                    pl.semaphore_signal(
                        free_sem, inc=1, device_id=sibling, device_id_type=MESH_ID
                    )

            return job

        def store_middle(number):
            at = lax.rem(number, 2)
            return pltpu.make_async_copy(
                chunk_two.at[at], rows_of(middle, number), chunk_sems.at[2, at]
            )

        def back_rows(pair, here, keys, mask):
            column = lambda k: slice(k * third + pair * PAIR, k * third + (pair + 1) * PAIR)
            return attend_back_block(
                scale,
                qkv[here, column(0)],
                qkv[keys, column(1)],
                qkv[keys, column(2)],
                grad_mixed[here, column(0)],
                mask,
            )

        def store_qkv(pair, k, here, value):
            shared[here, k * third + pair * PAIR : k * third + (pair + 1) * PAIR] = low(value)

        def fine_job(pair, begin):
            def job():
                here = slice(begin, min(begin + QUERY_BLOCK, start))
                keys = slice(0, start)
                inside = lax.broadcasted_iota(jnp.int32, (start, here.stop - begin), 0) < fine
                grad_q, grad_k, grad_v = back_rows(pair, here, keys, inside)
                store_qkv(pair, 0, here, grad_q)
                if begin == 0:
                    grad_key[...] = grad_k
                    grad_value[...] = grad_v
                else:
                    grad_key[...] += grad_k
                    grad_value[...] += grad_v
                if here.stop == start:
                    store_qkv(pair, 1, keys, grad_key[...])
                    store_qkv(pair, 2, keys, grad_value[...])

            return job

        def coarse_job(pair):
            def job():
                here = slice(start, rows)
                same = segment[here, :] == segment_row[...]
                for k, value in enumerate(back_rows(pair, here, here, same)):
                    store_qkv(pair, k, here, value)

            return job

        def weight_job():
            grad_w_qkv[...] = tn(normed_part[...], shared[:, : 3 * third])

        def partial_job():
            partial[...] = nt(shared[:, : 3 * third], w_qkv[...])
            pl.semaphore_wait(free_sem, 1)
            swap(1).start()

        def one_job():
            def body(number, at):
                def before(inner):
                    return chunk_two[at, inner, :]

                def after(here, inner, value):
                    partial[here, :] = value
                    bundle[points : points + 1, :] += column_sum(low(value).astype(jnp.float32))

                norm_rows(number, at, chunk_one, gain_one, 0, points + 1, before, after)

            swap(1).wait()
            over_chunks(0, count, [(standard_one, chunk_one, 0), (middle, chunk_two, 2)], body)
            pltpu.make_async_copy(partial, grad_embedded, out_sem).start()

        def base_job():
            half = grad_w_base.shape[0]
            channels = patches.shape[0]
            part = grad_w_base.shape[1] // channels
            area = 2 * part
            columns = pl.ds(pl.multiple_of(core * half, 128), half)
            stride = tokens.shape[1]
            some = low(partial[:fine, columns])
            wanted = fine_pairs[:, pl.ds(pl.multiple_of(place_x * part, 128), part)]
            for c in range(channels):
                gathered = low(tn(patches[c, :fine, :], some))
                total = tn(gathered, wanted)
                for k in range(3):
                    begin = start + k * stride
                    here = pl.ds(pl.multiple_of(c * area + place_x * part, 128), part)
                    total += tn(low(partial[begin : begin + stride, columns]), tokens[k, :, here])
                grad_w_base[:, c * part : (c + 1) * part] = total

        def bundle_job():
            gathered = tn(pos_fine[...], low(partial[:fine, :]))
            for k in range(3):
                begin = start + k * tokens.shape[1]
                gathered += tn(pos[k], low(partial[begin : begin + pos.shape[1], :]))
            bundle[:points, :] = gathered
            sums = column_sum(shared[:, : 3 * third].astype(jnp.float32))
            bundle[points + 7 : points + 8, :third] = sums[:, :third]
            bundle[points + 7 : points + 8, third : 2 * third] = sums[:, 2 * third :]
            pltpu.make_async_copy(partial, grad_embedded, out_sem).wait()

        cuts = [count * k // 4 for k in range(5)]
        jobs = [[ffn_job(a, b)] for a, b in zip(cuts[:-1], cuts[1:])]
        jobs += [[up_job], [two_job(0, count)]]
        for pair in range(third // PAIR):
            jobs += [[fine_job(pair, begin)] for begin in range(0, start, QUERY_BLOCK)]
            jobs[-1].append(coarse_job(pair))
        return jobs + [[weight_job], [partial_job], [one_job], [base_job], [bundle_job]]

    move_pieces(
        pieces,
        1.0 / replicas,
        [grad_w_down, grad_w_up, grad_w_out, grad_w_qkv, grad_w_base, bundle],
        outs,
        acc,
        land,
        land_right,
        land_left,
        sems,
        prepare,
    )


def back_and_sync(inside, anywhere, segment, out_shapes, grads, outs, fine, start, replicas):
    qkv = inside[0]
    rows, width = anywhere[0].shape
    w_qkv, w_out, w_up = inside[4:7]
    patches, fine_pairs, pos_fine, pos = inside[13:17]
    channels = patches.shape[0]
    pieces = sync_plan(grads, outs)
    count = len(pieces)
    high = max(p.rows for p in pieces)
    wide = max(p.cols for p in pieces)
    kernel = functools.partial(
        back_kernel, pieces, len(out_shapes), fine, start, pos.shape[2], replicas
    )
    f32 = lambda *dims: pltpu.VMEM(dims, jnp.float32)
    low = lambda *dims: pltpu.VMEM(dims, jnp.bfloat16)
    results = pl.pallas_call(
        kernel,
        out_shape=[jax.ShapeDtypeStruct(s, jnp.float32) for s in out_shapes]
        + [jax.ShapeDtypeStruct((rows, width), jnp.float32)] * 2,
        in_specs=[VMEM] * (len(inside) + 2) + [pl.BlockSpec(memory_space=pl.ANY)] * len(anywhere),
        out_specs=[pl.BlockSpec(memory_space=pl.ANY)] * (len(out_shapes) + 2),
        scratch_shapes=[
            low(rows, max(qkv.shape[1], w_up.shape[1])),
            low(rows, qkv.shape[1] // 3),
            f32(start, PAIR),
            f32(start, PAIR),
            f32(rows, width),
            f32(rows, width),
            f32(width // 2, qkv.shape[1]),
            f32(width // 2, channels * fine_pairs.shape[1] // 2),
            f32(width // 2, w_up.shape[1]),
            f32(w_out.shape[0] // 2, width),
            f32(2 * POINT_ROWS, width),
            f32(count, high // 2, wide),
            f32(count, high // 2, wide),
            f32(count, LINE - 1, high // 8, wide),
            f32(count, LINE - 1, high // 8, wide),
            pltpu.SemaphoreType.DMA((count, SEMS + 2)),
            pltpu.SemaphoreType.DMA((4,)),
            pltpu.SemaphoreType.REGULAR,
            f32(2, CHUNK, width),
            f32(2, CHUNK, width),
            low(2, CHUNK, width),
            low(2, CHUNK, width),
            pltpu.SemaphoreType.DMA((3, 2)),
            pltpu.SemaphoreType.DMA,
        ],
        compiler_params=pltpu.CompilerParams(
            collective_id=0, has_side_effects=True, vmem_limit_bytes=63 << 20
        ),
        name="back_and_sync",
    )(inside[0], segment[:, None], segment[None, start:], *inside[1:], *anywhere)
    return results[:-2], results[-2]


def tensor_sum(partial):
    return partial + lax.ppermute(partial, "tensor", [(0, 1), (1, 0)])


def from_partner(mine, core, replicas):
    there = [(i, i ^ 1) for i in range(replicas)]
    direct = lax.ppermute(mine, "dp", there)
    across = lax.ppermute(direct, "tensor", [(0, 1), (1, 0)])
    return direct, across


def merged_rows(fine_rows, light_rows, second, counts, start, stride, rows):
    width = fine_rows.shape[1]
    small = stride - stride % 4
    keep = jnp.arange(stride, dtype=jnp.int32)[:, None]
    fine = fine_rows.shape[0]
    padded = jnp.pad(light_rows, ((0, stride), (0, 0)))
    third = padded[:stride]
    fourth = lax.dynamic_slice_in_dim(padded, counts[2], stride, axis=0)
    blocks = [
        jnp.pad(fine_rows, ((0, start - fine), (0, 0))),
        jnp.pad(second, ((0, stride - second.shape[0]), (0, 0))),
        jnp.where(keep < counts[2], third, 0.0),
        jnp.where(keep < counts[3], fourth, 0.0),
        jnp.zeros((rows - start - 3 * stride, width), fine_rows.dtype),
    ]
    return jnp.concatenate(blocks, axis=0)


def own_rows(merged, is_fine, counts, fine, start, stride, rows):
    width = merged.shape[1]
    coarse = counts[1]
    heavy = jnp.concatenate(
        [
            merged[:fine],
            merged[start : start + stride],
            jnp.zeros((rows - fine - stride, width), merged.dtype),
        ],
        axis=0,
    )
    row = jnp.arange(rows, dtype=jnp.int32)[:, None]
    third = jnp.pad(merged[start + stride : start + 2 * stride], ((0, rows - stride), (0, 0)))
    fourth = jnp.pad(merged[start + 2 * stride : start + 3 * stride], ((stride, rows), (0, 0)))
    fourth = lax.dynamic_slice_in_dim(fourth, stride - counts[2], rows, axis=0)
    light = jnp.where(row < counts[2], third, fourth)
    used = jnp.where(is_fine, fine + coarse, counts[2] + counts[3])
    return jnp.where(row < used, jnp.where(is_fine, heavy, light), jnp.zeros_like(heavy))


def local(
    pixels,
    patch_size,
    counts,
    offsets,
    resize_table,
    pos_table,
    w_base,
    patch_bias,
    pos_base,
    gain_one,
    shift_one,
    w_query,
    bias_query,
    w_key,
    w_value,
    bias_value,
    w_out,
    bias_out,
    gain_two,
    shift_two,
    w_up,
    bias_up,
    w_down,
    bias_down,
    cotangent,
):
    wide = lambda value: value.astype(jnp.float32)
    images, channels, res, _ = pixels.shape
    rows_total = cotangent.shape[0]
    replicas = lax.axis_size("dp")
    core = lax.axis_index("tensor")
    side_x = lax.rem(lax.axis_index("dp"), 2)
    fine = (res // FINE) ** 2
    small = (res // COARSE[0]) ** 2
    start = up_to(fine, 16)
    stride = up_to(small, 8)
    rows = up_to(start + 3 * stride, 16)

    lane = jnp.arange(up_to(res, 128), dtype=jnp.int32)
    own_pix = jnp.pad(wide(pixels), ((0, 0), (0, 0), (0, 0), (0, -res % 128)))
    own_pix = jnp.where(lane == res, wide(patch_size)[:, None, None, None], own_pix)
    direct, across = from_partner(
        lax.dynamic_index_in_dim(own_pix, core, 0, keepdims=False), core, replicas
    )
    pix = jnp.concatenate([own_pix, direct[None], across[None]], axis=0)
    half_rows = rows_total // 2
    own_cotangent = wide(cotangent)
    cot_direct, cot_across = from_partner(
        lax.dynamic_slice_in_dim(own_cotangent, core * half_rows, half_rows, axis=0),
        core,
        replicas,
    )
    is_fine = patch_size[0] == FINE
    other = jnp.where(core == 0, jnp.array([2, 3], jnp.int32), jnp.array([3, 2], jnp.int32))
    order = jnp.where(
        is_fine,
        jnp.concatenate([jnp.array([0, 1], jnp.int32), other]),
        jnp.concatenate([other, jnp.array([0, 1], jnp.int32)]),
    )
    found = jnp.concatenate([patch_size, jnp.stack([direct[0, 0, res], across[0, 0, res]]).astype(jnp.int32)])
    sizes = jnp.take(found, order)
    counts4 = (res // sizes) ** 2
    table = jnp.take(resize_table, sizes, axis=0)
    pos_fine = pos_table[res // FINE, :fine]
    pos = jnp.take(pos_table[:, :small], res // sizes[1:], axis=0)

    row = jnp.arange(rows, dtype=jnp.int32)
    slot = jnp.where(row < start, 0, (row - start) // stride + 1)
    first = jnp.where(slot == 0, 0, start + (slot - 1) * stride)
    limit = jnp.where(
        slot == 0,
        counts4[0],
        jnp.where(slot == 1, counts4[1], jnp.where(slot == 2, counts4[2], counts4[3])),
    )
    valid = (slot < 4) & (row - first < limit)
    segment = jnp.where(valid, slot, 4)
    valid_rows = wide(valid)[:, None]

    embedded, tokens, patches, mixed_weight, fine_pairs = embed(
        sizes, order, pix, table, pos_fine, pos, w_base, patch_bias, pos_base, rows
    )
    w_qkv = jnp.concatenate([w_query, w_key, w_value], axis=1)
    bias_qkv = jnp.concatenate([bias_query, jnp.zeros_like(bias_query), bias_value])
    centered = embedded - jnp.mean(embedded, axis=-1, keepdims=True)
    inverse_one = lax.rsqrt(jnp.mean(centered * centered, axis=-1, keepdims=True) + 1e-06)
    standard_one = centered * inverse_one
    normed_one = (standard_one * wide(gain_one) + wide(shift_one)).astype(jnp.bfloat16)
    qkv = (
        jnp.dot(normed_one, w_qkv, preferred_element_type=jnp.float32) + wide(bias_qkv)
    ).astype(jnp.bfloat16)
    mixed = attend(qkv, segment, fine, start)
    attended = tensor_sum(jnp.dot(mixed, w_out, preferred_element_type=jnp.float32)) + wide(
        bias_out
    )
    middle = embedded + attended
    centered = middle - jnp.mean(middle, axis=-1, keepdims=True)
    inverse_two = lax.rsqrt(jnp.mean(centered * centered, axis=-1, keepdims=True) + 1e-06)
    standard_two = centered * inverse_two
    normed_two = (standard_two * wide(gain_two) + wide(shift_two)).astype(jnp.bfloat16)
    hidden = jnp.dot(normed_two, w_up, preferred_element_type=jnp.float32) + wide(bias_up)
    activated = jax.nn.gelu(hidden).astype(jnp.bfloat16)
    branch = tensor_sum(jnp.dot(activated, w_down, preferred_element_type=jnp.float32)) + wide(
        bias_down
    )
    output = own_rows(
        (middle + branch).astype(jnp.bfloat16), is_fine, counts4, fine, start, stride, rows_total
    )
    other_cotangent = jnp.where(
        core == 0,
        jnp.concatenate([cot_direct, cot_across]),
        jnp.concatenate([cot_across, cot_direct]),
    )
    fine_cotangent = jnp.where(is_fine, own_cotangent, other_cotangent)
    light_cotangent = jnp.where(
        is_fine, other_cotangent[: 2 * stride], own_cotangent[: 2 * stride]
    )
    grad_out = (
        merged_rows(
            fine_cotangent[:fine],
            light_cotangent,
            fine_cotangent[fine : fine + small],
            counts4,
            start,
            stride,
            rows,
        )
        * valid_rows
    )
    grad_branch = grad_out.astype(jnp.bfloat16)
    own_part = lambda value: lax.dynamic_slice_in_dim(
        value, side_x * (value.shape[1] // 2), value.shape[1] // 2, axis=1
    )
    grad_w_down = jnp.einsum(
        "tf,td->fd", own_part(activated), grad_branch, preferred_element_type=jnp.float32
    )
    points = pos.shape[2]
    width = grad_branch.shape[1]
    used = points + 8 + w_up.shape[1] // width
    bundle = jnp.concatenate(
        [
            jnp.zeros((points + 6, width), jnp.float32),
            jnp.sum(grad_branch, axis=0, dtype=jnp.float32)[None],
            jnp.zeros((2 * POINT_ROWS - points - 7, width), jnp.float32),
        ],
        axis=0,
    )
    area = w_base.shape[1] // channels
    ff = w_down.shape[0]
    deep = w_up.shape[0]
    cut = bias_query.shape[0]
    out_shapes = [
        w_base.shape,
        w_down.shape,
        w_up.shape,
        w_query.shape,
        w_key.shape,
        w_value.shape,
        w_out.shape,
        bundle.shape,
    ]
    grads = [
        (ff // 2, width, 0),
        (deep // 2, ff, 0),
        (cut // 2, width, 0),
        (deep // 2, 3 * cut, 0),
        (width // 2, w_base.shape[1] // 2, 0),
        (POINT_ROWS, width, POINT_ROWS),
    ]
    outs = [
        [(1, width, ff // 2, 0, 0, 0)],
        [(2, ff, deep // 2, 0, 0, 0)],
        [(6, width, cut // 2, 0, 0, 0)],
        [(3 + k, cut, deep // 2, 0, 0, 0) for k in range(3)],
        [(0, area // 2, 0, width // 2, area // 2, area * c) for c in range(channels)],
        [(7, width, POINT_ROWS, 0, 0, 0)],
    ]
    synced, grad_embedded = back_and_sync(
        [
            qkv,
            own_part(normed_one),
            own_part(normed_two),
            own_part(mixed),
            w_qkv,
            w_out,
            w_up,
            w_down,
            wide(bias_up)[None],
            jnp.concatenate([inverse_one, inverse_two], axis=1),
            wide(gain_one)[None],
            wide(gain_two)[None],
            tokens,
            patches,
            fine_pairs,
            pos_fine,
            pos,
            bundle,
        ],
        [standard_one, standard_two, normed_two, grad_branch, grad_w_down],
        segment,
        out_shapes,
        grads,
        outs,
        fine,
        start,
        replicas,
    )
    beyond = replicas // 16
    step = 1
    while step < beyond:
        swap = [(i, (i // 16 ^ step) * 16 + i % 16) for i in range(replicas)]
        synced = [part + lax.ppermute(part, "dp", swap) for part in synced]
        step *= 2
    pixel_grad = pixel_back(
        sizes,
        is_fine.astype(jnp.int32)[None],
        grad_embedded,
        table,
        w_base,
        mixed_weight,
        pixels.shape,
    )
    base_s, down_s, up_s, query_s, key_s, value_s, out_s, small_s = synced
    line = lambda k: small_s[points + k]
    return (
        output,
        pixel_grad,
        base_s,
        line(0),
        small_s[:points].T,
        line(1),
        line(2),
        query_s,
        line(7)[:cut],
        key_s,
        value_s,
        line(7)[cut:],
        out_s,
        line(3),
        line(4),
        line(5),
        up_s,
        small_s[points + 8 : used].reshape(-1),
        down_s,
        line(6),
    )


def solution(mesh):
    in_specs = (
        P("dp", None, None, None),
        P("dp"),
        P("dp"),
        P("dp"),
        P(),
        P(),
        P(),
        P(),
        P(),
        P(),
        P(),
        P(None, "tensor"),
        P("tensor"),
        P(None, "tensor"),
        P(None, "tensor"),
        P("tensor"),
        P("tensor", None),
        P(),
        P(),
        P(),
        P(None, "tensor"),
        P("tensor"),
        P("tensor", None),
        P(),
        P("dp", None),
    )
    out_specs = (
        P("dp", None),
        P("dp", None, None, None),
        P(),
        P(),
        P(),
        P(),
        P(),
        P(None, "tensor"),
        P("tensor"),
        P(None, "tensor"),
        P(None, "tensor"),
        P("tensor"),
        P("tensor", None),
        P(),
        P(),
        P(),
        P(None, "tensor"),
        P("tensor"),
        P("tensor", None),
        P(),
    )
    return jax.shard_map(local, mesh=mesh, in_specs=in_specs, out_specs=out_specs, check_vma=False)
```

```python
import functools
import math

import jax
import jax.numpy as jnp
from jax import lax
from jax.experimental import pallas as pl
from jax.experimental.pallas import tpu as pltpu
from jax.sharding import PartitionSpec as P

HD = 64
VMEM = pl.BlockSpec(memory_space=pltpu.VMEM)
SMEM = pl.BlockSpec(memory_space=pltpu.SMEM)


def standardize(values):
    centered = values - jnp.mean(values, axis=-1, keepdims=True)
    spread = jnp.mean(centered * centered, axis=-1, keepdims=True)
    return centered * lax.rsqrt(spread + 1e-06)


FINE = 8
COARSE = (24, 30, 40, 48)


def nt(left, right):
    return lax.dot_general(left, right, (((1,), (1,)), ((), ())), preferred_element_type=jnp.float32)


def tn(left, right):
    return lax.dot_general(left, right, (((0,), (0,)), ((), ())), preferred_element_type=jnp.float32)


def nn(left, right):
    return jnp.dot(left, right, preferred_element_type=jnp.float32)


def up_to(value, step):
    return value + -value % step


def loop(count, body, unroll):
    if unroll:
        for i in range(count):
            body(i)
    else:
        pl.loop(0, count)(body)


def aligned(start, side):
    return pl.multiple_of(start, 8) if side % 8 == 0 and not isinstance(start, int) else start


def fill_pairs(pair, long, table, side):
    base = table.shape[1]
    entry = lax.broadcasted_iota(jnp.int32, (base, base * base), 0)
    place = lax.broadcasted_iota(jnp.int32, (base, base * base), 1)
    repeat = (place // base == entry).astype(jnp.bfloat16)
    tile = (place % base == entry).astype(jnp.bfloat16)
    wide = nn(table, repeat)[:side]
    long[...] = nn(table, tile)

    def one(s):
        pair[pl.ds(aligned(s * side, side), side), :] = wide * long[pl.ds(s, 1), :]

    loop(side, one, True)


def cut_patches(line, pix, image, channel, side, grid, res):
    def one(x):
        block = pix[image, channel, pl.ds(aligned(x * side, side), side), :]
        line[pl.ds(aligned(x * res, 8), res), :side] = block.T[:res]

    loop(grid, one, True)
    return jnp.concatenate(
        [line[pl.ds(s, grid * grid, stride=side), :side] for s in range(side)], axis=1
    ).astype(jnp.bfloat16)


def place_patches(line, pixel_grad, image, channel, patch, side, grid, res):
    for s in range(side):
        line[pl.ds(s, grid * grid, stride=side), :side] = patch[:, s * side : (s + 1) * side]

    def one(x):
        block = line[pl.ds(aligned(x * res, 8), res), :side]
        pixel_grad[image, channel, pl.ds(aligned(x * side, side), side), :] = block.T

    loop(grid, one, True)


def embed_kernel(
    sizes,
    slots,
    table,
    pos_fine,
    pos_all,
    weight,
    bias,
    pos_base,
    gain,
    shift,
    own,
    direct,
    across,
    emb,
    standard,
    inverse,
    normed,
    tokens,
    patches,
    mixed_weight,
    fine_pairs,
    pos,
    segment,
    segment_row,
    pix,
    line,
    pair,
    long,
    sems,
):
    area = table.shape[2] ** 2
    channels, res = pix.shape[1:3]
    grid = res // FINE
    count = grid * grid
    start = up_to(count, 16)
    stride = tokens.shape[1]
    low = jnp.bfloat16
    copies = [
        pltpu.make_async_copy(source, pix.at[slots[k]], sems.at[k])
        for k, source in enumerate((own.at[0], own.at[1], direct, across))
    ]
    for copy in copies:
        copy.start()
    emb[...] = jnp.broadcast_to(bias[...], emb.shape)
    tokens[...] = jnp.zeros_like(tokens)
    fill_pairs(pair, long, table[FINE], FINE)
    fine_pairs[...] = pair[: FINE * FINE, :].astype(low)
    emb[:count, :] += nt(pos_fine[...], pos_base[...])
    for target, axis in ((segment, 0), (segment_row, 1)):
        row = lax.broadcasted_iota(jnp.int32, target.shape, axis)
        found = jnp.full(target.shape, 4, jnp.int32)
        for k in range(1, 4):
            side = res // sizes[k]
            within = row - (k - 1) * stride
            found = jnp.where((within >= 0) & (within < side * side), k, found)
        target[...] = found
    for copy in copies:
        copy.wait()

    for c in range(channels):
        columns = slice(c * area, (c + 1) * area)
        patch = cut_patches(line, pix, 0, c, FINE, grid, res)
        mixed = nt(fine_pairs[...], weight[:, columns]).astype(low)
        mixed_weight[c] = mixed
        patches[c, :count, :] = patch
        emb[:count, :] += nn(patch, mixed)

    @pl.loop(1, 4)
    def _(slot):
        row = pl.multiple_of(start + (slot - 1) * stride, 8)
        for side in COARSE:
            grid = res // side
            count = grid * grid

            @pl.when(sizes[slot] == side)
            def _():
                fill_pairs(pair, long, table[side], side)
                here = pl.ds(row, count)
                pos[slot - 1] = pos_all[grid]
                emb[here, :] += nt(pos_all[grid, :count, :], pos_base[...])
                for c in range(channels):
                    columns = slice(c * area, (c + 1) * area)
                    patch = cut_patches(line, pix, slot, c, side, grid, res)
                    token = nn(patch, pair[: side * side, :].astype(low)).astype(low)
                    tokens[slot - 1, :count, columns] = token
                    emb[here, :] += nt(token, weight[:, columns])

    @pl.loop(0, emb.shape[0] // 16)
    def _(i):
        here = pl.ds(pl.multiple_of(i * 16, 16), 16)
        value = emb[here, :]
        centered = value - jnp.mean(value, axis=1, keepdims=True)
        scale = lax.rsqrt(jnp.mean(centered * centered, axis=1, keepdims=True) + 1e-06)
        standard[here, :] = centered * scale
        inverse[here, :] = scale
        normed[here, :] = (centered * scale * gain[...] + shift[...]).astype(low)


def embed(sizes, slots, table, pos_fine, pos_all, w_base, rows_of, pos_base, pixels, rows):
    own = pixels[0]
    _, channels, res, lanes = own.shape
    width, features = w_base.shape
    fine = (res // FINE) ** 2
    side = table.shape[1]
    area = features // channels
    stride = pos_all.shape[1]
    rest = rows - up_to(fine, 16)
    shape = jax.ShapeDtypeStruct
    return pl.pallas_call(
        embed_kernel,
        out_shape=[
            shape((rows, width), jnp.float32),
            shape((rows, width), jnp.float32),
            shape((rows, 1), jnp.float32),
            shape((rows, width), jnp.bfloat16),
            shape((3, stride, features), jnp.bfloat16),
            shape((channels, up_to(fine, 16), FINE * FINE), jnp.bfloat16),
            shape((channels, FINE * FINE, width), jnp.bfloat16),
            shape((FINE * FINE, area), jnp.bfloat16),
            shape((3,) + pos_all.shape[1:], jnp.bfloat16),
            shape((rest, 1), jnp.int32),
            shape((1, rest), jnp.int32),
        ],
        in_specs=[SMEM] * 2 + [VMEM] * 8 + [pl.BlockSpec(memory_space=pl.ANY)] * 3,
        out_specs=[VMEM] * 11,
        scratch_shapes=[
            pltpu.VMEM((4, channels, res, lanes), jnp.float32),
            pltpu.VMEM((res * res // FINE, 128), jnp.float32),
            pltpu.VMEM((side * side, area), jnp.float32),
            pltpu.VMEM((side, area), jnp.float32),
            pltpu.SemaphoreType.DMA((4,)),
        ],
        compiler_params=pltpu.CompilerParams(vmem_limit_bytes=56 << 20),
        name="embed",
    )(sizes, slots, table, pos_fine, pos_all, w_base, rows_of[0], pos_base, *rows_of[1:], *pixels)


def pixel_kernel(sizes, is_fine, grad, table, weight, mixed_weight, pixel_grad, line, pair, long):
    area = table.shape[2] ** 2
    channels, res = pixel_grad.shape[1:3]
    start = up_to((res // FINE) ** 2, 16)
    stride = up_to((res // COARSE[0]) ** 2, 8)
    low = jnp.bfloat16

    @pl.when(is_fine[0] == 1)
    def _():
        grid = res // FINE
        count = grid * grid
        for c in range(channels):
            patch = nt(grad[:count, :].astype(low), mixed_weight[c])
            place_patches(line, pixel_grad, 0, c, patch, FINE, grid, res)

    @pl.loop(1, 4)
    def _(slot):
        row = pl.multiple_of(start + (slot - 1) * stride, 8)
        wanted = jnp.where(slot == 1, is_fine[0], 1 - is_fine[0])
        image = jnp.where(slot == 1, 1, slot - 2)
        for side in COARSE:
            grid = res // side
            count = grid * grid

            @pl.when((sizes[slot] == side) & (wanted == 1))
            def _():
                fill_pairs(pair, long, table[side], side)
                rows = grad[pl.ds(row, count), :].astype(low)

                @pl.loop(0, channels)
                def _(c):
                    columns = pl.ds(pl.multiple_of(c * area, area), area)
                    token = nn(rows, weight[:, columns]).astype(low)
                    patch = nt(token, pair[: side * side, :].astype(low))
                    place_patches(line, pixel_grad, image, c, patch, side, grid, res)


def pixel_back(sizes, is_fine, grad, table, w_base, mixed_weight, shape):
    _, channels, res, _ = shape
    width, features = w_base.shape
    side = table.shape[1]
    return pl.pallas_call(
        pixel_kernel,
        out_shape=jax.ShapeDtypeStruct(shape, jnp.float32),
        in_specs=[SMEM] * 2 + [VMEM] * 4,
        out_specs=VMEM,
        scratch_shapes=[
            pltpu.VMEM((res * res // FINE, 128), jnp.float32),
            pltpu.VMEM((side * side, features // channels), jnp.float32),
            pltpu.VMEM((side, features // channels), jnp.float32),
        ],
        compiler_params=pltpu.CompilerParams(vmem_limit_bytes=40 << 20),
        name="pixel_back",
    )(sizes, is_fine, grad, table, w_base, mixed_weight)


PAIR = 2 * HD


def pair_halves(rows):
    lane = lax.broadcasted_iota(jnp.int32, (rows, PAIR), 1)
    return [lane < HD, lane >= HD]


def attend_block(scale, query, key, value, mask):
    halves = pair_halves(query.shape[0])
    both = []
    for h in range(2):
        own = jnp.where(halves[h], query, jnp.zeros_like(query))
        scores = jnp.where(mask, nt(own, key) * scale, -1000000000.0)
        weights = jnp.exp(scores - jnp.max(scores, axis=1, keepdims=True))
        inverse = 1.0 / jnp.sum(weights, axis=1, keepdims=True)
        both.append(nn((weights * inverse).astype(jnp.bfloat16), value))
    return jnp.where(halves[0], both[0], both[1]).astype(jnp.bfloat16)


def block_masks(fine, start, rows, segment, segment_row, axis):
    inside = lax.broadcasted_iota(jnp.int32, (start, start), axis) < fine
    same = segment[...] == segment_row[...]
    return inside, same


def attend_kernel(scale, fine, start, query, key, value, segment, segment_row, mixed):
    rows = query.shape[0]
    masks = block_masks(fine, start, rows, segment, segment_row, 1)
    for here, mask in zip((slice(0, start), slice(start, rows)), masks):
        mixed[here, :] = attend_block(scale, query[here, :], key[here, :], value[here, :], mask)


def attend(qkv, segment, segment_row, fine, start):
    rows, width = qkv.shape
    heads = width // 3 // PAIR
    kernel = functools.partial(attend_kernel, 1.0 / math.sqrt(HD), fine, start)
    column = lambda k: pl.BlockSpec((rows, PAIR), lambda j: (0, k * heads + j))
    return pl.pallas_call(
        kernel,
        grid=(heads,),
        out_shape=jax.ShapeDtypeStruct((rows, width // 3), jnp.bfloat16),
        in_specs=[
            column(0),
            column(1),
            column(2),
            pl.BlockSpec((rows - start, 1), lambda j: (0, 0)),
            pl.BlockSpec((1, rows - start), lambda j: (0, 0)),
        ],
        out_specs=column(0),
        compiler_params=pltpu.CompilerParams(vmem_limit_bytes=48 << 20),
        name="attend",
    )(qkv, qkv, qkv, segment, segment_row)


def attend_back_block(scale, query, key, value, grad_mixed, mask):
    halves = pair_halves(query.shape[0])
    grad_query, grad_key, grad_value = [], 0.0, 0.0
    for h in range(2):
        own = jnp.where(halves[h], query, jnp.zeros_like(query))
        grad = jnp.where(halves[h], grad_mixed, jnp.zeros_like(grad_mixed))
        scores = jnp.where(mask, nt(key, own) * scale, -1000000000.0)
        weights = jnp.exp(scores - jnp.max(scores, axis=0, keepdims=True))
        probs = weights * (1.0 / jnp.sum(weights, axis=0, keepdims=True))
        grad_probs = nt(value, grad)
        inner = jnp.sum(probs * grad_probs, axis=0, keepdims=True)
        grad_scores = (probs * (grad_probs - inner)).astype(jnp.bfloat16)
        grad_value = grad_value + nn(probs.astype(jnp.bfloat16), grad)
        grad_key = grad_key + nn(grad_scores, own)
        grad_query.append(tn(grad_scores, key))
    grad_query = jnp.where(halves[0], grad_query[0], grad_query[1])
    return grad_query * scale, grad_key * scale, grad_value


LINE = 4
MESH_ID = pl.DeviceIdType.MESH
PIECE_ROWS = 192
PIECE_COLS = 384
CROSS_EVERY = 3
SEMS = 48


class Piece:
    def __init__(self, source, row, col, rows, cols, target, out_row, out_col, swap, cross):
        self.source, self.row, self.col, self.rows, self.cols = source, row, col, rows, cols
        self.target, self.out_row, self.out_col = target, out_row, out_col
        self.swap, self.cross = swap, cross


def move_pieces(pieces, scale, grads, outs, acc, land, land_right, land_left, sems, prepare):
    device = lax.axis_index("dp")
    core = lax.axis_index("tensor")
    place_x = lax.rem(device, 2)
    place_y = lax.rem(device // 2, 2)
    place_z = lax.rem(device // 4, LINE)
    mirror = LINE - 1 - place_z
    beside_x = (device + 1 - 2 * place_x, core)
    beside_y = (device + 2 - 4 * place_y, core)
    sibling = (device, 1 - core)
    up = (device + 4, core)
    down = (device - 4, core)

    barrier = pltpu.get_barrier_semaphore()
    for partner in (beside_x, beside_y, sibling):
        pl.semaphore_signal(barrier, inc=1, device_id=partner, device_id_type=MESH_ID)

    @pl.when(place_z < LINE - 1)
    def _():
        pl.semaphore_signal(barrier, inc=1, device_id=up, device_id_type=MESH_ID)

    @pl.when(place_z > 0)
    def _():
        pl.semaphore_signal(barrier, inc=1, device_id=down, device_id_type=MESH_ID)

    inner = (place_z + LINE - 1) // LINE + (2 * (LINE - 1) - place_z) // LINE
    pl.semaphore_wait(barrier, 3 + inner)

    def remote(src, dst, send, recv, where):
        return pltpu.make_async_remote_copy(
            src_ref=src,
            dst_ref=dst,
            send_sem=send,
            recv_sem=recv,
            device_id=where,
            device_id_type=MESH_ID,
        )

    work = prepare(core, place_x, sibling, remote)

    def rows_at(ref, start, size, column, width):
        return ref.at[pl.ds(pl.multiple_of(start, 8), size), pl.ds(pl.multiple_of(column, 128), width)]

    def add_rows(total, start, extra, size, width, factor=None):
        step = 24 if size % 24 == 0 else 8

        @pl.loop(0, size // step)
        def _(i):
            here = pl.ds(pl.multiple_of(start + i * step, 8), step)
            there = pl.ds(pl.multiple_of(i * step, 8), step)
            value = total[here, :width] + extra[there, :width]
            total[here, :width] = value if factor is None else value * factor

    def build(number, piece):
        half, chunk, width = piece.rows // 2, piece.rows // 8, piece.cols
        grad, out = grads[piece.source], outs[piece.target]
        mine = acc.at[number]
        sem = lambda k: sems.at[number, k]

        def out_at(x, owner, row, size):
            return rows_at(out, piece.out_row(x, owner) + row, size, piece.out_col(x), width)

        def y_copy():
            return remote(
                rows_at(grad, piece.row(place_x) + (1 - place_y) * half, half, piece.col, width),
                land.at[number, :half, :width],
                sem(0),
                sem(1),
                beside_y,
            )

        def load():
            return pltpu.make_async_copy(
                rows_at(grad, piece.row(place_x) + place_y * half, half, piece.col, width),
                mine.at[:half, :width],
                sem(2),
            )

        def right(k):
            return remote(
                rows_at(mine, (LINE - k + place_z) * chunk, chunk, 0, width),
                land_right.at[number, k - 1, :chunk, :width],
                sem(2 + k),
                sem(5 + k),
                up,
            )

        def left(k):
            return remote(
                rows_at(mine, (k - 1 - mirror) * chunk, chunk, 0, width),
                land_left.at[number, k - 1, :chunk, :width],
                sem(8 + k),
                sem(11 + k),
                down,
            )

        def got(slots, k, first, where):
            here = slots.at[number, k - 1, :chunk, :width]
            return remote(here, here, sem(first + k), sem(first + 3 + k), where)

        def send_line(k):
            @pl.when((place_z <= k - 1) & (place_z < LINE - 1))
            def _():
                right(k).start()

            @pl.when((mirror <= k - 1) & (mirror < LINE - 1))
            def _():
                left(k).start()

        def wait_line(k):
            @pl.when((place_z >= 1) & (place_z <= k))
            def _():
                got(land_right, k, 2, down).wait_recv()
                add_rows(
                    mine, (LINE - 1 - k + place_z) * chunk, land_right.at[number, k - 1], chunk, width
                )

            @pl.when((mirror >= 1) & (mirror <= k))
            def _():
                got(land_left, k, 8, up).wait_recv()
                add_rows(mine, (k - mirror) * chunk, land_left.at[number, k - 1], chunk, width)

        def own_chunk():
            return rows_at(mine, place_z * chunk, chunk, 0, width)

        def store():
            return pltpu.make_async_copy(
                own_chunk(), out_at(place_x, core, place_y * half + place_z * chunk, chunk), sem(17)
            )

        def share_out():
            return remote(
                own_chunk(),
                out_at(place_x, core, place_y * half + place_z * chunk, chunk),
                sem(15),
                sem(16),
                beside_x if piece.cross else beside_y,
            )

        def share_in():
            if piece.cross:
                there = out_at(1 - place_x, core, place_y * half + place_z * chunk, chunk)
                return remote(there, there, sem(15), sem(16), beside_x)
            there = out_at(place_x, core, (1 - place_y) * half + place_z * chunk, chunk)
            return remote(there, there, sem(15), sem(16), beside_y)

        def spread(k, position, where, first):
            copies = []
            for b in range(2):
                if piece.cross:
                    here = out_at(b, core, place_y * half + position * chunk, chunk)
                else:
                    here = out_at(place_x, core, b * half + position * chunk, chunk)
                at = first + 2 * (k - 1) + b
                copies.append(remote(here, here, sem(at), sem(at + 6), where))
            return copies

        def send_spread(k):
            @pl.when((place_z >= k - 1) & (place_z < LINE - 1))
            def _():
                for copy in spread(k, place_z - (k - 1), up, 18):
                    copy.start()

            @pl.when((mirror >= k - 1) & (mirror < LINE - 1))
            def _():
                for copy in spread(k, place_z + (k - 1), down, 30):
                    copy.start()

        def wait_spread(k):
            @pl.when(place_z >= k)
            def _():
                for copy in spread(k, place_z - k, down, 18):
                    copy.wait_recv()

            @pl.when(mirror >= k)
            def _():
                for copy in spread(k, place_z + k, up, 30):
                    copy.wait_recv()

        def last(outgoing):
            if piece.cross:
                row = (place_y if outgoing else 1 - place_y) * half
                views = [out_at(b, core, row, half) for b in range(2)]
                return [
                    remote(v, v, sem(42 + b), sem(44 + b), beside_y) for b, v in enumerate(views)
                ]
            view = out_at(place_x if outgoing else 1 - place_x, core, 0, piece.rows)
            return [remote(view, view, sem(42), sem(44), beside_x)]

        def swap(owner):
            views = [out_at(b, owner, 0, piece.rows) for b in range(2)]
            return [remote(v, v, sem(46 + b), sem(48 + b), sibling) for b, v in enumerate(views)]

        def stage_0():
            y_copy().start()
            load().start()

        def stage_1():
            load().wait()
            y_copy().wait_recv()
            add_rows(mine, 0, land.at[number], half, width)
            send_line(1)

        def stage_2():
            wait_line(1)
            send_line(2)

        def stage_3():
            wait_line(2)
            send_line(3)

        def stage_4():
            wait_line(3)

            @pl.loop(0, chunk // 8)
            def _(i):
                here = pl.ds(pl.multiple_of(place_z * chunk + i * 8, 8), 8)
                mine[here, :width] = mine[here, :width] * scale

            share_out().start()
            store().start()

        def stage_5():
            store().wait()
            share_in().wait_recv()
            send_spread(1)

        def stage_6():
            wait_spread(1)
            send_spread(2)

        def stage_7():
            wait_spread(2)
            send_spread(3)

        def stage_8():
            wait_spread(3)
            for copy in last(True):
                copy.start()

        def stage_9():
            for copy in last(False):
                copy.wait_recv()
            if piece.swap:
                for copy in swap(core):
                    copy.start()

        def stage_10():
            if piece.swap:
                for copy in swap(1 - core):
                    copy.wait_recv()
                for copy in swap(core):
                    copy.wait_send()
            y_copy().wait_send()
            share_out().wait_send()
            for copy in last(True):
                copy.wait_send()
            for k in range(1, LINE):

                @pl.when((place_z <= k - 1) & (place_z < LINE - 1))
                def _():
                    right(k).wait_send()

                @pl.when((mirror <= k - 1) & (mirror < LINE - 1))
                def _():
                    left(k).wait_send()

                @pl.when((place_z >= k - 1) & (place_z < LINE - 1))
                def _():
                    for copy in spread(k, place_z - (k - 1), up, 18):
                        copy.wait_send()

                @pl.when((mirror >= k - 1) & (mirror < LINE - 1))
                def _():
                    for copy in spread(k, place_z + (k - 1), down, 30):
                        copy.wait_send()

        return [
            stage_0,
            stage_1,
            stage_2,
            stage_3,
            stage_4,
            stage_5,
            stage_6,
            stage_7,
            stage_8,
            stage_9,
            stage_10,
        ]

    lines = [build(number, piece) for number, piece in enumerate(pieces)]
    groups = [lines[i : i + GROUP] for i in range(0, len(lines), GROUP)]
    depth = len(lines[0])
    for j in range(min(AHEAD, len(groups))):
        for line in groups[j]:
            line[0]()
    late = depth - 2
    for tick in range(len(groups) + depth - 1):
        if tick + AHEAD < len(groups):
            for line in groups[tick + AHEAD]:
                line[0]()
        for job in work.pop(0) if work else ():
            job()
        active = range(max(0, tick - depth + 1), min(tick, len(groups)))
        for j in [j for j in active if tick - j < late] + [j for j in active if tick - j >= late]:
            for line in groups[j]:
                line[tick - j]()


GROUP = 2
AHEAD = 1


def sync_plan(grads, outs):
    pieces = []
    for source, (rows, cols, step_x) in enumerate(grads):
        start = 0
        for target, width, row_x, row_core, col_x, out_start in outs[source]:
            tall = min(PIECE_ROWS, rows)
            wide = min(PIECE_COLS, width)
            if width % wide:
                wide = width // 2
            for row in range(0, rows, tall):
                for col in range(0, width, wide):
                    pieces.append(
                        Piece(
                            source,
                            lambda x, row=row, a=step_x: row + x * a,
                            start + col,
                            tall,
                            wide,
                            target,
                            lambda x, core, row=row, a=row_x, b=row_core: row + x * a + core * b,
                            lambda x, c=out_start + col, a=col_x: c + x * a,
                            row_core != 0,
                            len(pieces) % CROSS_EVERY == CROSS_EVERY - 1,
                        )
                    )
            start += width
    return pieces


QUERY_BLOCK = 384
FIRST_TICKS = 8
LN_ROWS = 112
POINT_ROWS = 64


def back_kernel(pieces, sizes, fine, start, points, counts, *refs):
    replicas, given = counts
    (
        qkv,
        grad_mixed,
        segment,
        segment_row,
        normed_part,
        w_qkv,
        standard,
        inverse,
        grad_middle,
        gain,
        tokens,
        patches,
        fine_pairs,
        pos_fine,
        pos,
        rest,
    ) = refs[:16]
    early = refs[16 : 16 + given]
    refs = refs[16 + given :]
    outs, grad_embedded, refs = refs[:sizes], refs[sizes], refs[sizes + 1 :]
    (
        grad_qkv,
        grad_key,
        grad_value,
        partial,
        arrived,
        grad_w_qkv,
        grad_w_base,
        bundle,
        acc,
        land,
        land_right,
        land_left,
        sems,
        swap_sems,
        chunk_standard,
        chunk_middle,
        chunk_sems,
    ) = refs
    rows, width = standard.shape
    third = qkv.shape[1] // 3
    scale = 1.0 / math.sqrt(HD)
    low = lambda value: value.astype(jnp.bfloat16)
    blocks = range(0, rows, LN_ROWS)

    def prepare(core, place_x, sibling, remote):
        def back_rows(pair, here, keys, mask):
            column = lambda k: slice(k * third + pair * PAIR, k * third + (pair + 1) * PAIR)
            return attend_back_block(
                scale,
                qkv[here, column(0)],
                qkv[keys, column(1)],
                qkv[keys, column(2)],
                grad_mixed[here, column(0)],
                mask,
            )

        def store_qkv(pair, k, here, value):
            grad_qkv[here, k * third + pair * PAIR : k * third + (pair + 1) * PAIR] = low(value)

        def fine_job(pair, begin):
            def job():
                here = slice(begin, min(begin + QUERY_BLOCK, start))
                keys = slice(0, start)
                inside = lax.broadcasted_iota(jnp.int32, (start, here.stop - begin), 0) < fine
                grad_q, grad_k, grad_v = back_rows(pair, here, keys, inside)
                store_qkv(pair, 0, here, grad_q)
                if begin == 0:
                    grad_key[...] = grad_k
                    grad_value[...] = grad_v
                else:
                    grad_key[...] += grad_k
                    grad_value[...] += grad_v
                if here.stop == start:
                    store_qkv(pair, 1, keys, grad_key[...])
                    store_qkv(pair, 2, keys, grad_value[...])

            return job

        def coarse_job(pair):
            def job():
                here = slice(start, rows)
                same = segment[...] == segment_row[...]
                for k, value in enumerate(back_rows(pair, here, here, same)):
                    store_qkv(pair, k, here, value)

            return job

        def weight_job():
            grad_w_qkv[...] = tn(normed_part[...], grad_qkv[...])

        def partial_job():
            partial[...] = nt(grad_qkv[...], w_qkv[...])
            swap().start()

        def swap():
            return remote(partial, arrived, swap_sems.at[0], swap_sems.at[1], sibling)

        def chunk_copies(number):
            here = pl.ds(pl.multiple_of(number * LN_ROWS, 8), LN_ROWS)
            at = lax.rem(number, 2)
            return [
                pltpu.make_async_copy(standard.at[here], chunk_standard.at[at], chunk_sems.at[0, at]),
                pltpu.make_async_copy(
                    grad_middle.at[here], chunk_middle.at[at], chunk_sems.at[1, at]
                ),
            ]

        def norm_job():
            swap().wait()
            for copy in chunk_copies(0):
                copy.start()
            for k in range(3):
                bundle[points + k : points + k + 1, :] = jnp.zeros((1, width), jnp.float32)

            @pl.loop(0, len(blocks))
            def _(number):
                @pl.when(number + 1 < len(blocks))
                def _():
                    for copy in chunk_copies(number + 1):
                        copy.start()

                for copy in chunk_copies(number):
                    copy.wait()
                at = lax.rem(number, 2)

                @pl.loop(0, LN_ROWS // 16)
                def _(i):
                    inner = pl.ds(pl.multiple_of(i * 16, 8), 16)
                    here = pl.ds(pl.multiple_of(number * LN_ROWS + i * 16, 8), 16)
                    grad = partial[here, :] + arrived[here, :]
                    z = chunk_standard[at, inner, :]
                    up = grad * gain[...]
                    mean = jnp.mean(up, axis=1, keepdims=True)
                    along = jnp.mean(up * z, axis=1, keepdims=True)
                    value = (
                        chunk_middle[at, inner, :] + (up - mean - z * along) * inverse[here, :]
                    )
                    grad_embedded[here, :] = value
                    column = lambda v: jnp.sum(v, axis=0, keepdims=True)
                    bundle[points : points + 1, :] += column(low(value).astype(jnp.float32))
                    bundle[points + 1 : points + 2, :] += column(grad * z)
                    bundle[points + 2 : points + 3, :] += column(grad)

        def base_job():
            half = grad_w_base.shape[0]
            channels = patches.shape[0]
            part = grad_w_base.shape[1] // channels
            area = 2 * part
            columns = pl.ds(pl.multiple_of(core * half, 128), half)
            stride = tokens.shape[1]
            some = low(grad_embedded[:fine, columns])
            wanted = fine_pairs[:, pl.ds(pl.multiple_of(place_x * part, 128), part)]
            for c in range(channels):
                gathered = low(tn(patches[c, :fine, :], some))
                total = tn(gathered, wanted)
                for k in range(3):
                    begin = start + k * stride
                    here = pl.ds(pl.multiple_of(c * area + place_x * part, 128), part)
                    total += tn(low(grad_embedded[begin : begin + stride, columns]), tokens[k, :, here])
                grad_w_base[:, c * part : (c + 1) * part] = total

        def bundle_job():
            gathered = tn(pos_fine[...], low(grad_embedded[:fine, :]))
            count = pos.shape[1]
            for k in range(3):
                begin = start + k * tokens.shape[1]
                gathered += tn(pos[k], low(grad_embedded[begin : begin + count, :]))
            bundle[:points, :] = gathered
            bundle[points + 3 : 2 * POINT_ROWS, :] = rest[points + 3 : 2 * POINT_ROWS, :]
            sums = jnp.sum(grad_qkv[...].astype(jnp.float32), axis=0, keepdims=True)
            bundle[points + 7 : points + 8, :third] = sums[:, :third]
            bundle[points + 7 : points + 8, third : 2 * third] = sums[:, 2 * third :]

        heads = []
        for pair in range(third // PAIR):
            heads += [fine_job(pair, begin) for begin in range(0, start, QUERY_BLOCK)]
            heads.append(coarse_job(pair))
        ticks = FIRST_TICKS
        parts = [heads[len(heads) * k // ticks : len(heads) * (k + 1) // ticks] for k in range(ticks)]
        parts[-1] = parts[-1] + [weight_job]
        return parts + [[partial_job], [norm_job], [base_job], [bundle_job]]

    move_pieces(
        pieces,
        1.0 / replicas,
        list(early) + [grad_w_qkv, grad_w_base, bundle],
        outs,
        acc,
        land,
        land_right,
        land_left,
        sems,
        prepare,
    )


def back_and_sync(
    qkv,
    grad_mixed,
    segment,
    segment_row,
    normed_part,
    w_qkv,
    standard,
    inverse,
    grad_middle,
    gain,
    tokens,
    patches,
    fine_pairs,
    pos_fine,
    pos,
    rest,
    early,
    out_shapes,
    grads,
    outs,
    fine,
    start,
    replicas,
):
    rows, width = standard.shape
    channels = patches.shape[0]
    pieces = sync_plan(grads, outs)
    count = len(pieces)
    high = max(p.rows for p in pieces)
    wide = max(p.cols for p in pieces)
    points = pos.shape[2]
    kernel = functools.partial(
        back_kernel, pieces, len(out_shapes), fine, start, points, (replicas, len(early))
    )
    f32 = lambda *dims: pltpu.VMEM(dims, jnp.float32)
    anywhere = pl.BlockSpec(memory_space=pl.ANY)
    results = pl.pallas_call(
        kernel,
        out_shape=[jax.ShapeDtypeStruct(s, jnp.float32) for s in out_shapes]
        + [jax.ShapeDtypeStruct((rows, width), jnp.float32)],
        in_specs=[VMEM] * 6
        + [anywhere, VMEM, anywhere]
        + [VMEM] * 7
        + [anywhere] * len(early),
        out_specs=[anywhere] * len(out_shapes) + [VMEM],
        scratch_shapes=[
            pltpu.VMEM(qkv.shape, jnp.bfloat16),
            f32(start, PAIR),
            f32(start, PAIR),
            f32(rows, width),
            f32(rows, width),
            f32(width // 2, qkv.shape[1]),
            f32(width // 2, channels * fine_pairs.shape[1] // 2),
            f32(2 * POINT_ROWS, width),
            f32(count, high // 2, wide),
            f32(count, high // 2, wide),
            f32(count, LINE - 1, high // 8, wide),
            f32(count, LINE - 1, high // 8, wide),
            pltpu.SemaphoreType.DMA((count, SEMS + 2)),
            pltpu.SemaphoreType.DMA((2,)),
            f32(2, LN_ROWS, width),
            f32(2, LN_ROWS, width),
            pltpu.SemaphoreType.DMA((2, 2)),
        ],
        compiler_params=pltpu.CompilerParams(
            collective_id=0, has_side_effects=True, vmem_limit_bytes=63 << 20
        ),
        name="back_and_sync",
    )(
        qkv,
        grad_mixed,
        segment,
        segment_row,
        normed_part,
        w_qkv,
        standard,
        inverse,
        grad_middle,
        gain,
        tokens,
        patches,
        fine_pairs,
        pos_fine,
        pos,
        rest,
        *early,
    )
    return results[:-1], results[-1]


def tensor_sum(partial):
    return partial + lax.ppermute(partial, "tensor", [(0, 1), (1, 0)])


def swap_cores(value):
    return lax.ppermute(value, "tensor", [(0, 1), (1, 0)])


def merged_rows(fine_rows, light_rows, second, counts, start, stride, rows):
    width = fine_rows.shape[1]
    keep = jnp.arange(stride, dtype=jnp.int32)[:, None]
    fine = fine_rows.shape[0]
    padded = jnp.pad(light_rows, ((0, stride), (0, 0)))
    third = padded[:stride]
    fourth = lax.dynamic_slice_in_dim(padded, counts[2], stride, axis=0)
    blocks = [
        jnp.pad(fine_rows, ((0, start - fine), (0, 0))),
        jnp.pad(second, ((0, stride - second.shape[0]), (0, 0))),
        jnp.where(keep < counts[2], third, 0.0),
        jnp.where(keep < counts[3], fourth, 0.0),
        jnp.zeros((rows - start - 3 * stride, width), fine_rows.dtype),
    ]
    return jnp.concatenate(blocks, axis=0)


def own_rows(merged, is_fine, counts, fine, start, stride, rows):
    width = merged.shape[1]
    coarse = counts[1]
    heavy = jnp.concatenate(
        [
            merged[:fine],
            merged[start : start + stride],
            jnp.zeros((rows - fine - stride, width), merged.dtype),
        ],
        axis=0,
    )
    row = jnp.arange(rows, dtype=jnp.int32)[:, None]
    third = jnp.pad(merged[start + stride : start + 2 * stride], ((0, rows - stride), (0, 0)))
    fourth = jnp.pad(merged[start + 2 * stride : start + 3 * stride], ((stride, rows), (0, 0)))
    fourth = lax.dynamic_slice_in_dim(fourth, stride - counts[2], rows, axis=0)
    light = jnp.where(row < counts[2], third, fourth)
    used = jnp.where(is_fine, fine + coarse, counts[2] + counts[3])
    return jnp.where(row < used, jnp.where(is_fine, heavy, light), jnp.zeros_like(heavy))


def local(
    pixels,
    patch_size,
    counts,
    offsets,
    resize_table,
    pos_table,
    w_base,
    patch_bias,
    pos_base,
    gain_one,
    shift_one,
    w_query,
    bias_query,
    w_key,
    w_value,
    bias_value,
    w_out,
    bias_out,
    gain_two,
    shift_two,
    w_up,
    bias_up,
    w_down,
    bias_down,
    cotangent,
):
    wide = lambda value: value.astype(jnp.float32)
    images, channels, res, _ = pixels.shape
    rows_total = cotangent.shape[0]
    replicas = lax.axis_size("dp")
    core = lax.axis_index("tensor")
    side_x = lax.rem(lax.axis_index("dp"), 2)
    fine = (res // FINE) ** 2
    small = (res // COARSE[0]) ** 2
    start = up_to(fine, 16)
    stride = up_to(small, 8)
    rows = up_to(start + 3 * stride, 16)

    there = [(i, i ^ 1) for i in range(replicas)]
    other_sizes = lax.ppermute(patch_size, "dp", there)
    own_pix = jnp.pad(wide(pixels), ((0, 0), (0, 0), (0, 0), (0, -res % 128)))
    direct = lax.ppermute(
        lax.dynamic_index_in_dim(own_pix, core, 0, keepdims=False), "dp", there
    )
    half_rows = rows_total // 2
    own_cotangent = wide(cotangent)
    cot_half = lax.dynamic_slice_in_dim(own_cotangent, core * half_rows, half_rows, axis=0)
    w_qkv = jnp.concatenate([w_query, w_key, w_value], axis=1)
    bias_qkv = jnp.concatenate([bias_query, jnp.zeros_like(bias_query), bias_value])
    pos_fine = pos_table[res // FINE, :fine]
    pos_coarse = pos_table[:, :stride]
    direct, other_sizes, cot_half, w_qkv, bias_qkv, pos_fine, pos_coarse = (
        lax.optimization_barrier(
            (direct, other_sizes, cot_half, w_qkv, bias_qkv, pos_fine, pos_coarse)
        )
    )
    across = swap_cores(direct)
    cot_direct = lax.ppermute(cot_half, "dp", there)
    cot_across = swap_cores(cot_direct)
    is_fine = patch_size[0] == FINE
    fine_first = is_fine.astype(jnp.int32)
    sizes = jnp.where(
        is_fine,
        jnp.concatenate([patch_size, other_sizes]),
        jnp.concatenate([other_sizes, patch_size]),
    )
    slots = jnp.stack([0 * core, 0 * core + 1, core, 1 - core]) + 2 * jnp.stack(
        [1 - fine_first] * 2 + [fine_first] * 2
    )
    counts4 = (res // sizes) ** 2
    (
        embedded,
        standard_one,
        inverse_one,
        normed_one,
        tokens,
        patches,
        mixed_weight,
        fine_pairs,
        pos,
        segment,
        segment_row,
    ) = embed(
        sizes,
        slots,
        resize_table,
        pos_fine,
        pos_coarse,
        w_base,
        [wide(patch_bias)[None], wide(gain_one)[None], wide(shift_one)[None]],
        pos_base,
        [own_pix, direct, across],
        rows,
    )
    qkv = (
        jnp.dot(normed_one, w_qkv, preferred_element_type=jnp.float32) + wide(bias_qkv)
    ).astype(jnp.bfloat16)
    mixed = attend(qkv, segment, segment_row, fine, start)
    attended = tensor_sum(jnp.dot(mixed, w_out, preferred_element_type=jnp.float32)) + wide(
        bias_out
    )
    middle = embedded + attended
    standard_two, standard_back_two = jax.vjp(standardize, middle)
    normed_two = (standard_two * wide(gain_two) + wide(shift_two)).astype(jnp.bfloat16)
    hidden = jnp.dot(normed_two, w_up, preferred_element_type=jnp.float32) + wide(bias_up)
    activated_wide, gelu_back = jax.vjp(jax.nn.gelu, hidden)
    activated = activated_wide.astype(jnp.bfloat16)
    branch = tensor_sum(jnp.dot(activated, w_down, preferred_element_type=jnp.float32)) + wide(
        bias_down
    )
    output = own_rows(
        (middle + branch).astype(jnp.bfloat16), is_fine, counts4, fine, start, stride, rows_total
    )
    other_cotangent = jnp.where(
        core == 0,
        jnp.concatenate([cot_direct, cot_across]),
        jnp.concatenate([cot_across, cot_direct]),
    )
    fine_cotangent = jnp.where(is_fine, own_cotangent, other_cotangent)
    light_cotangent = jnp.where(
        is_fine, other_cotangent[: 2 * stride], own_cotangent[: 2 * stride]
    )
    grad_out = (
        merged_rows(
            fine_cotangent[:fine],
            light_cotangent,
            fine_cotangent[fine : fine + small],
            counts4,
            start,
            stride,
            rows,
        )
    )
    grad_branch = grad_out.astype(jnp.bfloat16)
    own_part = lambda value: lax.dynamic_slice_in_dim(
        value, side_x * (value.shape[1] // 2), value.shape[1] // 2, axis=1
    )
    grad_w_down = jnp.einsum(
        "tf,td->fd", own_part(activated), grad_branch, preferred_element_type=jnp.float32
    )
    grad_activated = jnp.einsum(
        "td,fd->tf", grad_branch, w_down, preferred_element_type=jnp.float32
    )
    grad_hidden = gelu_back(grad_activated)[0].astype(jnp.bfloat16)
    grad_w_up = jnp.einsum(
        "td,tf->df", own_part(normed_two), grad_hidden, preferred_element_type=jnp.float32
    )
    grad_bias_up = jnp.sum(grad_hidden, axis=0, dtype=jnp.float32)
    grad_normed_two = tensor_sum(
        jnp.einsum("tf,df->td", grad_hidden, w_up, preferred_element_type=jnp.float32)
    )
    grad_middle = grad_out + standard_back_two(grad_normed_two * wide(gain_two))[0]
    grad_attended = grad_middle.astype(jnp.bfloat16)
    grad_w_out = jnp.einsum(
        "te,td->ed", own_part(mixed), grad_attended, preferred_element_type=jnp.float32
    )
    grad_mixed = jnp.einsum(
        "td,ed->te", grad_attended, w_out, preferred_element_type=jnp.float32
    ).astype(jnp.bfloat16)
    points = pos.shape[2]
    width = grad_attended.shape[1]
    bundle = jnp.concatenate(
        [
            jnp.zeros((points + 3, width), jnp.float32),
            jnp.sum(grad_attended, axis=0, dtype=jnp.float32)[None],
            jnp.sum(grad_normed_two * standard_two, axis=0)[None],
            jnp.sum(grad_normed_two, axis=0)[None],
            jnp.sum(grad_branch, axis=0, dtype=jnp.float32)[None],
            jnp.zeros((1, width), jnp.float32),
            grad_bias_up.reshape(-1, width),
        ],
        axis=0,
    )
    used = bundle.shape[0]
    bundle = jnp.pad(bundle, ((0, 2 * POINT_ROWS - used), (0, 0)))
    early = [grad_w_down, grad_w_up, grad_w_out]
    area = w_base.shape[1] // channels
    ff = w_down.shape[0]
    deep = w_up.shape[0]
    cut = bias_query.shape[0]
    out_shapes = [
        w_base.shape,
        w_down.shape,
        w_up.shape,
        w_query.shape,
        w_key.shape,
        w_value.shape,
        w_out.shape,
        bundle.shape,
    ]
    grads = [
        (ff // 2, width, 0),
        (deep // 2, ff, 0),
        (cut // 2, width, 0),
        (deep // 2, 3 * cut, 0),
        (width // 2, w_base.shape[1] // 2, 0),
        (POINT_ROWS, width, POINT_ROWS),
    ]
    outs = [
        [(1, width, ff // 2, 0, 0, 0)],
        [(2, ff, deep // 2, 0, 0, 0)],
        [(6, width, cut // 2, 0, 0, 0)],
        [(3 + k, cut, deep // 2, 0, 0, 0) for k in range(3)],
        [(0, area // 2, 0, width // 2, area // 2, area * c) for c in range(channels)],
        [(7, width, POINT_ROWS, 0, 0, 0)],
    ]
    synced, grad_embedded = back_and_sync(
        qkv,
        grad_mixed,
        segment,
        segment_row,
        own_part(normed_one),
        w_qkv,
        standard_one,
        inverse_one,
        grad_middle,
        wide(gain_one)[None],
        tokens,
        patches,
        fine_pairs,
        pos_fine,
        pos,
        bundle,
        early,
        out_shapes,
        grads,
        outs,
        fine,
        start,
        replicas,
    )
    beyond = replicas // 16
    step = 1
    while step < beyond:
        swap = [(i, (i // 16 ^ step) * 16 + i % 16) for i in range(replicas)]
        synced = [part + lax.ppermute(part, "dp", swap) for part in synced]
        step *= 2
    pixel_grad = pixel_back(
        sizes,
        is_fine.astype(jnp.int32)[None],
        grad_embedded,
        resize_table,
        w_base,
        mixed_weight,
        pixels.shape,
    )
    base_s, down_s, up_s, query_s, key_s, value_s, out_s, small_s = synced
    line = lambda k: small_s[points + k]
    return (
        output,
        pixel_grad,
        base_s,
        line(0),
        small_s[:points].T,
        line(1),
        line(2),
        query_s,
        line(7)[:cut],
        key_s,
        value_s,
        line(7)[cut:],
        out_s,
        line(3),
        line(4),
        line(5),
        up_s,
        small_s[points + 8 : used].reshape(-1),
        down_s,
        line(6),
    )


def solution(mesh):
    in_specs = (
        P("dp", None, None, None),
        P("dp"),
        P("dp"),
        P("dp"),
        P(),
        P(),
        P(),
        P(),
        P(),
        P(),
        P(),
        P(None, "tensor"),
        P("tensor"),
        P(None, "tensor"),
        P(None, "tensor"),
        P("tensor"),
        P("tensor", None),
        P(),
        P(),
        P(),
        P(None, "tensor"),
        P("tensor"),
        P("tensor", None),
        P(),
        P("dp", None),
    )
    out_specs = (
        P("dp", None),
        P("dp", None, None, None),
        P(),
        P(),
        P(),
        P(),
        P(),
        P(None, "tensor"),
        P("tensor"),
        P(None, "tensor"),
        P(None, "tensor"),
        P("tensor"),
        P("tensor", None),
        P(),
        P(),
        P(),
        P(None, "tensor"),
        P("tensor"),
        P("tensor", None),
        P(),
    )
    return jax.shard_map(local, mesh=mesh, in_specs=in_specs, out_specs=out_specs, check_vma=False)
```

```python
import functools
import math

import jax
import jax.numpy as jnp
from jax import lax
from jax.experimental import pallas as pl
from jax.experimental.pallas import tpu as pltpu
from jax.sharding import PartitionSpec as P

HD = 64
VMEM = pl.BlockSpec(memory_space=pltpu.VMEM)
SMEM = pl.BlockSpec(memory_space=pltpu.SMEM)


def standardize(values):
    centered = values - jnp.mean(values, axis=-1, keepdims=True)
    spread = jnp.mean(centered * centered, axis=-1, keepdims=True)
    return centered * lax.rsqrt(spread + 1e-06)


FINE = 8
COARSE = (24, 30, 40, 48)
NORM_ROWS = 112


def nt(left, right):
    return lax.dot_general(left, right, (((1,), (1,)), ((), ())), preferred_element_type=jnp.float32)


def tn(left, right):
    return lax.dot_general(left, right, (((0,), (0,)), ((), ())), preferred_element_type=jnp.float32)


def nn(left, right):
    return jnp.dot(left, right, preferred_element_type=jnp.float32)


def up_to(value, step):
    return value + -value % step


def loop(count, body, unroll):
    if unroll:
        for i in range(count):
            body(i)
    else:
        pl.loop(0, count)(body)


def aligned(start, side):
    return pl.multiple_of(start, 8) if side % 8 == 0 and not isinstance(start, int) else start


def fill_pairs(pair, long, table, side):
    base = table.shape[1]
    entry = lax.broadcasted_iota(jnp.int32, (base, base * base), 0)
    place = lax.broadcasted_iota(jnp.int32, (base, base * base), 1)
    repeat = (place // base == entry).astype(jnp.bfloat16)
    tile = (place % base == entry).astype(jnp.bfloat16)
    wide = nn(table, repeat)[:side]
    long[...] = nn(table, tile)

    def one(s):
        pair[pl.ds(aligned(s * side, side), side), :] = wide * long[pl.ds(s, 1), :]

    loop(side, one, True)


def cut_patches(line, pix, image, channel, side, grid, res):
    def one(x):
        block = pix[image, channel, pl.ds(aligned(x * side, side), side), :]
        line[pl.ds(aligned(x * res, 8), res), :side] = block.T[:res]

    loop(grid, one, True)
    return jnp.concatenate(
        [line[pl.ds(s, grid * grid, stride=side), :side] for s in range(side)], axis=1
    ).astype(jnp.bfloat16)


def place_patches(line, pixel_grad, image, channel, patch, side, grid, res):
    for s in range(side):
        line[pl.ds(s, grid * grid, stride=side), :side] = patch[:, s * side : (s + 1) * side]

    def one(x):
        block = line[pl.ds(aligned(x * res, 8), res), :side]
        pixel_grad[image, channel, pl.ds(aligned(x * side, side), side), :] = block.T

    loop(grid, one, True)


def embed_kernel(
    sizes,
    slots,
    table,
    pos_fine,
    pos_all,
    weight,
    bias,
    pos_base,
    gain,
    shift,
    own,
    direct,
    across,
    emb,
    standard,
    inverse,
    normed,
    tokens,
    patches,
    mixed_weight,
    fine_pairs,
    pos,
    segment,
    segment_row,
    pix,
    line,
    pair,
    long,
    sems,
):
    area = table.shape[2] ** 2
    channels, res = pix.shape[1:3]
    grid = res // FINE
    count = grid * grid
    start = up_to(count, 16)
    stride = tokens.shape[1]
    low = jnp.bfloat16
    copies = [
        pltpu.make_async_copy(source, pix.at[slots[k]], sems.at[k])
        for k, source in enumerate((own.at[0], own.at[1], direct, across))
    ]
    for copy in copies:
        copy.start()
    emb[...] = jnp.broadcast_to(bias[...], emb.shape)
    tokens[...] = jnp.zeros_like(tokens)
    fill_pairs(pair, long, table[FINE], FINE)
    fine_pairs[...] = pair[: FINE * FINE, :].astype(low)
    emb[:count, :] += nt(pos_fine[...], pos_base[...])
    for target, axis in ((segment, 0), (segment_row, 1)):
        row = lax.broadcasted_iota(jnp.int32, target.shape, axis)
        found = jnp.full(target.shape, 4, jnp.int32)
        for k in range(1, 4):
            side = res // sizes[k]
            within = row - (k - 1) * stride
            found = jnp.where((within >= 0) & (within < side * side), k, found)
        target[...] = found
    for copy in copies:
        copy.wait()

    for c in range(channels):
        columns = slice(c * area, (c + 1) * area)
        patch = cut_patches(line, pix, 0, c, FINE, grid, res)
        mixed = nt(fine_pairs[...], weight[:, columns]).astype(low)
        mixed_weight[c] = mixed
        patches[c, :count, :] = patch
        emb[:count, :] += nn(patch, mixed)

    @pl.loop(1, 4)
    def _(slot):
        row = pl.multiple_of(start + (slot - 1) * stride, 8)
        for side in COARSE:
            grid = res // side
            count = grid * grid

            @pl.when(sizes[slot] == side)
            def _():
                fill_pairs(pair, long, table[side], side)
                here = pl.ds(row, count)
                pos[slot - 1] = pos_all[grid]
                emb[here, :] += nt(pos_all[grid, :count, :], pos_base[...])
                for c in range(channels):
                    columns = slice(c * area, (c + 1) * area)
                    patch = cut_patches(line, pix, slot, c, side, grid, res)
                    token = nn(patch, pair[: side * side, :].astype(low)).astype(low)
                    tokens[slot - 1, :count, columns] = token
                    emb[here, :] += nt(token, weight[:, columns])

    @pl.loop(0, emb.shape[0] // NORM_ROWS)
    def _(i):
        here = pl.ds(pl.multiple_of(i * NORM_ROWS, 16), NORM_ROWS)
        value = emb[here, :]
        centered = value - jnp.mean(value, axis=1, keepdims=True)
        scale = lax.rsqrt(jnp.mean(centered * centered, axis=1, keepdims=True) + 1e-06)
        standard[here, :] = centered * scale
        inverse[here, :] = scale
        normed[here, :] = (centered * scale * gain[...] + shift[...]).astype(low)


def embed(sizes, slots, table, pos_fine, pos_all, w_base, rows_of, pos_base, pixels, rows):
    own = pixels[0]
    _, channels, res, lanes = own.shape
    width, features = w_base.shape
    fine = (res // FINE) ** 2
    side = table.shape[1]
    area = features // channels
    stride = pos_all.shape[1]
    rest = rows - up_to(fine, 16)
    shape = jax.ShapeDtypeStruct
    return pl.pallas_call(
        embed_kernel,
        out_shape=[
            shape((rows, width), jnp.float32),
            shape((rows, width), jnp.float32),
            shape((rows, 1), jnp.float32),
            shape((rows, width), jnp.bfloat16),
            shape((3, stride, features), jnp.bfloat16),
            shape((channels, up_to(fine, 16), FINE * FINE), jnp.bfloat16),
            shape((channels, FINE * FINE, width), jnp.bfloat16),
            shape((FINE * FINE, area), jnp.bfloat16),
            shape((3,) + pos_all.shape[1:], jnp.bfloat16),
            shape((rest, 1), jnp.int32),
            shape((1, rest), jnp.int32),
        ],
        in_specs=[SMEM] * 2 + [VMEM] * 8 + [pl.BlockSpec(memory_space=pl.ANY)] * 3,
        out_specs=[VMEM] * 11,
        scratch_shapes=[
            pltpu.VMEM((4, channels, res, lanes), jnp.float32),
            pltpu.VMEM((res * res // FINE, 128), jnp.float32),
            pltpu.VMEM((side * side, area), jnp.float32),
            pltpu.VMEM((side, area), jnp.float32),
            pltpu.SemaphoreType.DMA((4,)),
        ],
        compiler_params=pltpu.CompilerParams(vmem_limit_bytes=56 << 20),
        name="embed",
    )(sizes, slots, table, pos_fine, pos_all, w_base, rows_of[0], pos_base, *rows_of[1:], *pixels)


def pixel_kernel(sizes, is_fine, grad, table, weight, mixed_weight, pixel_grad, line, pair, long):
    area = table.shape[2] ** 2
    channels, res = pixel_grad.shape[1:3]
    start = up_to((res // FINE) ** 2, 16)
    stride = up_to((res // COARSE[0]) ** 2, 8)
    low = jnp.bfloat16

    @pl.when(is_fine[0] == 1)
    def _():
        grid = res // FINE
        count = grid * grid
        for c in range(channels):
            patch = nt(grad[:count, :].astype(low), mixed_weight[c])
            place_patches(line, pixel_grad, 0, c, patch, FINE, grid, res)

    @pl.loop(1, 4)
    def _(slot):
        row = pl.multiple_of(start + (slot - 1) * stride, 8)
        wanted = jnp.where(slot == 1, is_fine[0], 1 - is_fine[0])
        image = jnp.where(slot == 1, 1, slot - 2)
        for side in COARSE:
            grid = res // side
            count = grid * grid

            @pl.when((sizes[slot] == side) & (wanted == 1))
            def _():
                fill_pairs(pair, long, table[side], side)
                rows = grad[pl.ds(row, count), :].astype(low)

                @pl.loop(0, channels)
                def _(c):
                    columns = pl.ds(pl.multiple_of(c * area, area), area)
                    token = nn(rows, weight[:, columns]).astype(low)
                    patch = nt(token, pair[: side * side, :].astype(low))
                    place_patches(line, pixel_grad, image, c, patch, side, grid, res)


def pixel_back(sizes, is_fine, grad, table, w_base, mixed_weight, shape):
    _, channels, res, _ = shape
    width, features = w_base.shape
    side = table.shape[1]
    return pl.pallas_call(
        pixel_kernel,
        out_shape=jax.ShapeDtypeStruct(shape, jnp.float32),
        in_specs=[SMEM] * 2 + [VMEM] * 4,
        out_specs=VMEM,
        scratch_shapes=[
            pltpu.VMEM((res * res // FINE, 128), jnp.float32),
            pltpu.VMEM((side * side, features // channels), jnp.float32),
            pltpu.VMEM((side, features // channels), jnp.float32),
        ],
        compiler_params=pltpu.CompilerParams(vmem_limit_bytes=40 << 20),
        name="pixel_back",
    )(sizes, is_fine, grad, table, w_base, mixed_weight)


PAIR = 2 * HD


def pair_halves(rows):
    lane = lax.broadcasted_iota(jnp.int32, (rows, PAIR), 1)
    return [lane < HD, lane >= HD]


def attend_block(scale, query, key, value, mask):
    halves = pair_halves(query.shape[0])
    both = []
    for h in range(2):
        own = jnp.where(halves[h], query, jnp.zeros_like(query))
        scores = jnp.where(mask, nt(own, key) * scale, -1000000000.0)
        weights = jnp.exp(scores - jnp.max(scores, axis=1, keepdims=True))
        inverse = 1.0 / jnp.sum(weights, axis=1, keepdims=True)
        both.append(nn((weights * inverse).astype(jnp.bfloat16), value))
    return jnp.where(halves[0], both[0], both[1]).astype(jnp.bfloat16)


def block_masks(fine, start, rows, segment, segment_row, axis):
    inside = lax.broadcasted_iota(jnp.int32, (start, start), axis) < fine
    same = segment[...] == segment_row[...]
    return inside, same


def attend_kernel(scale, fine, start, query, key, value, segment, segment_row, mixed):
    rows = query.shape[0]
    masks = block_masks(fine, start, rows, segment, segment_row, 1)
    for here, mask in zip((slice(0, start), slice(start, rows)), masks):
        mixed[here, :] = attend_block(scale, query[here, :], key[here, :], value[here, :], mask)


def attend(qkv, segment, segment_row, fine, start):
    rows, width = qkv.shape
    heads = width // 3 // PAIR
    kernel = functools.partial(attend_kernel, 1.0 / math.sqrt(HD), fine, start)
    column = lambda k: pl.BlockSpec((rows, PAIR), lambda j: (0, k * heads + j))
    return pl.pallas_call(
        kernel,
        grid=(heads,),
        out_shape=jax.ShapeDtypeStruct((rows, width // 3), jnp.bfloat16),
        in_specs=[
            column(0),
            column(1),
            column(2),
            pl.BlockSpec((rows - start, 1), lambda j: (0, 0)),
            pl.BlockSpec((1, rows - start), lambda j: (0, 0)),
        ],
        out_specs=column(0),
        compiler_params=pltpu.CompilerParams(vmem_limit_bytes=48 << 20),
        name="attend",
    )(qkv, qkv, qkv, segment, segment_row)


def attend_back_block(scale, query, key, value, grad_mixed, mask):
    halves = pair_halves(query.shape[0])
    grad_query, grad_key, grad_value = [], 0.0, 0.0
    for h in range(2):
        own = jnp.where(halves[h], query, jnp.zeros_like(query))
        grad = jnp.where(halves[h], grad_mixed, jnp.zeros_like(grad_mixed))
        scores = jnp.where(mask, nt(key, own) * scale, -1000000000.0)
        weights = jnp.exp(scores - jnp.max(scores, axis=0, keepdims=True))
        probs = weights * (1.0 / jnp.sum(weights, axis=0, keepdims=True))
        grad_probs = nt(value, grad)
        inner = jnp.sum(probs * grad_probs, axis=0, keepdims=True)
        grad_scores = (probs * (grad_probs - inner)).astype(jnp.bfloat16)
        grad_value = grad_value + nn(probs.astype(jnp.bfloat16), grad)
        grad_key = grad_key + nn(grad_scores, own)
        grad_query.append(tn(grad_scores, key))
    grad_query = jnp.where(halves[0], grad_query[0], grad_query[1])
    return grad_query * scale, grad_key * scale, grad_value


LINE = 4
MESH_ID = pl.DeviceIdType.MESH
PIECE_ROWS = 192
PIECE_COLS = 384
CROSS_EVERY = 3
SEMS = 48


class Piece:
    def __init__(self, source, row, col, rows, cols, target, out_row, out_col, swap, cross):
        self.source, self.row, self.col, self.rows, self.cols = source, row, col, rows, cols
        self.target, self.out_row, self.out_col = target, out_row, out_col
        self.swap, self.cross = swap, cross


def move_pieces(pieces, scale, grads, outs, acc, land, land_right, land_left, sems, prepare):
    device = lax.axis_index("dp")
    core = lax.axis_index("tensor")
    place_x = lax.rem(device, 2)
    place_y = lax.rem(device // 2, 2)
    place_z = lax.rem(device // 4, LINE)
    mirror = LINE - 1 - place_z
    beside_x = (device + 1 - 2 * place_x, core)
    beside_y = (device + 2 - 4 * place_y, core)
    sibling = (device, 1 - core)
    up = (device + 4, core)
    down = (device - 4, core)

    barrier = pltpu.get_barrier_semaphore()
    for partner in (beside_x, beside_y, sibling):
        pl.semaphore_signal(barrier, inc=1, device_id=partner, device_id_type=MESH_ID)

    @pl.when(place_z < LINE - 1)
    def _():
        pl.semaphore_signal(barrier, inc=1, device_id=up, device_id_type=MESH_ID)

    @pl.when(place_z > 0)
    def _():
        pl.semaphore_signal(barrier, inc=1, device_id=down, device_id_type=MESH_ID)

    inner = (place_z + LINE - 1) // LINE + (2 * (LINE - 1) - place_z) // LINE
    pl.semaphore_wait(barrier, 3 + inner)

    def remote(src, dst, send, recv, where):
        return pltpu.make_async_remote_copy(
            src_ref=src,
            dst_ref=dst,
            send_sem=send,
            recv_sem=recv,
            device_id=where,
            device_id_type=MESH_ID,
        )

    work = prepare(core, place_x, sibling, remote)

    def rows_at(ref, start, size, column, width):
        return ref.at[pl.ds(pl.multiple_of(start, 8), size), pl.ds(pl.multiple_of(column, 128), width)]

    def add_rows(total, start, extra, size, width, factor=None):
        step = 24 if size % 24 == 0 else 8

        @pl.loop(0, size // step)
        def _(i):
            here = pl.ds(pl.multiple_of(start + i * step, 8), step)
            there = pl.ds(pl.multiple_of(i * step, 8), step)
            value = total[here, :width] + extra[there, :width]
            total[here, :width] = value if factor is None else value * factor

    def build(number, piece):
        half, chunk, width = piece.rows // 2, piece.rows // 8, piece.cols
        grad, out = grads[piece.source], outs[piece.target]
        mine = acc.at[number]
        sem = lambda k: sems.at[number, k]

        def out_at(x, owner, row, size):
            return rows_at(out, piece.out_row(x, owner) + row, size, piece.out_col(x), width)

        def y_copy():
            return remote(
                rows_at(grad, piece.row(place_x) + (1 - place_y) * half, half, piece.col, width),
                land.at[number, :half, :width],
                sem(0),
                sem(1),
                beside_y,
            )

        def load():
            return pltpu.make_async_copy(
                rows_at(grad, piece.row(place_x) + place_y * half, half, piece.col, width),
                mine.at[:half, :width],
                sem(2),
            )

        def right(k):
            return remote(
                rows_at(mine, (LINE - k + place_z) * chunk, chunk, 0, width),
                land_right.at[number, k - 1, :chunk, :width],
                sem(2 + k),
                sem(5 + k),
                up,
            )

        def left(k):
            return remote(
                rows_at(mine, (k - 1 - mirror) * chunk, chunk, 0, width),
                land_left.at[number, k - 1, :chunk, :width],
                sem(8 + k),
                sem(11 + k),
                down,
            )

        def got(slots, k, first, where):
            here = slots.at[number, k - 1, :chunk, :width]
            return remote(here, here, sem(first + k), sem(first + 3 + k), where)

        def send_line(k):
            @pl.when((place_z <= k - 1) & (place_z < LINE - 1))
            def _():
                right(k).start()

            @pl.when((mirror <= k - 1) & (mirror < LINE - 1))
            def _():
                left(k).start()

        def wait_line(k):
            @pl.when((place_z >= 1) & (place_z <= k))
            def _():
                got(land_right, k, 2, down).wait_recv()
                add_rows(
                    mine, (LINE - 1 - k + place_z) * chunk, land_right.at[number, k - 1], chunk, width
                )

            @pl.when((mirror >= 1) & (mirror <= k))
            def _():
                got(land_left, k, 8, up).wait_recv()
                add_rows(mine, (k - mirror) * chunk, land_left.at[number, k - 1], chunk, width)

        def own_chunk():
            return rows_at(mine, place_z * chunk, chunk, 0, width)

        def store():
            return pltpu.make_async_copy(
                own_chunk(), out_at(place_x, core, place_y * half + place_z * chunk, chunk), sem(17)
            )

        def share_out():
            return remote(
                own_chunk(),
                out_at(place_x, core, place_y * half + place_z * chunk, chunk),
                sem(15),
                sem(16),
                beside_x if piece.cross else beside_y,
            )

        def share_in():
            if piece.cross:
                there = out_at(1 - place_x, core, place_y * half + place_z * chunk, chunk)
                return remote(there, there, sem(15), sem(16), beside_x)
            there = out_at(place_x, core, (1 - place_y) * half + place_z * chunk, chunk)
            return remote(there, there, sem(15), sem(16), beside_y)

        def spread(k, position, where, first):
            copies = []
            for b in range(2):
                if piece.cross:
                    here = out_at(b, core, place_y * half + position * chunk, chunk)
                else:
                    here = out_at(place_x, core, b * half + position * chunk, chunk)
                at = first + 2 * (k - 1) + b
                copies.append(remote(here, here, sem(at), sem(at + 6), where))
            return copies

        def send_spread(k):
            @pl.when((place_z >= k - 1) & (place_z < LINE - 1))
            def _():
                for copy in spread(k, place_z - (k - 1), up, 18):
                    copy.start()

            @pl.when((mirror >= k - 1) & (mirror < LINE - 1))
            def _():
                for copy in spread(k, place_z + (k - 1), down, 30):
                    copy.start()

        def wait_spread(k):
            @pl.when(place_z >= k)
            def _():
                for copy in spread(k, place_z - k, down, 18):
                    copy.wait_recv()

            @pl.when(mirror >= k)
            def _():
                for copy in spread(k, place_z + k, up, 30):
                    copy.wait_recv()

        def last(outgoing):
            if piece.cross:
                row = (place_y if outgoing else 1 - place_y) * half
                views = [out_at(b, core, row, half) for b in range(2)]
                return [
                    remote(v, v, sem(42 + b), sem(44 + b), beside_y) for b, v in enumerate(views)
                ]
            view = out_at(place_x if outgoing else 1 - place_x, core, 0, piece.rows)
            return [remote(view, view, sem(42), sem(44), beside_x)]

        def swap(owner):
            views = [out_at(b, owner, 0, piece.rows) for b in range(2)]
            return [remote(v, v, sem(46 + b), sem(48 + b), sibling) for b, v in enumerate(views)]

        def stage_0():
            y_copy().start()
            load().start()

        def stage_1():
            load().wait()
            y_copy().wait_recv()
            add_rows(mine, 0, land.at[number], half, width)
            send_line(1)

        def stage_2():
            wait_line(1)
            send_line(2)

        def stage_3():
            wait_line(2)
            send_line(3)

        def stage_4():
            wait_line(3)

            @pl.loop(0, chunk // 8)
            def _(i):
                here = pl.ds(pl.multiple_of(place_z * chunk + i * 8, 8), 8)
                mine[here, :width] = mine[here, :width] * scale

            share_out().start()
            store().start()

        def stage_5():
            store().wait()
            share_in().wait_recv()
            send_spread(1)

        def stage_6():
            wait_spread(1)
            send_spread(2)

        def stage_7():
            wait_spread(2)
            send_spread(3)

        def stage_8():
            wait_spread(3)
            for copy in last(True):
                copy.start()

        def stage_9():
            for copy in last(False):
                copy.wait_recv()
            if piece.swap:
                for copy in swap(core):
                    copy.start()

        def stage_10():
            if piece.swap:
                for copy in swap(1 - core):
                    copy.wait_recv()
                for copy in swap(core):
                    copy.wait_send()
            y_copy().wait_send()
            share_out().wait_send()
            for copy in last(True):
                copy.wait_send()
            for k in range(1, LINE):

                @pl.when((place_z <= k - 1) & (place_z < LINE - 1))
                def _():
                    right(k).wait_send()

                @pl.when((mirror <= k - 1) & (mirror < LINE - 1))
                def _():
                    left(k).wait_send()

                @pl.when((place_z >= k - 1) & (place_z < LINE - 1))
                def _():
                    for copy in spread(k, place_z - (k - 1), up, 18):
                        copy.wait_send()

                @pl.when((mirror >= k - 1) & (mirror < LINE - 1))
                def _():
                    for copy in spread(k, place_z + (k - 1), down, 30):
                        copy.wait_send()

        return [
            stage_0,
            stage_1,
            stage_2,
            stage_3,
            stage_4,
            stage_5,
            stage_6,
            stage_7,
            stage_8,
            stage_9,
            stage_10,
        ]

    lines = [build(number, piece) for number, piece in enumerate(pieces)]
    groups = [lines[i : i + GROUP] for i in range(0, len(lines), GROUP)]
    depth = len(lines[0])
    for j in range(min(AHEAD, len(groups))):
        for line in groups[j]:
            line[0]()
    late = depth - 2
    for tick in range(len(groups) + depth - 1):
        if tick + AHEAD < len(groups):
            for line in groups[tick + AHEAD]:
                line[0]()
        for job in work.pop(0) if work else ():
            job()
        active = range(max(0, tick - depth + 1), min(tick, len(groups)))
        for j in [j for j in active if tick - j < late] + [j for j in active if tick - j >= late]:
            for line in groups[j]:
                line[tick - j]()


GROUP = 2
AHEAD = 1


def sync_plan(grads, outs):
    pieces = []
    for source, (rows, cols, step_x) in enumerate(grads):
        start = 0
        for target, width, row_x, row_core, col_x, out_start in outs[source]:
            tall = min(PIECE_ROWS, rows)
            wide = min(PIECE_COLS, width)
            if width % wide:
                wide = width // 2
            for row in range(0, rows, tall):
                for col in range(0, width, wide):
                    pieces.append(
                        Piece(
                            source,
                            lambda x, row=row, a=step_x: row + x * a,
                            start + col,
                            tall,
                            wide,
                            target,
                            lambda x, core, row=row, a=row_x, b=row_core: row + x * a + core * b,
                            lambda x, c=out_start + col, a=col_x: c + x * a,
                            row_core != 0,
                            len(pieces) % CROSS_EVERY == CROSS_EVERY - 1,
                        )
                    )
            start += width
    return pieces


QUERY_BLOCK = 384
FIRST_TICKS = 8
LN_ROWS = 112
POINT_ROWS = 64


def back_kernel(pieces, sizes, fine, start, points, counts, *refs):
    replicas, given = counts
    (
        qkv,
        grad_mixed,
        segment,
        segment_row,
        normed_part,
        w_qkv,
        standard,
        inverse,
        grad_middle,
        gain,
        tokens,
        patches,
        fine_pairs,
        pos_fine,
        pos,
        rest,
    ) = refs[:16]
    early = refs[16 : 16 + given]
    refs = refs[16 + given :]
    outs, grad_embedded, refs = refs[:sizes], refs[sizes], refs[sizes + 1 :]
    (
        grad_qkv,
        grad_key,
        grad_value,
        partial,
        arrived,
        grad_w_qkv,
        grad_w_base,
        bundle,
        acc,
        land,
        land_right,
        land_left,
        sems,
        swap_sems,
        chunk_standard,
        chunk_middle,
        chunk_sems,
    ) = refs
    rows, width = standard.shape
    third = qkv.shape[1] // 3
    scale = 1.0 / math.sqrt(HD)
    low = lambda value: value.astype(jnp.bfloat16)
    blocks = range(0, rows, LN_ROWS)

    def prepare(core, place_x, sibling, remote):
        def back_rows(pair, here, keys, mask):
            column = lambda k: slice(k * third + pair * PAIR, k * third + (pair + 1) * PAIR)
            return attend_back_block(
                scale,
                qkv[here, column(0)],
                qkv[keys, column(1)],
                qkv[keys, column(2)],
                grad_mixed[here, column(0)],
                mask,
            )

        def store_qkv(pair, k, here, value):
            grad_qkv[here, k * third + pair * PAIR : k * third + (pair + 1) * PAIR] = low(value)

        def fine_job(pair, begin):
            def job():
                here = slice(begin, min(begin + QUERY_BLOCK, start))
                keys = slice(0, start)
                inside = lax.broadcasted_iota(jnp.int32, (start, here.stop - begin), 0) < fine
                grad_q, grad_k, grad_v = back_rows(pair, here, keys, inside)
                store_qkv(pair, 0, here, grad_q)
                if begin == 0:
                    grad_key[...] = grad_k
                    grad_value[...] = grad_v
                else:
                    grad_key[...] += grad_k
                    grad_value[...] += grad_v
                if here.stop == start:
                    store_qkv(pair, 1, keys, grad_key[...])
                    store_qkv(pair, 2, keys, grad_value[...])

            return job

        def coarse_job(pair):
            def job():
                here = slice(start, rows)
                same = segment[...] == segment_row[...]
                for k, value in enumerate(back_rows(pair, here, here, same)):
                    store_qkv(pair, k, here, value)

            return job

        def weight_job():
            grad_w_qkv[...] = tn(normed_part[...], grad_qkv[...])

        def partial_job():
            partial[...] = nt(grad_qkv[...], w_qkv[...])
            swap().start()

        def swap():
            return remote(partial, arrived, swap_sems.at[0], swap_sems.at[1], sibling)

        def chunk_copies(number):
            here = pl.ds(pl.multiple_of(number * LN_ROWS, 8), LN_ROWS)
            at = lax.rem(number, 2)
            return [
                pltpu.make_async_copy(standard.at[here], chunk_standard.at[at], chunk_sems.at[0, at]),
                pltpu.make_async_copy(
                    grad_middle.at[here], chunk_middle.at[at], chunk_sems.at[1, at]
                ),
            ]

        def norm_job():
            swap().wait()
            for copy in chunk_copies(0):
                copy.start()
            for k in range(3):
                bundle[points + k : points + k + 1, :] = jnp.zeros((1, width), jnp.float32)

            @pl.loop(0, len(blocks))
            def _(number):
                @pl.when(number + 1 < len(blocks))
                def _():
                    for copy in chunk_copies(number + 1):
                        copy.start()

                for copy in chunk_copies(number):
                    copy.wait()
                at = lax.rem(number, 2)
                here = pl.ds(pl.multiple_of(number * LN_ROWS, 16), LN_ROWS)
                grad = partial[here, :] + arrived[here, :]
                z = chunk_standard[at]
                up = grad * gain[...]
                mean = jnp.mean(up, axis=1, keepdims=True)
                along = jnp.mean(up * z, axis=1, keepdims=True)
                value = chunk_middle[at] + (up - mean - z * along) * inverse[here, :]
                grad_embedded[here, :] = value
                column = lambda v: jnp.sum(v, axis=0, keepdims=True)
                bundle[points : points + 1, :] += column(low(value).astype(jnp.float32))
                bundle[points + 1 : points + 2, :] += column(grad * z)
                bundle[points + 2 : points + 3, :] += column(grad)

        def base_job():
            half = grad_w_base.shape[0]
            channels = patches.shape[0]
            part = grad_w_base.shape[1] // channels
            area = 2 * part
            columns = pl.ds(pl.multiple_of(core * half, 128), half)
            stride = tokens.shape[1]
            some = low(grad_embedded[:fine, columns])
            wanted = fine_pairs[:, pl.ds(pl.multiple_of(place_x * part, 128), part)]
            for c in range(channels):
                gathered = low(tn(patches[c, :fine, :], some))
                total = tn(gathered, wanted)
                for k in range(3):
                    begin = start + k * stride
                    here = pl.ds(pl.multiple_of(c * area + place_x * part, 128), part)
                    total += tn(low(grad_embedded[begin : begin + stride, columns]), tokens[k, :, here])
                grad_w_base[:, c * part : (c + 1) * part] = total

        def bundle_job():
            gathered = tn(pos_fine[...], low(grad_embedded[:fine, :]))
            count = pos.shape[1]
            for k in range(3):
                begin = start + k * tokens.shape[1]
                gathered += tn(pos[k], low(grad_embedded[begin : begin + count, :]))
            bundle[:points, :] = gathered
            bundle[points + 3 : 2 * POINT_ROWS, :] = rest[points + 3 : 2 * POINT_ROWS, :]
            sums = jnp.sum(grad_qkv[...].astype(jnp.float32), axis=0, keepdims=True)
            bundle[points + 7 : points + 8, :third] = sums[:, :third]
            bundle[points + 7 : points + 8, third : 2 * third] = sums[:, 2 * third :]

        heads = []
        for pair in range(third // PAIR):
            heads += [fine_job(pair, begin) for begin in range(0, start, QUERY_BLOCK)]
            heads.append(coarse_job(pair))
        ticks = FIRST_TICKS
        parts = [heads[len(heads) * k // ticks : len(heads) * (k + 1) // ticks] for k in range(ticks)]
        parts[-1] = parts[-1] + [weight_job]
        return parts + [[partial_job], [norm_job], [base_job], [bundle_job]]

    move_pieces(
        pieces,
        1.0 / replicas,
        list(early) + [grad_w_qkv, grad_w_base, bundle],
        outs,
        acc,
        land,
        land_right,
        land_left,
        sems,
        prepare,
    )


def back_and_sync(
    qkv,
    grad_mixed,
    segment,
    segment_row,
    normed_part,
    w_qkv,
    standard,
    inverse,
    grad_middle,
    gain,
    tokens,
    patches,
    fine_pairs,
    pos_fine,
    pos,
    rest,
    early,
    out_shapes,
    grads,
    outs,
    fine,
    start,
    replicas,
):
    rows, width = standard.shape
    channels = patches.shape[0]
    pieces = sync_plan(grads, outs)
    count = len(pieces)
    high = max(p.rows for p in pieces)
    wide = max(p.cols for p in pieces)
    points = pos.shape[2]
    kernel = functools.partial(
        back_kernel, pieces, len(out_shapes), fine, start, points, (replicas, len(early))
    )
    f32 = lambda *dims: pltpu.VMEM(dims, jnp.float32)
    anywhere = pl.BlockSpec(memory_space=pl.ANY)
    results = pl.pallas_call(
        kernel,
        out_shape=[jax.ShapeDtypeStruct(s, jnp.float32) for s in out_shapes]
        + [jax.ShapeDtypeStruct((rows, width), jnp.float32)],
        in_specs=[VMEM] * 6
        + [anywhere, VMEM, anywhere]
        + [VMEM] * 7
        + [anywhere] * len(early),
        out_specs=[anywhere] * len(out_shapes) + [VMEM],
        scratch_shapes=[
            pltpu.VMEM(qkv.shape, jnp.bfloat16),
            f32(start, PAIR),
            f32(start, PAIR),
            f32(rows, width),
            f32(rows, width),
            f32(width // 2, qkv.shape[1]),
            f32(width // 2, channels * fine_pairs.shape[1] // 2),
            f32(2 * POINT_ROWS, width),
            f32(count, high // 2, wide),
            f32(count, high // 2, wide),
            f32(count, LINE - 1, high // 8, wide),
            f32(count, LINE - 1, high // 8, wide),
            pltpu.SemaphoreType.DMA((count, SEMS + 2)),
            pltpu.SemaphoreType.DMA((2,)),
            f32(2, LN_ROWS, width),
            f32(2, LN_ROWS, width),
            pltpu.SemaphoreType.DMA((2, 2)),
        ],
        compiler_params=pltpu.CompilerParams(
            collective_id=0, has_side_effects=True, vmem_limit_bytes=63 << 20
        ),
        name="back_and_sync",
    )(
        qkv,
        grad_mixed,
        segment,
        segment_row,
        normed_part,
        w_qkv,
        standard,
        inverse,
        grad_middle,
        gain,
        tokens,
        patches,
        fine_pairs,
        pos_fine,
        pos,
        rest,
        *early,
    )
    return results[:-1], results[-1]


def tensor_sum(partial):
    return partial + lax.ppermute(partial, "tensor", [(0, 1), (1, 0)])


def swap_cores(value):
    return lax.ppermute(value, "tensor", [(0, 1), (1, 0)])


def merged_rows(fine_rows, light_rows, second, counts, start, stride, rows):
    width = fine_rows.shape[1]
    keep = jnp.arange(stride, dtype=jnp.int32)[:, None]
    fine = fine_rows.shape[0]
    padded = jnp.pad(light_rows, ((0, stride), (0, 0)))
    third = padded[:stride]
    fourth = lax.dynamic_slice_in_dim(padded, counts[2], stride, axis=0)
    blocks = [
        jnp.pad(fine_rows, ((0, start - fine), (0, 0))),
        jnp.pad(second, ((0, stride - second.shape[0]), (0, 0))),
        jnp.where(keep < counts[2], third, 0.0),
        jnp.where(keep < counts[3], fourth, 0.0),
        jnp.zeros((rows - start - 3 * stride, width), fine_rows.dtype),
    ]
    return jnp.concatenate(blocks, axis=0)


def own_rows(merged, is_fine, counts, fine, start, stride, rows):
    width = merged.shape[1]
    coarse = counts[1]
    heavy = jnp.concatenate(
        [
            merged[:fine],
            merged[start : start + stride],
            jnp.zeros((rows - fine - stride, width), merged.dtype),
        ],
        axis=0,
    )
    row = jnp.arange(rows, dtype=jnp.int32)[:, None]
    third = jnp.pad(merged[start + stride : start + 2 * stride], ((0, rows - stride), (0, 0)))
    fourth = jnp.pad(merged[start + 2 * stride : start + 3 * stride], ((stride, rows), (0, 0)))
    fourth = lax.dynamic_slice_in_dim(fourth, stride - counts[2], rows, axis=0)
    light = jnp.where(row < counts[2], third, fourth)
    used = jnp.where(is_fine, fine + coarse, counts[2] + counts[3])
    return jnp.where(row < used, jnp.where(is_fine, heavy, light), jnp.zeros_like(heavy))


def local(
    pixels,
    patch_size,
    counts,
    offsets,
    resize_table,
    pos_table,
    w_base,
    patch_bias,
    pos_base,
    gain_one,
    shift_one,
    w_query,
    bias_query,
    w_key,
    w_value,
    bias_value,
    w_out,
    bias_out,
    gain_two,
    shift_two,
    w_up,
    bias_up,
    w_down,
    bias_down,
    cotangent,
):
    wide = lambda value: value.astype(jnp.float32)
    images, channels, res, _ = pixels.shape
    rows_total = cotangent.shape[0]
    replicas = lax.axis_size("dp")
    core = lax.axis_index("tensor")
    side_x = lax.rem(lax.axis_index("dp"), 2)
    fine = (res // FINE) ** 2
    small = (res // COARSE[0]) ** 2
    start = up_to(fine, 16)
    stride = up_to(small, 8)
    rows = up_to(start + 3 * stride, 16)

    there = [(i, i ^ 1) for i in range(replicas)]
    other_sizes = lax.ppermute(patch_size, "dp", there)
    own_pix = jnp.pad(wide(pixels), ((0, 0), (0, 0), (0, 0), (0, -res % 128)))
    direct = lax.ppermute(
        lax.dynamic_index_in_dim(own_pix, core, 0, keepdims=False), "dp", there
    )
    half_rows = rows_total // 2
    own_cotangent = wide(cotangent)
    cot_half = lax.dynamic_slice_in_dim(own_cotangent, core * half_rows, half_rows, axis=0)
    w_qkv = jnp.concatenate([w_query, w_key, w_value], axis=1)
    bias_qkv = jnp.concatenate([bias_query, jnp.zeros_like(bias_query), bias_value])
    pos_fine = pos_table[res // FINE, :fine]
    pos_coarse = pos_table[:, :stride]
    direct, other_sizes, cot_half, w_qkv, bias_qkv, pos_fine, pos_coarse = (
        lax.optimization_barrier(
            (direct, other_sizes, cot_half, w_qkv, bias_qkv, pos_fine, pos_coarse)
        )
    )
    across = swap_cores(direct)
    cot_direct = lax.ppermute(cot_half, "dp", there)
    is_fine = patch_size[0] == FINE
    fine_first = is_fine.astype(jnp.int32)
    sizes = jnp.where(
        is_fine,
        jnp.concatenate([patch_size, other_sizes]),
        jnp.concatenate([other_sizes, patch_size]),
    )
    slots = jnp.stack([0 * core, 0 * core + 1, core, 1 - core]) + 2 * jnp.stack(
        [1 - fine_first] * 2 + [fine_first] * 2
    )
    counts4 = (res // sizes) ** 2
    (
        embedded,
        standard_one,
        inverse_one,
        normed_one,
        tokens,
        patches,
        mixed_weight,
        fine_pairs,
        pos,
        segment,
        segment_row,
    ) = embed(
        sizes,
        slots,
        resize_table,
        pos_fine,
        pos_coarse,
        w_base,
        [wide(patch_bias)[None], wide(gain_one)[None], wide(shift_one)[None]],
        pos_base,
        [own_pix, direct, across],
        rows,
    )
    qkv = (
        jnp.dot(normed_one, w_qkv, preferred_element_type=jnp.float32) + wide(bias_qkv)
    ).astype(jnp.bfloat16)
    qkv, cot_direct = lax.optimization_barrier((qkv, cot_direct))
    cot_across = swap_cores(cot_direct)
    mixed = attend(qkv, segment, segment_row, fine, start)
    attended = tensor_sum(jnp.dot(mixed, w_out, preferred_element_type=jnp.float32)) + wide(
        bias_out
    )
    middle = embedded + attended
    standard_two, standard_back_two = jax.vjp(standardize, middle)
    normed_two = (standard_two * wide(gain_two) + wide(shift_two)).astype(jnp.bfloat16)
    hidden = jnp.dot(normed_two, w_up, preferred_element_type=jnp.float32) + wide(bias_up)
    activated_wide, gelu_back = jax.vjp(jax.nn.gelu, hidden)
    activated = activated_wide.astype(jnp.bfloat16)
    branch = tensor_sum(jnp.dot(activated, w_down, preferred_element_type=jnp.float32)) + wide(
        bias_down
    )
    output = own_rows(
        (middle + branch).astype(jnp.bfloat16), is_fine, counts4, fine, start, stride, rows_total
    )
    other_cotangent = jnp.where(
        core == 0,
        jnp.concatenate([cot_direct, cot_across]),
        jnp.concatenate([cot_across, cot_direct]),
    )
    fine_cotangent = jnp.where(is_fine, own_cotangent, other_cotangent)
    light_cotangent = jnp.where(
        is_fine, other_cotangent[: 2 * stride], own_cotangent[: 2 * stride]
    )
    grad_out = (
        merged_rows(
            fine_cotangent[:fine],
            light_cotangent,
            fine_cotangent[fine : fine + small],
            counts4,
            start,
            stride,
            rows,
        )
    )
    grad_branch = grad_out.astype(jnp.bfloat16)
    own_part = lambda value: lax.dynamic_slice_in_dim(
        value, side_x * (value.shape[1] // 2), value.shape[1] // 2, axis=1
    )
    grad_w_down = jnp.einsum(
        "tf,td->fd", own_part(activated), grad_branch, preferred_element_type=jnp.float32
    )
    grad_activated = jnp.einsum(
        "td,fd->tf", grad_branch, w_down, preferred_element_type=jnp.float32
    )
    grad_hidden = gelu_back(grad_activated)[0].astype(jnp.bfloat16)
    grad_w_up = jnp.einsum(
        "td,tf->df", own_part(normed_two), grad_hidden, preferred_element_type=jnp.float32
    )
    grad_bias_up = jnp.sum(grad_hidden, axis=0, dtype=jnp.float32)
    grad_normed_two = tensor_sum(
        jnp.einsum("tf,df->td", grad_hidden, w_up, preferred_element_type=jnp.float32)
    )
    grad_middle = grad_out + standard_back_two(grad_normed_two * wide(gain_two))[0]
    grad_attended = grad_middle.astype(jnp.bfloat16)
    grad_w_out = jnp.einsum(
        "te,td->ed", own_part(mixed), grad_attended, preferred_element_type=jnp.float32
    )
    grad_mixed = jnp.einsum(
        "td,ed->te", grad_attended, w_out, preferred_element_type=jnp.float32
    ).astype(jnp.bfloat16)
    points = pos.shape[2]
    width = grad_attended.shape[1]
    bundle = jnp.concatenate(
        [
            jnp.zeros((points + 3, width), jnp.float32),
            jnp.sum(grad_attended, axis=0, dtype=jnp.float32)[None],
            jnp.sum(grad_normed_two * standard_two, axis=0)[None],
            jnp.sum(grad_normed_two, axis=0)[None],
            jnp.sum(grad_branch, axis=0, dtype=jnp.float32)[None],
            jnp.zeros((1, width), jnp.float32),
            grad_bias_up.reshape(-1, width),
        ],
        axis=0,
    )
    used = bundle.shape[0]
    bundle = jnp.pad(bundle, ((0, 2 * POINT_ROWS - used), (0, 0)))
    early = [grad_w_down, grad_w_up, grad_w_out]
    area = w_base.shape[1] // channels
    ff = w_down.shape[0]
    deep = w_up.shape[0]
    cut = bias_query.shape[0]
    out_shapes = [
        w_base.shape,
        w_down.shape,
        w_up.shape,
        w_query.shape,
        w_key.shape,
        w_value.shape,
        w_out.shape,
        bundle.shape,
    ]
    grads = [
        (ff // 2, width, 0),
        (deep // 2, ff, 0),
        (cut // 2, width, 0),
        (deep // 2, 3 * cut, 0),
        (width // 2, w_base.shape[1] // 2, 0),
        (POINT_ROWS, width, POINT_ROWS),
    ]
    outs = [
        [(1, width, ff // 2, 0, 0, 0)],
        [(2, ff, deep // 2, 0, 0, 0)],
        [(6, width, cut // 2, 0, 0, 0)],
        [(3 + k, cut, deep // 2, 0, 0, 0) for k in range(3)],
        [(0, area // 2, 0, width // 2, area // 2, area * c) for c in range(channels)],
        [(7, width, POINT_ROWS, 0, 0, 0)],
    ]
    synced, grad_embedded = back_and_sync(
        qkv,
        grad_mixed,
        segment,
        segment_row,
        own_part(normed_one),
        w_qkv,
        standard_one,
        inverse_one,
        grad_middle,
        wide(gain_one)[None],
        tokens,
        patches,
        fine_pairs,
        pos_fine,
        pos,
        bundle,
        early,
        out_shapes,
        grads,
        outs,
        fine,
        start,
        replicas,
    )
    beyond = replicas // 16
    step = 1
    while step < beyond:
        swap = [(i, (i // 16 ^ step) * 16 + i % 16) for i in range(replicas)]
        synced = [part + lax.ppermute(part, "dp", swap) for part in synced]
        step *= 2
    pixel_grad = pixel_back(
        sizes,
        is_fine.astype(jnp.int32)[None],
        grad_embedded,
        resize_table,
        w_base,
        mixed_weight,
        pixels.shape,
    )
    base_s, down_s, up_s, query_s, key_s, value_s, out_s, small_s = synced
    line = lambda k: small_s[points + k]
    return (
        output,
        pixel_grad,
        base_s,
        line(0),
        small_s[:points].T,
        line(1),
        line(2),
        query_s,
        line(7)[:cut],
        key_s,
        value_s,
        line(7)[cut:],
        out_s,
        line(3),
        line(4),
        line(5),
        up_s,
        small_s[points + 8 : used].reshape(-1),
        down_s,
        line(6),
    )


def solution(mesh):
    in_specs = (
        P("dp", None, None, None),
        P("dp"),
        P("dp"),
        P("dp"),
        P(),
        P(),
        P(),
        P(),
        P(),
        P(),
        P(),
        P(None, "tensor"),
        P("tensor"),
        P(None, "tensor"),
        P(None, "tensor"),
        P("tensor"),
        P("tensor", None),
        P(),
        P(),
        P(),
        P(None, "tensor"),
        P("tensor"),
        P("tensor", None),
        P(),
        P("dp", None),
    )
    out_specs = (
        P("dp", None),
        P("dp", None, None, None),
        P(),
        P(),
        P(),
        P(),
        P(),
        P(None, "tensor"),
        P("tensor"),
        P(None, "tensor"),
        P(None, "tensor"),
        P("tensor"),
        P("tensor", None),
        P(),
        P(),
        P(),
        P(None, "tensor"),
        P("tensor"),
        P("tensor", None),
        P(),
    )
    return jax.shard_map(local, mesh=mesh, in_specs=in_specs, out_specs=out_specs, check_vma=False)
```

```python
import functools
import math

import jax
import jax.numpy as jnp
from jax import lax
from jax.experimental import pallas as pl
from jax.experimental.pallas import tpu as pltpu
from jax.sharding import PartitionSpec as P

HD = 64
VMEM = pl.BlockSpec(memory_space=pltpu.VMEM)
SMEM = pl.BlockSpec(memory_space=pltpu.SMEM)


def standardize(values):
    centered = values - jnp.mean(values, axis=-1, keepdims=True)
    spread = jnp.mean(centered * centered, axis=-1, keepdims=True)
    return centered * lax.rsqrt(spread + 1e-06)


FINE = 8
COARSE = (24, 30, 40, 48)
NORM_ROWS = 112


def nt(left, right):
    return lax.dot_general(left, right, (((1,), (1,)), ((), ())), preferred_element_type=jnp.float32)


def tn(left, right):
    return lax.dot_general(left, right, (((0,), (0,)), ((), ())), preferred_element_type=jnp.float32)


def nn(left, right):
    return jnp.dot(left, right, preferred_element_type=jnp.float32)


def up_to(value, step):
    return value + -value % step


def loop(count, body, unroll):
    if unroll:
        for i in range(count):
            body(i)
    else:
        pl.loop(0, count)(body)


def aligned(start, side):
    return pl.multiple_of(start, 8) if side % 8 == 0 and not isinstance(start, int) else start


def fill_pairs(pair, long, table, side):
    base = table.shape[1]
    entry = lax.broadcasted_iota(jnp.int32, (base, base * base), 0)
    place = lax.broadcasted_iota(jnp.int32, (base, base * base), 1)
    repeat = (place // base == entry).astype(jnp.bfloat16)
    tile = (place % base == entry).astype(jnp.bfloat16)
    wide = nn(table, repeat)[:side]
    long[...] = nn(table, tile)

    def one(s):
        pair[pl.ds(aligned(s * side, side), side), :] = wide * long[pl.ds(s, 1), :]

    loop(side, one, side % 8 != 0)


def cut_patches(line, pix, image, channel, side, grid, res):
    def one(x):
        block = pix[image, channel, pl.ds(aligned(x * side, side), side), :]
        line[pl.ds(aligned(x * res, 8), res), :side] = block.T[:res]

    loop(grid, one, True)
    return jnp.concatenate(
        [line[pl.ds(s, grid * grid, stride=side), :side] for s in range(side)], axis=1
    ).astype(jnp.bfloat16)


def place_patches(line, pixel_grad, image, channel, patch, side, grid, res):
    for s in range(side):
        line[pl.ds(s, grid * grid, stride=side), :side] = patch[:, s * side : (s + 1) * side]

    def one(x):
        block = line[pl.ds(aligned(x * res, 8), res), :side]
        pixel_grad[image, channel, pl.ds(aligned(x * side, side), side), :] = block.T

    loop(grid, one, True)


def embed_kernel(
    sizes,
    slots,
    table,
    pos_fine,
    pos_all,
    weight,
    bias,
    pos_base,
    gain,
    shift,
    own,
    direct,
    across,
    emb,
    standard,
    inverse,
    normed,
    tokens,
    patches,
    mixed_weight,
    fine_pairs,
    pos,
    segment,
    segment_row,
    pix,
    line,
    pair,
    long,
    sems,
):
    area = table.shape[2] ** 2
    channels, res = pix.shape[1:3]
    grid = res // FINE
    count = grid * grid
    start = up_to(count, 16)
    stride = tokens.shape[1]
    low = jnp.bfloat16
    copies = [
        pltpu.make_async_copy(source, pix.at[slots[k]], sems.at[k])
        for k, source in enumerate((own.at[0], own.at[1], direct, across))
    ]
    for copy in copies:
        copy.start()
    emb[...] = jnp.broadcast_to(bias[...], emb.shape)
    tokens[...] = jnp.zeros_like(tokens)
    fill_pairs(pair, long, table[FINE], FINE)
    fine_pairs[...] = pair[: FINE * FINE, :].astype(low)
    emb[:count, :] += nt(pos_fine[...], pos_base[...])
    for target, axis in ((segment, 0), (segment_row, 1)):
        row = lax.broadcasted_iota(jnp.int32, target.shape, axis)
        found = jnp.full(target.shape, 4, jnp.int32)
        for k in range(1, 4):
            side = res // sizes[k]
            within = row - (k - 1) * stride
            found = jnp.where((within >= 0) & (within < side * side), k, found)
        target[...] = found
    for copy in copies:
        copy.wait()

    for c in range(channels):
        columns = slice(c * area, (c + 1) * area)
        patch = cut_patches(line, pix, 0, c, FINE, grid, res)
        mixed = nt(fine_pairs[...], weight[:, columns]).astype(low)
        mixed_weight[c] = mixed
        patches[c, :count, :] = patch
        emb[:count, :] += nn(patch, mixed)

    @pl.loop(1, 4)
    def _(slot):
        row = pl.multiple_of(start + (slot - 1) * stride, 8)
        for side in COARSE:
            grid = res // side
            count = grid * grid

            @pl.when(sizes[slot] == side)
            def _():
                fill_pairs(pair, long, table[side], side)
                here = pl.ds(row, count)
                pos[slot - 1] = pos_all[grid]
                emb[here, :] += nt(pos_all[grid, :count, :], pos_base[...])
                for c in range(channels):
                    columns = slice(c * area, (c + 1) * area)
                    patch = cut_patches(line, pix, slot, c, side, grid, res)
                    token = nn(patch, pair[: side * side, :].astype(low)).astype(low)
                    tokens[slot - 1, :count, columns] = token
                    emb[here, :] += nt(token, weight[:, columns])

    @pl.loop(0, emb.shape[0] // NORM_ROWS)
    def _(i):
        here = pl.ds(pl.multiple_of(i * NORM_ROWS, 16), NORM_ROWS)
        value = emb[here, :]
        centered = value - jnp.mean(value, axis=1, keepdims=True)
        scale = lax.rsqrt(jnp.mean(centered * centered, axis=1, keepdims=True) + 1e-06)
        standard[here, :] = centered * scale
        inverse[here, :] = scale
        normed[here, :] = (centered * scale * gain[...] + shift[...]).astype(low)


def embed(sizes, slots, table, pos_fine, pos_all, w_base, rows_of, pos_base, pixels, rows):
    own = pixels[0]
    _, channels, res, lanes = own.shape
    width, features = w_base.shape
    fine = (res // FINE) ** 2
    side = table.shape[1]
    area = features // channels
    stride = pos_all.shape[1]
    rest = rows - up_to(fine, 16)
    shape = jax.ShapeDtypeStruct
    return pl.pallas_call(
        embed_kernel,
        out_shape=[
            shape((rows, width), jnp.float32),
            shape((rows, width), jnp.float32),
            shape((rows, 1), jnp.float32),
            shape((rows, width), jnp.bfloat16),
            shape((3, stride, features), jnp.bfloat16),
            shape((channels, up_to(fine, 16), FINE * FINE), jnp.bfloat16),
            shape((channels, FINE * FINE, width), jnp.bfloat16),
            shape((FINE * FINE, area), jnp.bfloat16),
            shape((3,) + pos_all.shape[1:], jnp.bfloat16),
            shape((rest, 1), jnp.int32),
            shape((1, rest), jnp.int32),
        ],
        in_specs=[SMEM] * 2 + [VMEM] * 8 + [pl.BlockSpec(memory_space=pl.ANY)] * 3,
        out_specs=[VMEM] * 11,
        scratch_shapes=[
            pltpu.VMEM((4, channels, res, lanes), jnp.float32),
            pltpu.VMEM((res * res // FINE, 128), jnp.float32),
            pltpu.VMEM((side * side, area), jnp.float32),
            pltpu.VMEM((side, area), jnp.float32),
            pltpu.SemaphoreType.DMA((4,)),
        ],
        compiler_params=pltpu.CompilerParams(vmem_limit_bytes=56 << 20),
        name="embed",
    )(sizes, slots, table, pos_fine, pos_all, w_base, rows_of[0], pos_base, *rows_of[1:], *pixels)


def pixel_kernel(sizes, is_fine, grad, table, weight, mixed_weight, pixel_grad, line, pair, long):
    area = table.shape[2] ** 2
    channels, res = pixel_grad.shape[1:3]
    start = up_to((res // FINE) ** 2, 16)
    stride = up_to((res // COARSE[0]) ** 2, 8)
    low = jnp.bfloat16

    @pl.when(is_fine[0] == 1)
    def _():
        grid = res // FINE
        count = grid * grid
        for c in range(channels):
            patch = nt(grad[:count, :].astype(low), mixed_weight[c])
            place_patches(line, pixel_grad, 0, c, patch, FINE, grid, res)

    @pl.loop(1, 4)
    def _(slot):
        row = pl.multiple_of(start + (slot - 1) * stride, 8)
        wanted = jnp.where(slot == 1, is_fine[0], 1 - is_fine[0])
        image = jnp.where(slot == 1, 1, slot - 2)
        for side in COARSE:
            grid = res // side
            count = grid * grid

            @pl.when((sizes[slot] == side) & (wanted == 1))
            def _():
                fill_pairs(pair, long, table[side], side)
                rows = grad[pl.ds(row, count), :].astype(low)

                @pl.loop(0, channels)
                def _(c):
                    columns = pl.ds(pl.multiple_of(c * area, area), area)
                    token = nn(rows, weight[:, columns]).astype(low)
                    patch = nt(token, pair[: side * side, :].astype(low))
                    place_patches(line, pixel_grad, image, c, patch, side, grid, res)


def pixel_back(sizes, is_fine, grad, table, w_base, mixed_weight, shape):
    _, channels, res, _ = shape
    width, features = w_base.shape
    side = table.shape[1]
    return pl.pallas_call(
        pixel_kernel,
        out_shape=jax.ShapeDtypeStruct(shape, jnp.float32),
        in_specs=[SMEM] * 2 + [VMEM] * 4,
        out_specs=VMEM,
        scratch_shapes=[
            pltpu.VMEM((res * res // FINE, 128), jnp.float32),
            pltpu.VMEM((side * side, features // channels), jnp.float32),
            pltpu.VMEM((side, features // channels), jnp.float32),
        ],
        compiler_params=pltpu.CompilerParams(vmem_limit_bytes=40 << 20),
        name="pixel_back",
    )(sizes, is_fine, grad, table, w_base, mixed_weight)


PAIR = 2 * HD


def pair_halves(rows):
    lane = lax.broadcasted_iota(jnp.int32, (rows, PAIR), 1)
    return [lane < HD, lane >= HD]


def attend_block(scale, query, key, value, mask):
    halves = pair_halves(query.shape[0])
    both = []
    for h in range(2):
        own = jnp.where(halves[h], query, jnp.zeros_like(query))
        scores = jnp.where(mask, nt(own, key) * scale, -1000000000.0)
        weights = jnp.exp(scores - jnp.max(scores, axis=1, keepdims=True))
        inverse = 1.0 / jnp.sum(weights, axis=1, keepdims=True)
        both.append(nn((weights * inverse).astype(jnp.bfloat16), value))
    return jnp.where(halves[0], both[0], both[1]).astype(jnp.bfloat16)


def block_masks(fine, start, rows, segment, segment_row, axis):
    inside = lax.broadcasted_iota(jnp.int32, (start, start), axis) < fine
    same = segment[...] == segment_row[...]
    return inside, same


def attend_kernel(scale, fine, start, query, key, value, segment, segment_row, mixed):
    rows = query.shape[0]
    masks = block_masks(fine, start, rows, segment, segment_row, 1)
    for here, mask in zip((slice(0, start), slice(start, rows)), masks):
        mixed[here, :] = attend_block(scale, query[here, :], key[here, :], value[here, :], mask)


def attend(qkv, segment, segment_row, fine, start):
    rows, width = qkv.shape
    heads = width // 3 // PAIR
    kernel = functools.partial(attend_kernel, 1.0 / math.sqrt(HD), fine, start)
    column = lambda k: pl.BlockSpec((rows, PAIR), lambda j: (0, k * heads + j))
    return pl.pallas_call(
        kernel,
        grid=(heads,),
        out_shape=jax.ShapeDtypeStruct((rows, width // 3), jnp.bfloat16),
        in_specs=[
            column(0),
            column(1),
            column(2),
            pl.BlockSpec((rows - start, 1), lambda j: (0, 0)),
            pl.BlockSpec((1, rows - start), lambda j: (0, 0)),
        ],
        out_specs=column(0),
        compiler_params=pltpu.CompilerParams(vmem_limit_bytes=48 << 20),
        name="attend",
    )(qkv, qkv, qkv, segment, segment_row)


def attend_back_block(scale, query, key, value, grad_mixed, mask):
    halves = pair_halves(query.shape[0])
    grad_query, grad_key, grad_value = [], 0.0, 0.0
    for h in range(2):
        own = jnp.where(halves[h], query, jnp.zeros_like(query))
        grad = jnp.where(halves[h], grad_mixed, jnp.zeros_like(grad_mixed))
        scores = jnp.where(mask, nt(key, own) * scale, -1000000000.0)
        weights = jnp.exp(scores - jnp.max(scores, axis=0, keepdims=True))
        probs = weights * (1.0 / jnp.sum(weights, axis=0, keepdims=True))
        grad_probs = nt(value, grad)
        inner = jnp.sum(probs * grad_probs, axis=0, keepdims=True)
        grad_scores = (probs * (grad_probs - inner)).astype(jnp.bfloat16)
        grad_value = grad_value + nn(probs.astype(jnp.bfloat16), grad)
        grad_key = grad_key + nn(grad_scores, own)
        grad_query.append(tn(grad_scores, key))
    grad_query = jnp.where(halves[0], grad_query[0], grad_query[1])
    return grad_query * scale, grad_key * scale, grad_value


LINE = 4
MESH_ID = pl.DeviceIdType.MESH
PIECE_ROWS = 192
PIECE_COLS = 384
CROSS_EVERY = 3
SEMS = 48


class Piece:
    def __init__(self, source, row, col, rows, cols, target, out_row, out_col, swap, cross):
        self.source, self.row, self.col, self.rows, self.cols = source, row, col, rows, cols
        self.target, self.out_row, self.out_col = target, out_row, out_col
        self.swap, self.cross = swap, cross


def move_pieces(pieces, scale, grads, outs, acc, land, land_right, land_left, sems, prepare):
    device = lax.axis_index("dp")
    core = lax.axis_index("tensor")
    place_x = lax.rem(device, 2)
    place_y = lax.rem(device // 2, 2)
    place_z = lax.rem(device // 4, LINE)
    mirror = LINE - 1 - place_z
    beside_x = (device + 1 - 2 * place_x, core)
    beside_y = (device + 2 - 4 * place_y, core)
    sibling = (device, 1 - core)
    up = (device + 4, core)
    down = (device - 4, core)

    barrier = pltpu.get_barrier_semaphore()
    for partner in (beside_x, beside_y, sibling):
        pl.semaphore_signal(barrier, inc=1, device_id=partner, device_id_type=MESH_ID)

    @pl.when(place_z < LINE - 1)
    def _():
        pl.semaphore_signal(barrier, inc=1, device_id=up, device_id_type=MESH_ID)

    @pl.when(place_z > 0)
    def _():
        pl.semaphore_signal(barrier, inc=1, device_id=down, device_id_type=MESH_ID)

    inner = (place_z + LINE - 1) // LINE + (2 * (LINE - 1) - place_z) // LINE
    pl.semaphore_wait(barrier, 3 + inner)

    def remote(src, dst, send, recv, where):
        return pltpu.make_async_remote_copy(
            src_ref=src,
            dst_ref=dst,
            send_sem=send,
            recv_sem=recv,
            device_id=where,
            device_id_type=MESH_ID,
        )

    work = prepare(core, place_x, sibling, remote)

    def rows_at(ref, start, size, column, width):
        return ref.at[pl.ds(pl.multiple_of(start, 8), size), pl.ds(pl.multiple_of(column, 128), width)]

    def add_rows(total, start, extra, size, width, factor=None):
        step = 24 if size % 24 == 0 else 8

        @pl.loop(0, size // step)
        def _(i):
            here = pl.ds(pl.multiple_of(start + i * step, 8), step)
            there = pl.ds(pl.multiple_of(i * step, 8), step)
            value = total[here, :width] + extra[there, :width]
            total[here, :width] = value if factor is None else value * factor

    def build(number, piece):
        half, chunk, width = piece.rows // 2, piece.rows // 8, piece.cols
        grad, out = grads[piece.source], outs[piece.target]
        mine = acc.at[number]
        sem = lambda k: sems.at[number, k]

        def out_at(x, owner, row, size):
            return rows_at(out, piece.out_row(x, owner) + row, size, piece.out_col(x), width)

        def y_copy():
            return remote(
                rows_at(grad, piece.row(place_x) + (1 - place_y) * half, half, piece.col, width),
                land.at[number, :half, :width],
                sem(0),
                sem(1),
                beside_y,
            )

        def load():
            return pltpu.make_async_copy(
                rows_at(grad, piece.row(place_x) + place_y * half, half, piece.col, width),
                mine.at[:half, :width],
                sem(2),
            )

        def right(k):
            return remote(
                rows_at(mine, (LINE - k + place_z) * chunk, chunk, 0, width),
                land_right.at[number, k - 1, :chunk, :width],
                sem(2 + k),
                sem(5 + k),
                up,
            )

        def left(k):
            return remote(
                rows_at(mine, (k - 1 - mirror) * chunk, chunk, 0, width),
                land_left.at[number, k - 1, :chunk, :width],
                sem(8 + k),
                sem(11 + k),
                down,
            )

        def got(slots, k, first, where):
            here = slots.at[number, k - 1, :chunk, :width]
            return remote(here, here, sem(first + k), sem(first + 3 + k), where)

        def send_line(k):
            @pl.when((place_z <= k - 1) & (place_z < LINE - 1))
            def _():
                right(k).start()

            @pl.when((mirror <= k - 1) & (mirror < LINE - 1))
            def _():
                left(k).start()

        def wait_line(k):
            @pl.when((place_z >= 1) & (place_z <= k))
            def _():
                got(land_right, k, 2, down).wait_recv()
                add_rows(
                    mine, (LINE - 1 - k + place_z) * chunk, land_right.at[number, k - 1], chunk, width
                )

            @pl.when((mirror >= 1) & (mirror <= k))
            def _():
                got(land_left, k, 8, up).wait_recv()
                add_rows(mine, (k - mirror) * chunk, land_left.at[number, k - 1], chunk, width)

        def own_chunk():
            return rows_at(mine, place_z * chunk, chunk, 0, width)

        def store():
            return pltpu.make_async_copy(
                own_chunk(), out_at(place_x, core, place_y * half + place_z * chunk, chunk), sem(17)
            )

        def share_out():
            return remote(
                own_chunk(),
                out_at(place_x, core, place_y * half + place_z * chunk, chunk),
                sem(15),
                sem(16),
                beside_x if piece.cross else beside_y,
            )

        def share_in():
            if piece.cross:
                there = out_at(1 - place_x, core, place_y * half + place_z * chunk, chunk)
                return remote(there, there, sem(15), sem(16), beside_x)
            there = out_at(place_x, core, (1 - place_y) * half + place_z * chunk, chunk)
            return remote(there, there, sem(15), sem(16), beside_y)

        def spread(k, position, where, first):
            copies = []
            for b in range(2):
                if piece.cross:
                    here = out_at(b, core, place_y * half + position * chunk, chunk)
                else:
                    here = out_at(place_x, core, b * half + position * chunk, chunk)
                at = first + 2 * (k - 1) + b
                copies.append(remote(here, here, sem(at), sem(at + 6), where))
            return copies

        def send_spread(k):
            @pl.when((place_z >= k - 1) & (place_z < LINE - 1))
            def _():
                for copy in spread(k, place_z - (k - 1), up, 18):
                    copy.start()

            @pl.when((mirror >= k - 1) & (mirror < LINE - 1))
            def _():
                for copy in spread(k, place_z + (k - 1), down, 30):
                    copy.start()

        def wait_spread(k):
            @pl.when(place_z >= k)
            def _():
                for copy in spread(k, place_z - k, down, 18):
                    copy.wait_recv()

            @pl.when(mirror >= k)
            def _():
                for copy in spread(k, place_z + k, up, 30):
                    copy.wait_recv()

        def last(outgoing):
            if piece.cross:
                row = (place_y if outgoing else 1 - place_y) * half
                views = [out_at(b, core, row, half) for b in range(2)]
                return [
                    remote(v, v, sem(42 + b), sem(44 + b), beside_y) for b, v in enumerate(views)
                ]
            view = out_at(place_x if outgoing else 1 - place_x, core, 0, piece.rows)
            return [remote(view, view, sem(42), sem(44), beside_x)]

        def swap(owner):
            views = [out_at(b, owner, 0, piece.rows) for b in range(2)]
            return [remote(v, v, sem(46 + b), sem(48 + b), sibling) for b, v in enumerate(views)]

        def stage_0():
            y_copy().start()
            load().start()

        def stage_1():
            load().wait()
            y_copy().wait_recv()
            add_rows(mine, 0, land.at[number], half, width)
            send_line(1)

        def stage_2():
            wait_line(1)
            send_line(2)

        def stage_3():
            wait_line(2)
            send_line(3)

        def stage_4():
            wait_line(3)

            @pl.loop(0, chunk // 8)
            def _(i):
                here = pl.ds(pl.multiple_of(place_z * chunk + i * 8, 8), 8)
                mine[here, :width] = mine[here, :width] * scale

            share_out().start()
            store().start()

        def stage_5():
            store().wait()
            share_in().wait_recv()
            send_spread(1)

        def stage_6():
            wait_spread(1)
            send_spread(2)

        def stage_7():
            wait_spread(2)
            send_spread(3)

        def stage_8():
            wait_spread(3)
            for copy in last(True):
                copy.start()

        def stage_9():
            for copy in last(False):
                copy.wait_recv()
            if piece.swap:
                for copy in swap(core):
                    copy.start()

        def stage_10():
            if piece.swap:
                for copy in swap(1 - core):
                    copy.wait_recv()
                for copy in swap(core):
                    copy.wait_send()
            y_copy().wait_send()
            share_out().wait_send()
            for copy in last(True):
                copy.wait_send()
            for k in range(1, LINE):

                @pl.when((place_z <= k - 1) & (place_z < LINE - 1))
                def _():
                    right(k).wait_send()

                @pl.when((mirror <= k - 1) & (mirror < LINE - 1))
                def _():
                    left(k).wait_send()

                @pl.when((place_z >= k - 1) & (place_z < LINE - 1))
                def _():
                    for copy in spread(k, place_z - (k - 1), up, 18):
                        copy.wait_send()

                @pl.when((mirror >= k - 1) & (mirror < LINE - 1))
                def _():
                    for copy in spread(k, place_z + (k - 1), down, 30):
                        copy.wait_send()

        return [
            stage_0,
            stage_1,
            stage_2,
            stage_3,
            stage_4,
            stage_5,
            stage_6,
            stage_7,
            stage_8,
            stage_9,
            stage_10,
        ]

    lines = [build(number, piece) for number, piece in enumerate(pieces)]
    groups = [lines[i : i + GROUP] for i in range(0, len(lines), GROUP)]
    depth = len(lines[0])
    for j in range(min(AHEAD, len(groups))):
        for line in groups[j]:
            line[0]()
    late = depth - 2
    for tick in range(len(groups) + depth - 1):
        if tick + AHEAD < len(groups):
            for line in groups[tick + AHEAD]:
                line[0]()
        for job in work.pop(0) if work else ():
            job()
        active = range(max(0, tick - depth + 1), min(tick, len(groups)))
        for j in [j for j in active if tick - j < late] + [j for j in active if tick - j >= late]:
            for line in groups[j]:
                line[tick - j]()


GROUP = 2
AHEAD = 1


def sync_plan(grads, outs):
    pieces = []
    for source, (rows, cols, step_x) in enumerate(grads):
        start = 0
        for target, width, row_x, row_core, col_x, out_start in outs[source]:
            tall = min(PIECE_ROWS, rows)
            wide = min(PIECE_COLS, width)
            if width % wide:
                wide = width // 2
            for row in range(0, rows, tall):
                for col in range(0, width, wide):
                    pieces.append(
                        Piece(
                            source,
                            lambda x, row=row, a=step_x: row + x * a,
                            start + col,
                            tall,
                            wide,
                            target,
                            lambda x, core, row=row, a=row_x, b=row_core: row + x * a + core * b,
                            lambda x, c=out_start + col, a=col_x: c + x * a,
                            row_core != 0,
                            len(pieces) % CROSS_EVERY == CROSS_EVERY - 1,
                        )
                    )
            start += width
    return pieces


QUERY_BLOCK = 384
FIRST_TICKS = 8
LN_ROWS = 112
POINT_ROWS = 64


def back_kernel(pieces, sizes, fine, start, points, counts, *refs):
    replicas, given = counts
    (
        qkv,
        grad_mixed,
        segment,
        segment_row,
        normed_part,
        w_qkv,
        standard,
        inverse,
        grad_middle,
        gain,
        tokens,
        patches,
        fine_pairs,
        pos_fine,
        pos,
        rest,
    ) = refs[:16]
    early = refs[16 : 16 + given]
    refs = refs[16 + given :]
    outs, grad_embedded, refs = refs[:sizes], refs[sizes], refs[sizes + 1 :]
    (
        grad_qkv,
        grad_key,
        grad_value,
        partial,
        arrived,
        grad_w_qkv,
        grad_w_base,
        bundle,
        acc,
        land,
        land_right,
        land_left,
        sems,
        swap_sems,
        chunk_standard,
        chunk_middle,
        chunk_sems,
    ) = refs
    rows, width = standard.shape
    third = qkv.shape[1] // 3
    scale = 1.0 / math.sqrt(HD)
    low = lambda value: value.astype(jnp.bfloat16)
    blocks = range(0, rows, LN_ROWS)

    def prepare(core, place_x, sibling, remote):
        def back_rows(pair, here, keys, mask):
            column = lambda k: slice(k * third + pair * PAIR, k * third + (pair + 1) * PAIR)
            return attend_back_block(
                scale,
                qkv[here, column(0)],
                qkv[keys, column(1)],
                qkv[keys, column(2)],
                grad_mixed[here, column(0)],
                mask,
            )

        def store_qkv(pair, k, here, value):
            grad_qkv[here, k * third + pair * PAIR : k * third + (pair + 1) * PAIR] = low(value)

        def fine_job(pair, begin):
            def job():
                here = slice(begin, min(begin + QUERY_BLOCK, start))
                keys = slice(0, start)
                inside = lax.broadcasted_iota(jnp.int32, (start, here.stop - begin), 0) < fine
                grad_q, grad_k, grad_v = back_rows(pair, here, keys, inside)
                store_qkv(pair, 0, here, grad_q)
                if begin == 0:
                    grad_key[...] = grad_k
                    grad_value[...] = grad_v
                else:
                    grad_key[...] += grad_k
                    grad_value[...] += grad_v
                if here.stop == start:
                    store_qkv(pair, 1, keys, grad_key[...])
                    store_qkv(pair, 2, keys, grad_value[...])

            return job

        def coarse_job(pair):
            def job():
                here = slice(start, rows)
                same = segment[...] == segment_row[...]
                for k, value in enumerate(back_rows(pair, here, here, same)):
                    store_qkv(pair, k, here, value)

            return job

        def weight_job():
            grad_w_qkv[...] = tn(normed_part[...], grad_qkv[...])

        def partial_job():
            partial[...] = nt(grad_qkv[...], w_qkv[...])
            swap().start()

        def swap():
            return remote(partial, arrived, swap_sems.at[0], swap_sems.at[1], sibling)

        def chunk_copies(number):
            here = pl.ds(pl.multiple_of(number * LN_ROWS, 8), LN_ROWS)
            at = lax.rem(number, 2)
            return [
                pltpu.make_async_copy(standard.at[here], chunk_standard.at[at], chunk_sems.at[0, at]),
                pltpu.make_async_copy(
                    grad_middle.at[here], chunk_middle.at[at], chunk_sems.at[1, at]
                ),
            ]

        def norm_job():
            swap().wait()
            for copy in chunk_copies(0):
                copy.start()
            for k in range(3):
                bundle[points + k : points + k + 1, :] = jnp.zeros((1, width), jnp.float32)

            @pl.loop(0, len(blocks))
            def _(number):
                @pl.when(number + 1 < len(blocks))
                def _():
                    for copy in chunk_copies(number + 1):
                        copy.start()

                for copy in chunk_copies(number):
                    copy.wait()
                at = lax.rem(number, 2)
                here = pl.ds(pl.multiple_of(number * LN_ROWS, 16), LN_ROWS)
                grad = partial[here, :] + arrived[here, :]
                z = chunk_standard[at]
                up = grad * gain[...]
                mean = jnp.mean(up, axis=1, keepdims=True)
                along = jnp.mean(up * z, axis=1, keepdims=True)
                value = chunk_middle[at] + (up - mean - z * along) * inverse[here, :]
                grad_embedded[here, :] = value
                column = lambda v: jnp.sum(v, axis=0, keepdims=True)
                bundle[points : points + 1, :] += column(low(value).astype(jnp.float32))
                bundle[points + 1 : points + 2, :] += column(grad * z)
                bundle[points + 2 : points + 3, :] += column(grad)

        def base_job():
            half = grad_w_base.shape[0]
            channels = patches.shape[0]
            part = grad_w_base.shape[1] // channels
            area = 2 * part
            columns = pl.ds(pl.multiple_of(core * half, 128), half)
            stride = tokens.shape[1]
            some = low(grad_embedded[:fine, columns])
            wanted = fine_pairs[:, pl.ds(pl.multiple_of(place_x * part, 128), part)]
            for c in range(channels):
                gathered = low(tn(patches[c, :fine, :], some))
                total = tn(gathered, wanted)
                for k in range(3):
                    begin = start + k * stride
                    here = pl.ds(pl.multiple_of(c * area + place_x * part, 128), part)
                    total += tn(low(grad_embedded[begin : begin + stride, columns]), tokens[k, :, here])
                grad_w_base[:, c * part : (c + 1) * part] = total

        def bundle_job():
            gathered = tn(pos_fine[...], low(grad_embedded[:fine, :]))
            count = pos.shape[1]
            for k in range(3):
                begin = start + k * tokens.shape[1]
                gathered += tn(pos[k], low(grad_embedded[begin : begin + count, :]))
            bundle[:points, :] = gathered
            bundle[points + 3 : 2 * POINT_ROWS, :] = rest[points + 3 : 2 * POINT_ROWS, :]
            sums = jnp.sum(grad_qkv[...].astype(jnp.float32), axis=0, keepdims=True)
            bundle[points + 7 : points + 8, :third] = sums[:, :third]
            bundle[points + 7 : points + 8, third : 2 * third] = sums[:, 2 * third :]

        heads = []
        for pair in range(third // PAIR):
            heads += [fine_job(pair, begin) for begin in range(0, start, QUERY_BLOCK)]
            heads.append(coarse_job(pair))
        ticks = FIRST_TICKS
        parts = [heads[len(heads) * k // ticks : len(heads) * (k + 1) // ticks] for k in range(ticks)]
        parts[-1] = parts[-1] + [weight_job]
        return parts + [[partial_job], [norm_job], [base_job], [bundle_job]]

    move_pieces(
        pieces,
        1.0 / replicas,
        list(early) + [grad_w_qkv, grad_w_base, bundle],
        outs,
        acc,
        land,
        land_right,
        land_left,
        sems,
        prepare,
    )


def back_and_sync(
    qkv,
    grad_mixed,
    segment,
    segment_row,
    normed_part,
    w_qkv,
    standard,
    inverse,
    grad_middle,
    gain,
    tokens,
    patches,
    fine_pairs,
    pos_fine,
    pos,
    rest,
    early,
    out_shapes,
    grads,
    outs,
    fine,
    start,
    replicas,
):
    rows, width = standard.shape
    channels = patches.shape[0]
    pieces = sync_plan(grads, outs)
    count = len(pieces)
    high = max(p.rows for p in pieces)
    wide = max(p.cols for p in pieces)
    points = pos.shape[2]
    kernel = functools.partial(
        back_kernel, pieces, len(out_shapes), fine, start, points, (replicas, len(early))
    )
    f32 = lambda *dims: pltpu.VMEM(dims, jnp.float32)
    anywhere = pl.BlockSpec(memory_space=pl.ANY)
    results = pl.pallas_call(
        kernel,
        out_shape=[jax.ShapeDtypeStruct(s, jnp.float32) for s in out_shapes]
        + [jax.ShapeDtypeStruct((rows, width), jnp.float32)],
        in_specs=[VMEM] * 6
        + [anywhere, VMEM, anywhere]
        + [VMEM] * 7
        + [anywhere] * len(early),
        out_specs=[anywhere] * len(out_shapes) + [VMEM],
        scratch_shapes=[
            pltpu.VMEM(qkv.shape, jnp.bfloat16),
            f32(start, PAIR),
            f32(start, PAIR),
            f32(rows, width),
            f32(rows, width),
            f32(width // 2, qkv.shape[1]),
            f32(width // 2, channels * fine_pairs.shape[1] // 2),
            f32(2 * POINT_ROWS, width),
            f32(count, high // 2, wide),
            f32(count, high // 2, wide),
            f32(count, LINE - 1, high // 8, wide),
            f32(count, LINE - 1, high // 8, wide),
            pltpu.SemaphoreType.DMA((count, SEMS + 2)),
            pltpu.SemaphoreType.DMA((2,)),
            f32(2, LN_ROWS, width),
            f32(2, LN_ROWS, width),
            pltpu.SemaphoreType.DMA((2, 2)),
        ],
        compiler_params=pltpu.CompilerParams(
            collective_id=0, has_side_effects=True, vmem_limit_bytes=63 << 20
        ),
        name="back_and_sync",
    )(
        qkv,
        grad_mixed,
        segment,
        segment_row,
        normed_part,
        w_qkv,
        standard,
        inverse,
        grad_middle,
        gain,
        tokens,
        patches,
        fine_pairs,
        pos_fine,
        pos,
        rest,
        *early,
    )
    return results[:-1], results[-1]


def tensor_sum(partial):
    return partial + lax.ppermute(partial, "tensor", [(0, 1), (1, 0)])


def swap_cores(value):
    return lax.ppermute(value, "tensor", [(0, 1), (1, 0)])


def merged_rows(fine_rows, light_rows, second, counts, start, stride, rows):
    width = fine_rows.shape[1]
    keep = jnp.arange(stride, dtype=jnp.int32)[:, None]
    fine = fine_rows.shape[0]
    padded = jnp.pad(light_rows, ((0, stride), (0, 0)))
    third = padded[:stride]
    fourth = lax.dynamic_slice_in_dim(padded, counts[2], stride, axis=0)
    blocks = [
        jnp.pad(fine_rows, ((0, start - fine), (0, 0))),
        jnp.pad(second, ((0, stride - second.shape[0]), (0, 0))),
        jnp.where(keep < counts[2], third, 0.0),
        jnp.where(keep < counts[3], fourth, 0.0),
        jnp.zeros((rows - start - 3 * stride, width), fine_rows.dtype),
    ]
    return jnp.concatenate(blocks, axis=0)


def own_rows(merged, is_fine, counts, fine, start, stride, rows):
    width = merged.shape[1]
    coarse = counts[1]
    heavy = jnp.concatenate(
        [
            merged[:fine],
            merged[start : start + stride],
            jnp.zeros((rows - fine - stride, width), merged.dtype),
        ],
        axis=0,
    )
    row = jnp.arange(rows, dtype=jnp.int32)[:, None]
    third = jnp.pad(merged[start + stride : start + 2 * stride], ((0, rows - stride), (0, 0)))
    fourth = jnp.pad(merged[start + 2 * stride : start + 3 * stride], ((stride, rows), (0, 0)))
    fourth = lax.dynamic_slice_in_dim(fourth, stride - counts[2], rows, axis=0)
    light = jnp.where(row < counts[2], third, fourth)
    used = jnp.where(is_fine, fine + coarse, counts[2] + counts[3])
    return jnp.where(row < used, jnp.where(is_fine, heavy, light), jnp.zeros_like(heavy))


def local(
    pixels,
    patch_size,
    counts,
    offsets,
    resize_table,
    pos_table,
    w_base,
    patch_bias,
    pos_base,
    gain_one,
    shift_one,
    w_query,
    bias_query,
    w_key,
    w_value,
    bias_value,
    w_out,
    bias_out,
    gain_two,
    shift_two,
    w_up,
    bias_up,
    w_down,
    bias_down,
    cotangent,
):
    wide = lambda value: value.astype(jnp.float32)
    images, channels, res, _ = pixels.shape
    rows_total = cotangent.shape[0]
    replicas = lax.axis_size("dp")
    core = lax.axis_index("tensor")
    side_x = lax.rem(lax.axis_index("dp"), 2)
    fine = (res // FINE) ** 2
    small = (res // COARSE[0]) ** 2
    start = up_to(fine, 16)
    stride = up_to(small, 8)
    rows = up_to(start + 3 * stride, 16)

    there = [(i, i ^ 1) for i in range(replicas)]
    other_sizes = lax.ppermute(patch_size, "dp", there)
    own_pix = jnp.pad(wide(pixels), ((0, 0), (0, 0), (0, 0), (0, -res % 128)))
    direct = lax.ppermute(
        lax.dynamic_index_in_dim(own_pix, core, 0, keepdims=False), "dp", there
    )
    half_rows = rows_total // 2
    own_cotangent = wide(cotangent)
    cot_half = lax.dynamic_slice_in_dim(own_cotangent, core * half_rows, half_rows, axis=0)
    w_qkv = jnp.concatenate([w_query, w_key, w_value], axis=1)
    bias_qkv = jnp.concatenate([bias_query, jnp.zeros_like(bias_query), bias_value])
    pos_fine = pos_table[res // FINE, :fine]
    pos_coarse = pos_table[:, :stride]
    direct, other_sizes, cot_half, w_qkv, bias_qkv, pos_fine, pos_coarse = (
        lax.optimization_barrier(
            (direct, other_sizes, cot_half, w_qkv, bias_qkv, pos_fine, pos_coarse)
        )
    )
    across = swap_cores(direct)
    cot_direct = lax.ppermute(cot_half, "dp", there)
    is_fine = patch_size[0] == FINE
    fine_first = is_fine.astype(jnp.int32)
    sizes = jnp.where(
        is_fine,
        jnp.concatenate([patch_size, other_sizes]),
        jnp.concatenate([other_sizes, patch_size]),
    )
    slots = jnp.stack([0 * core, 0 * core + 1, core, 1 - core]) + 2 * jnp.stack(
        [1 - fine_first] * 2 + [fine_first] * 2
    )
    counts4 = (res // sizes) ** 2
    (
        embedded,
        standard_one,
        inverse_one,
        normed_one,
        tokens,
        patches,
        mixed_weight,
        fine_pairs,
        pos,
        segment,
        segment_row,
    ) = embed(
        sizes,
        slots,
        resize_table,
        pos_fine,
        pos_coarse,
        w_base,
        [wide(patch_bias)[None], wide(gain_one)[None], wide(shift_one)[None]],
        pos_base,
        [own_pix, direct, across],
        rows,
    )
    qkv = (
        jnp.dot(normed_one, w_qkv, preferred_element_type=jnp.float32) + wide(bias_qkv)
    ).astype(jnp.bfloat16)
    qkv, cot_direct = lax.optimization_barrier((qkv, cot_direct))
    cot_across = swap_cores(cot_direct)
    mixed = attend(qkv, segment, segment_row, fine, start)
    mixed, cot_across = lax.optimization_barrier((mixed, cot_across))
    attended = tensor_sum(jnp.dot(mixed, w_out, preferred_element_type=jnp.float32)) + wide(
        bias_out
    )
    middle = embedded + attended
    standard_two, standard_back_two = jax.vjp(standardize, middle)
    normed_two = (standard_two * wide(gain_two) + wide(shift_two)).astype(jnp.bfloat16)
    hidden = jnp.dot(normed_two, w_up, preferred_element_type=jnp.float32) + wide(bias_up)
    activated_wide, gelu_back = jax.vjp(jax.nn.gelu, hidden)
    activated = activated_wide.astype(jnp.bfloat16)
    branch = tensor_sum(jnp.dot(activated, w_down, preferred_element_type=jnp.float32)) + wide(
        bias_down
    )
    output = own_rows(
        (middle + branch).astype(jnp.bfloat16), is_fine, counts4, fine, start, stride, rows_total
    )
    other_cotangent = jnp.where(
        core == 0,
        jnp.concatenate([cot_direct, cot_across]),
        jnp.concatenate([cot_across, cot_direct]),
    )
    fine_cotangent = jnp.where(is_fine, own_cotangent, other_cotangent)
    light_cotangent = jnp.where(
        is_fine, other_cotangent[: 2 * stride], own_cotangent[: 2 * stride]
    )
    grad_out = (
        merged_rows(
            fine_cotangent[:fine],
            light_cotangent,
            fine_cotangent[fine : fine + small],
            counts4,
            start,
            stride,
            rows,
        )
    )
    grad_branch = grad_out.astype(jnp.bfloat16)
    own_part = lambda value: lax.dynamic_slice_in_dim(
        value, side_x * (value.shape[1] // 2), value.shape[1] // 2, axis=1
    )
    grad_w_down = jnp.einsum(
        "tf,td->fd", own_part(activated), grad_branch, preferred_element_type=jnp.float32
    )
    grad_activated = jnp.einsum(
        "td,fd->tf", grad_branch, w_down, preferred_element_type=jnp.float32
    )
    grad_hidden = gelu_back(grad_activated)[0].astype(jnp.bfloat16)
    grad_w_up = jnp.einsum(
        "td,tf->df", own_part(normed_two), grad_hidden, preferred_element_type=jnp.float32
    )
    grad_bias_up = jnp.sum(grad_hidden, axis=0, dtype=jnp.float32)
    grad_normed_two = tensor_sum(
        jnp.einsum("tf,df->td", grad_hidden, w_up, preferred_element_type=jnp.float32)
    )
    grad_middle = grad_out + standard_back_two(grad_normed_two * wide(gain_two))[0]
    grad_attended = grad_middle.astype(jnp.bfloat16)
    grad_w_out = jnp.einsum(
        "te,td->ed", own_part(mixed), grad_attended, preferred_element_type=jnp.float32
    )
    grad_mixed = jnp.einsum(
        "td,ed->te", grad_attended, w_out, preferred_element_type=jnp.float32
    ).astype(jnp.bfloat16)
    points = pos.shape[2]
    width = grad_attended.shape[1]
    bundle = jnp.concatenate(
        [
            jnp.zeros((points + 3, width), jnp.float32),
            jnp.sum(grad_attended, axis=0, dtype=jnp.float32)[None],
            jnp.sum(grad_normed_two * standard_two, axis=0)[None],
            jnp.sum(grad_normed_two, axis=0)[None],
            jnp.sum(grad_branch, axis=0, dtype=jnp.float32)[None],
            jnp.zeros((1, width), jnp.float32),
            grad_bias_up.reshape(-1, width),
        ],
        axis=0,
    )
    used = bundle.shape[0]
    bundle = jnp.pad(bundle, ((0, 2 * POINT_ROWS - used), (0, 0)))
    early = [grad_w_down, grad_w_up, grad_w_out]
    area = w_base.shape[1] // channels
    ff = w_down.shape[0]
    deep = w_up.shape[0]
    cut = bias_query.shape[0]
    out_shapes = [
        w_base.shape,
        w_down.shape,
        w_up.shape,
        w_query.shape,
        w_key.shape,
        w_value.shape,
        w_out.shape,
        bundle.shape,
    ]
    grads = [
        (ff // 2, width, 0),
        (deep // 2, ff, 0),
        (cut // 2, width, 0),
        (deep // 2, 3 * cut, 0),
        (width // 2, w_base.shape[1] // 2, 0),
        (POINT_ROWS, width, POINT_ROWS),
    ]
    outs = [
        [(1, width, ff // 2, 0, 0, 0)],
        [(2, ff, deep // 2, 0, 0, 0)],
        [(6, width, cut // 2, 0, 0, 0)],
        [(3 + k, cut, deep // 2, 0, 0, 0) for k in range(3)],
        [(0, area // 2, 0, width // 2, area // 2, area * c) for c in range(channels)],
        [(7, width, POINT_ROWS, 0, 0, 0)],
    ]
    synced, grad_embedded = back_and_sync(
        qkv,
        grad_mixed,
        segment,
        segment_row,
        own_part(normed_one),
        w_qkv,
        standard_one,
        inverse_one,
        grad_middle,
        wide(gain_one)[None],
        tokens,
        patches,
        fine_pairs,
        pos_fine,
        pos,
        bundle,
        early,
        out_shapes,
        grads,
        outs,
        fine,
        start,
        replicas,
    )
    beyond = replicas // 16
    step = 1
    while step < beyond:
        swap = [(i, (i // 16 ^ step) * 16 + i % 16) for i in range(replicas)]
        synced = [part + lax.ppermute(part, "dp", swap) for part in synced]
        step *= 2
    pixel_grad = pixel_back(
        sizes,
        is_fine.astype(jnp.int32)[None],
        grad_embedded,
        resize_table,
        w_base,
        mixed_weight,
        pixels.shape,
    )
    base_s, down_s, up_s, query_s, key_s, value_s, out_s, small_s = synced
    line = lambda k: small_s[points + k]
    return (
        output,
        pixel_grad,
        base_s,
        line(0),
        small_s[:points].T,
        line(1),
        line(2),
        query_s,
        line(7)[:cut],
        key_s,
        value_s,
        line(7)[cut:],
        out_s,
        line(3),
        line(4),
        line(5),
        up_s,
        small_s[points + 8 : used].reshape(-1),
        down_s,
        line(6),
    )


def solution(mesh):
    in_specs = (
        P("dp", None, None, None),
        P("dp"),
        P("dp"),
        P("dp"),
        P(),
        P(),
        P(),
        P(),
        P(),
        P(),
        P(),
        P(None, "tensor"),
        P("tensor"),
        P(None, "tensor"),
        P(None, "tensor"),
        P("tensor"),
        P("tensor", None),
        P(),
        P(),
        P(),
        P(None, "tensor"),
        P("tensor"),
        P("tensor", None),
        P(),
        P("dp", None),
    )
    out_specs = (
        P("dp", None),
        P("dp", None, None, None),
        P(),
        P(),
        P(),
        P(),
        P(),
        P(None, "tensor"),
        P("tensor"),
        P(None, "tensor"),
        P(None, "tensor"),
        P("tensor"),
        P("tensor", None),
        P(),
        P(),
        P(),
        P(None, "tensor"),
        P("tensor"),
        P("tensor", None),
        P(),
    )
    return jax.shard_map(local, mesh=mesh, in_specs=in_specs, out_specs=out_specs, check_vma=False)
```

```python
import functools
import math

import jax
import jax.numpy as jnp
from jax import lax
from jax.experimental import pallas as pl
from jax.experimental.pallas import tpu as pltpu
from jax.sharding import PartitionSpec as P

HD = 64
VMEM = pl.BlockSpec(memory_space=pltpu.VMEM)
SMEM = pl.BlockSpec(memory_space=pltpu.SMEM)


def standardize(values):
    centered = values - jnp.mean(values, axis=-1, keepdims=True)
    spread = jnp.mean(centered * centered, axis=-1, keepdims=True)
    return centered * lax.rsqrt(spread + 1e-06)


FINE = 8
COARSE = (24, 30, 40, 48)
NORM_ROWS = 112


def nt(left, right):
    return lax.dot_general(left, right, (((1,), (1,)), ((), ())), preferred_element_type=jnp.float32)


def tn(left, right):
    return lax.dot_general(left, right, (((0,), (0,)), ((), ())), preferred_element_type=jnp.float32)


def nn(left, right):
    return jnp.dot(left, right, preferred_element_type=jnp.float32)


def up_to(value, step):
    return value + -value % step


def loop(count, body, unroll):
    if unroll:
        for i in range(count):
            body(i)
    else:
        pl.loop(0, count)(body)


def aligned(start, side):
    return pl.multiple_of(start, 8) if side % 8 == 0 and not isinstance(start, int) else start


def fill_pairs(pair, long, table, side):
    base = table.shape[1]
    entry = lax.broadcasted_iota(jnp.int32, (base, base * base), 0)
    place = lax.broadcasted_iota(jnp.int32, (base, base * base), 1)
    repeat = (place // base == entry).astype(jnp.bfloat16)
    tile = (place % base == entry).astype(jnp.bfloat16)
    wide = nn(table, repeat)[:side]
    long[...] = nn(table, tile)

    def one(s):
        pair[pl.ds(aligned(s * side, side), side), :] = wide * long[pl.ds(s, 1), :]

    loop(side, one, side % 8 != 0)


def cut_patches(line, pix, image, channel, side, grid, res):
    def one(x):
        block = pix[image, channel, pl.ds(aligned(x * side, side), side), :]
        line[pl.ds(aligned(x * res, 8), res), :side] = block.T[:res]

    loop(grid, one, True)
    return jnp.concatenate(
        [line[pl.ds(s, grid * grid, stride=side), :side] for s in range(side)], axis=1
    ).astype(jnp.bfloat16)


def place_patches(line, pixel_grad, image, channel, patch, side, grid, res):
    for s in range(side):
        line[pl.ds(s, grid * grid, stride=side), :side] = patch[:, s * side : (s + 1) * side]

    def one(x):
        block = line[pl.ds(aligned(x * res, 8), res), :side]
        pixel_grad[image, channel, pl.ds(aligned(x * side, side), side), :] = block.T

    loop(grid, one, True)


def embed_kernel(
    sizes,
    slots,
    table,
    pos_fine,
    pos_all,
    weight,
    bias,
    pos_base,
    gain,
    shift,
    own,
    direct,
    across,
    emb,
    standard,
    inverse,
    normed,
    tokens,
    patches,
    mixed_weight,
    fine_pairs,
    pos,
    segment,
    segment_row,
    pix,
    line,
    pair,
    long,
    sems,
):
    area = table.shape[2] ** 2
    channels, res = pix.shape[1:3]
    grid = res // FINE
    count = grid * grid
    start = up_to(count, 16)
    stride = tokens.shape[1]
    low = jnp.bfloat16
    copies = [
        pltpu.make_async_copy(source, pix.at[slots[k]], sems.at[k])
        for k, source in enumerate((own.at[0], own.at[1], direct, across))
    ]
    for copy in copies:
        copy.start()
    emb[...] = jnp.broadcast_to(bias[...], emb.shape)
    tokens[...] = jnp.zeros_like(tokens)
    fill_pairs(pair, long, table[FINE], FINE)
    fine_pairs[...] = pair[: FINE * FINE, :].astype(low)
    emb[:count, :] += nt(pos_fine[...], pos_base[...])
    for target, axis in ((segment, 0), (segment_row, 1)):
        row = lax.broadcasted_iota(jnp.int32, target.shape, axis)
        found = jnp.full(target.shape, 4, jnp.int32)
        for k in range(1, 4):
            side = res // sizes[k]
            within = row - (k - 1) * stride
            found = jnp.where((within >= 0) & (within < side * side), k, found)
        target[...] = found
    for copy in copies:
        copy.wait()

    for c in range(channels):
        columns = slice(c * area, (c + 1) * area)
        patch = cut_patches(line, pix, 0, c, FINE, grid, res)
        mixed = nt(fine_pairs[...], weight[:, columns]).astype(low)
        mixed_weight[c] = mixed
        patches[c, :count, :] = patch
        emb[:count, :] += nn(patch, mixed)

    @pl.loop(1, 4)
    def _(slot):
        row = pl.multiple_of(start + (slot - 1) * stride, 8)
        for side in COARSE:
            grid = res // side
            count = grid * grid

            @pl.when(sizes[slot] == side)
            def _():
                fill_pairs(pair, long, table[side], side)
                here = pl.ds(row, count)
                pos[slot - 1] = pos_all[grid]
                emb[here, :] += nt(pos_all[grid, :count, :], pos_base[...])
                for c in range(channels):
                    columns = slice(c * area, (c + 1) * area)
                    patch = cut_patches(line, pix, slot, c, side, grid, res)
                    token = nn(patch, pair[: side * side, :].astype(low)).astype(low)
                    tokens[slot - 1, :count, columns] = token
                    emb[here, :] += nt(token, weight[:, columns])

    @pl.loop(0, emb.shape[0] // NORM_ROWS)
    def _(i):
        here = pl.ds(pl.multiple_of(i * NORM_ROWS, 16), NORM_ROWS)
        value = emb[here, :]
        centered = value - jnp.mean(value, axis=1, keepdims=True)
        scale = lax.rsqrt(jnp.mean(centered * centered, axis=1, keepdims=True) + 1e-06)
        standard[here, :] = centered * scale
        inverse[here, :] = scale
        normed[here, :] = (centered * scale * gain[...] + shift[...]).astype(low)


def embed(sizes, slots, table, pos_fine, pos_all, w_base, rows_of, pos_base, pixels, rows):
    own = pixels[0]
    _, channels, res, lanes = own.shape
    width, features = w_base.shape
    fine = (res // FINE) ** 2
    side = table.shape[1]
    area = features // channels
    stride = pos_all.shape[1]
    rest = rows - up_to(fine, 16)
    shape = jax.ShapeDtypeStruct
    return pl.pallas_call(
        embed_kernel,
        out_shape=[
            shape((rows, width), jnp.float32),
            shape((rows, width), jnp.float32),
            shape((rows, 1), jnp.float32),
            shape((rows, width), jnp.bfloat16),
            shape((3, stride, features), jnp.bfloat16),
            shape((channels, up_to(fine, 16), FINE * FINE), jnp.bfloat16),
            shape((channels, FINE * FINE, width), jnp.bfloat16),
            shape((FINE * FINE, area), jnp.bfloat16),
            shape((3,) + pos_all.shape[1:], jnp.bfloat16),
            shape((rest, 1), jnp.int32),
            shape((1, rest), jnp.int32),
        ],
        in_specs=[SMEM] * 2 + [VMEM] * 8 + [pl.BlockSpec(memory_space=pl.ANY)] * 3,
        out_specs=[VMEM] * 11,
        scratch_shapes=[
            pltpu.VMEM((4, channels, res, lanes), jnp.float32),
            pltpu.VMEM((res * res // FINE, 128), jnp.float32),
            pltpu.VMEM((side * side, area), jnp.float32),
            pltpu.VMEM((side, area), jnp.float32),
            pltpu.SemaphoreType.DMA((4,)),
        ],
        compiler_params=pltpu.CompilerParams(vmem_limit_bytes=56 << 20),
        name="embed",
    )(sizes, slots, table, pos_fine, pos_all, w_base, rows_of[0], pos_base, *rows_of[1:], *pixels)


def pixel_kernel(sizes, is_fine, grad, table, weight, mixed_weight, pixel_grad, line, pair, long):
    area = table.shape[2] ** 2
    channels, res = pixel_grad.shape[1:3]
    start = up_to((res // FINE) ** 2, 16)
    stride = up_to((res // COARSE[0]) ** 2, 8)
    low = jnp.bfloat16

    @pl.when(is_fine[0] == 1)
    def _():
        grid = res // FINE
        count = grid * grid
        for c in range(channels):
            patch = nt(grad[:count, :].astype(low), mixed_weight[c])
            place_patches(line, pixel_grad, 0, c, patch, FINE, grid, res)

    @pl.loop(1, 4)
    def _(slot):
        row = pl.multiple_of(start + (slot - 1) * stride, 8)
        wanted = jnp.where(slot == 1, is_fine[0], 1 - is_fine[0])
        image = jnp.where(slot == 1, 1, slot - 2)
        for side in COARSE:
            grid = res // side
            count = grid * grid

            @pl.when((sizes[slot] == side) & (wanted == 1))
            def _():
                fill_pairs(pair, long, table[side], side)
                rows = grad[pl.ds(row, count), :].astype(low)

                @pl.loop(0, channels)
                def _(c):
                    columns = pl.ds(pl.multiple_of(c * area, area), area)
                    token = nn(rows, weight[:, columns]).astype(low)
                    patch = nt(token, pair[: side * side, :].astype(low))
                    place_patches(line, pixel_grad, image, c, patch, side, grid, res)


def pixel_back(sizes, is_fine, grad, table, w_base, mixed_weight, shape):
    _, channels, res, _ = shape
    width, features = w_base.shape
    side = table.shape[1]
    return pl.pallas_call(
        pixel_kernel,
        out_shape=jax.ShapeDtypeStruct(shape, jnp.float32),
        in_specs=[SMEM] * 2 + [VMEM] * 4,
        out_specs=VMEM,
        scratch_shapes=[
            pltpu.VMEM((res * res // FINE, 128), jnp.float32),
            pltpu.VMEM((side * side, features // channels), jnp.float32),
            pltpu.VMEM((side, features // channels), jnp.float32),
        ],
        compiler_params=pltpu.CompilerParams(vmem_limit_bytes=40 << 20),
        name="pixel_back",
    )(sizes, is_fine, grad, table, w_base, mixed_weight)


PAIR = 2 * HD


def pair_halves(rows):
    lane = lax.broadcasted_iota(jnp.int32, (rows, PAIR), 1)
    return [lane < HD, lane >= HD]


def attend_block(scale, query, key, value, mask):
    halves = pair_halves(query.shape[0])
    both = []
    for h in range(2):
        own = jnp.where(halves[h], query, jnp.zeros_like(query))
        scores = jnp.where(mask, nt(own, key) * scale, -1000000000.0)
        weights = jnp.exp(scores - jnp.max(scores, axis=1, keepdims=True))
        inverse = 1.0 / jnp.sum(weights, axis=1, keepdims=True)
        both.append(nn((weights * inverse).astype(jnp.bfloat16), value))
    return jnp.where(halves[0], both[0], both[1]).astype(jnp.bfloat16)


def block_masks(fine, start, rows, segment, segment_row, axis):
    inside = lax.broadcasted_iota(jnp.int32, (start, start), axis) < fine
    same = segment[...] == segment_row[...]
    return inside, same


def attend_kernel(scale, fine, start, query, key, value, segment, segment_row, mixed):
    rows = query.shape[0]
    masks = block_masks(fine, start, rows, segment, segment_row, 1)
    for here, mask in zip((slice(0, start), slice(start, rows)), masks):
        mixed[here, :] = attend_block(scale, query[here, :], key[here, :], value[here, :], mask)


def attend(qkv, segment, segment_row, fine, start):
    rows, width = qkv.shape
    heads = width // 3 // PAIR
    kernel = functools.partial(attend_kernel, 1.0 / math.sqrt(HD), fine, start)
    column = lambda k: pl.BlockSpec((rows, PAIR), lambda j: (0, k * heads + j))
    return pl.pallas_call(
        kernel,
        grid=(heads,),
        out_shape=jax.ShapeDtypeStruct((rows, width // 3), jnp.bfloat16),
        in_specs=[
            column(0),
            column(1),
            column(2),
            pl.BlockSpec((rows - start, 1), lambda j: (0, 0)),
            pl.BlockSpec((1, rows - start), lambda j: (0, 0)),
        ],
        out_specs=column(0),
        compiler_params=pltpu.CompilerParams(vmem_limit_bytes=48 << 20),
        name="attend",
    )(qkv, qkv, qkv, segment, segment_row)


def attend_back_block(scale, query, key, value, grad_mixed, mask):
    halves = pair_halves(query.shape[0])
    grad_query, grad_key, grad_value = [], 0.0, 0.0
    for h in range(2):
        own = jnp.where(halves[h], query, jnp.zeros_like(query))
        grad = jnp.where(halves[h], grad_mixed, jnp.zeros_like(grad_mixed))
        scores = jnp.where(mask, nt(key, own) * scale, -1000000000.0)
        weights = jnp.exp(scores - jnp.max(scores, axis=0, keepdims=True))
        probs = weights * (1.0 / jnp.sum(weights, axis=0, keepdims=True))
        grad_probs = nt(value, grad)
        inner = jnp.sum(probs * grad_probs, axis=0, keepdims=True)
        grad_scores = (probs * (grad_probs - inner)).astype(jnp.bfloat16)
        grad_value = grad_value + nn(probs.astype(jnp.bfloat16), grad)
        grad_key = grad_key + nn(grad_scores, own)
        grad_query.append(tn(grad_scores, key))
    grad_query = jnp.where(halves[0], grad_query[0], grad_query[1])
    return grad_query * scale, grad_key * scale, grad_value


LINE = 4
MESH_ID = pl.DeviceIdType.MESH
PIECE_ROWS = 192
PIECE_COLS = 384
CROSS_EVERY = 3
SEMS = 48


class Piece:
    def __init__(self, source, row, col, rows, cols, target, out_row, out_col, swap, cross):
        self.source, self.row, self.col, self.rows, self.cols = source, row, col, rows, cols
        self.target, self.out_row, self.out_col = target, out_row, out_col
        self.swap, self.cross = swap, cross


def move_pieces(pieces, scale, grads, outs, acc, land, land_right, land_left, sems, prepare):
    device = lax.axis_index("dp")
    core = lax.axis_index("tensor")
    place_x = lax.rem(device, 2)
    place_y = lax.rem(device // 2, 2)
    place_z = lax.rem(device // 4, LINE)
    mirror = LINE - 1 - place_z
    beside_x = (device + 1 - 2 * place_x, core)
    beside_y = (device + 2 - 4 * place_y, core)
    sibling = (device, 1 - core)
    up = (device + 4, core)
    down = (device - 4, core)

    barrier = pltpu.get_barrier_semaphore()
    for partner in (beside_x, beside_y, sibling):
        pl.semaphore_signal(barrier, inc=1, device_id=partner, device_id_type=MESH_ID)

    @pl.when(place_z < LINE - 1)
    def _():
        pl.semaphore_signal(barrier, inc=1, device_id=up, device_id_type=MESH_ID)

    @pl.when(place_z > 0)
    def _():
        pl.semaphore_signal(barrier, inc=1, device_id=down, device_id_type=MESH_ID)

    inner = (place_z + LINE - 1) // LINE + (2 * (LINE - 1) - place_z) // LINE
    pl.semaphore_wait(barrier, 3 + inner)

    def remote(src, dst, send, recv, where):
        return pltpu.make_async_remote_copy(
            src_ref=src,
            dst_ref=dst,
            send_sem=send,
            recv_sem=recv,
            device_id=where,
            device_id_type=MESH_ID,
        )

    work = prepare(core, place_x, sibling, remote)

    def rows_at(ref, start, size, column, width):
        return ref.at[pl.ds(pl.multiple_of(start, 8), size), pl.ds(pl.multiple_of(column, 128), width)]

    def add_rows(total, start, extra, size, width, factor=None):
        step = 24 if size % 24 == 0 else 8

        @pl.loop(0, size // step)
        def _(i):
            here = pl.ds(pl.multiple_of(start + i * step, 8), step)
            there = pl.ds(pl.multiple_of(i * step, 8), step)
            value = total[here, :width] + extra[there, :width]
            total[here, :width] = value if factor is None else value * factor

    def build(number, piece):
        half, chunk, width = piece.rows // 2, piece.rows // 8, piece.cols
        grad, out = grads[piece.source], outs[piece.target]
        mine = acc.at[number]
        sem = lambda k: sems.at[number, k]

        def out_at(x, owner, row, size):
            return rows_at(out, piece.out_row(x, owner) + row, size, piece.out_col(x), width)

        def y_copy():
            return remote(
                rows_at(grad, piece.row(place_x) + (1 - place_y) * half, half, piece.col, width),
                land.at[number, :half, :width],
                sem(0),
                sem(1),
                beside_y,
            )

        def load():
            return pltpu.make_async_copy(
                rows_at(grad, piece.row(place_x) + place_y * half, half, piece.col, width),
                mine.at[:half, :width],
                sem(2),
            )

        def right(k):
            return remote(
                rows_at(mine, (LINE - k + place_z) * chunk, chunk, 0, width),
                land_right.at[number, k - 1, :chunk, :width],
                sem(2 + k),
                sem(5 + k),
                up,
            )

        def left(k):
            return remote(
                rows_at(mine, (k - 1 - mirror) * chunk, chunk, 0, width),
                land_left.at[number, k - 1, :chunk, :width],
                sem(8 + k),
                sem(11 + k),
                down,
            )

        def got(slots, k, first, where):
            here = slots.at[number, k - 1, :chunk, :width]
            return remote(here, here, sem(first + k), sem(first + 3 + k), where)

        def send_line(k):
            @pl.when((place_z <= k - 1) & (place_z < LINE - 1))
            def _():
                right(k).start()

            @pl.when((mirror <= k - 1) & (mirror < LINE - 1))
            def _():
                left(k).start()

        def wait_line(k):
            @pl.when((place_z >= 1) & (place_z <= k))
            def _():
                got(land_right, k, 2, down).wait_recv()
                add_rows(
                    mine, (LINE - 1 - k + place_z) * chunk, land_right.at[number, k - 1], chunk, width
                )

            @pl.when((mirror >= 1) & (mirror <= k))
            def _():
                got(land_left, k, 8, up).wait_recv()
                add_rows(mine, (k - mirror) * chunk, land_left.at[number, k - 1], chunk, width)

        def own_chunk():
            return rows_at(mine, place_z * chunk, chunk, 0, width)

        def store():
            return pltpu.make_async_copy(
                own_chunk(), out_at(place_x, core, place_y * half + place_z * chunk, chunk), sem(17)
            )

        def share_out():
            return remote(
                own_chunk(),
                out_at(place_x, core, place_y * half + place_z * chunk, chunk),
                sem(15),
                sem(16),
                beside_x if piece.cross else beside_y,
            )

        def share_in():
            if piece.cross:
                there = out_at(1 - place_x, core, place_y * half + place_z * chunk, chunk)
                return remote(there, there, sem(15), sem(16), beside_x)
            there = out_at(place_x, core, (1 - place_y) * half + place_z * chunk, chunk)
            return remote(there, there, sem(15), sem(16), beside_y)

        def spread(k, position, where, first):
            copies = []
            for b in range(2):
                if piece.cross:
                    here = out_at(b, core, place_y * half + position * chunk, chunk)
                else:
                    here = out_at(place_x, core, b * half + position * chunk, chunk)
                at = first + 2 * (k - 1) + b
                copies.append(remote(here, here, sem(at), sem(at + 6), where))
            return copies

        def send_spread(k):
            @pl.when((place_z >= k - 1) & (place_z < LINE - 1))
            def _():
                for copy in spread(k, place_z - (k - 1), up, 18):
                    copy.start()

            @pl.when((mirror >= k - 1) & (mirror < LINE - 1))
            def _():
                for copy in spread(k, place_z + (k - 1), down, 30):
                    copy.start()

        def wait_spread(k):
            @pl.when(place_z >= k)
            def _():
                for copy in spread(k, place_z - k, down, 18):
                    copy.wait_recv()

            @pl.when(mirror >= k)
            def _():
                for copy in spread(k, place_z + k, up, 30):
                    copy.wait_recv()

        def last(outgoing):
            if piece.cross:
                row = (place_y if outgoing else 1 - place_y) * half
                views = [out_at(b, core, row, half) for b in range(2)]
                return [
                    remote(v, v, sem(42 + b), sem(44 + b), beside_y) for b, v in enumerate(views)
                ]
            view = out_at(place_x if outgoing else 1 - place_x, core, 0, piece.rows)
            return [remote(view, view, sem(42), sem(44), beside_x)]

        def swap(owner):
            views = [out_at(b, owner, 0, piece.rows) for b in range(2)]
            return [remote(v, v, sem(46 + b), sem(48 + b), sibling) for b, v in enumerate(views)]

        def stage_0():
            y_copy().start()
            load().start()

        def stage_1():
            load().wait()
            y_copy().wait_recv()
            add_rows(mine, 0, land.at[number], half, width)
            send_line(1)

        def stage_2():
            wait_line(1)
            send_line(2)

        def stage_3():
            wait_line(2)
            send_line(3)

        def stage_4():
            wait_line(3)

            @pl.loop(0, chunk // 8)
            def _(i):
                here = pl.ds(pl.multiple_of(place_z * chunk + i * 8, 8), 8)
                mine[here, :width] = mine[here, :width] * scale

            share_out().start()
            store().start()

        def stage_5():
            store().wait()
            share_in().wait_recv()
            send_spread(1)

        def stage_6():
            wait_spread(1)
            send_spread(2)

        def stage_7():
            wait_spread(2)
            send_spread(3)

        def stage_8():
            wait_spread(3)
            for copy in last(True):
                copy.start()

        def stage_9():
            for copy in last(False):
                copy.wait_recv()
            if piece.swap:
                for copy in swap(core):
                    copy.start()

        def stage_10():
            if piece.swap:
                for copy in swap(1 - core):
                    copy.wait_recv()
                for copy in swap(core):
                    copy.wait_send()
            y_copy().wait_send()
            share_out().wait_send()
            for copy in last(True):
                copy.wait_send()
            for k in range(1, LINE):

                @pl.when((place_z <= k - 1) & (place_z < LINE - 1))
                def _():
                    right(k).wait_send()

                @pl.when((mirror <= k - 1) & (mirror < LINE - 1))
                def _():
                    left(k).wait_send()

                @pl.when((place_z >= k - 1) & (place_z < LINE - 1))
                def _():
                    for copy in spread(k, place_z - (k - 1), up, 18):
                        copy.wait_send()

                @pl.when((mirror >= k - 1) & (mirror < LINE - 1))
                def _():
                    for copy in spread(k, place_z + (k - 1), down, 30):
                        copy.wait_send()

        return [
            stage_0,
            stage_1,
            stage_2,
            stage_3,
            stage_4,
            stage_5,
            stage_6,
            stage_7,
            stage_8,
            stage_9,
            stage_10,
        ]

    lines = [build(number, piece) for number, piece in enumerate(pieces)]
    groups = [lines[i : i + GROUP] for i in range(0, len(lines), GROUP)]
    depth = len(lines[0])
    for j in range(min(AHEAD, len(groups))):
        for line in groups[j]:
            line[0]()
    late = depth - 2
    for tick in range(len(groups) + depth - 1):
        if tick + AHEAD < len(groups):
            for line in groups[tick + AHEAD]:
                line[0]()
        for job in work.pop(0) if work else ():
            job()
        active = range(max(0, tick - depth + 1), min(tick, len(groups)))
        for j in [j for j in active if tick - j < late] + [j for j in active if tick - j >= late]:
            for line in groups[j]:
                line[tick - j]()


GROUP = 2
AHEAD = 1


def sync_plan(grads, outs):
    pieces = []
    for source, (rows, cols, step_x) in enumerate(grads):
        start = 0
        for target, width, row_x, row_core, col_x, out_start in outs[source]:
            tall = min(PIECE_ROWS, rows)
            wide = min(PIECE_COLS, width)
            if width % wide:
                wide = width // 2
            for row in range(0, rows, tall):
                for col in range(0, width, wide):
                    pieces.append(
                        Piece(
                            source,
                            lambda x, row=row, a=step_x: row + x * a,
                            start + col,
                            tall,
                            wide,
                            target,
                            lambda x, core, row=row, a=row_x, b=row_core: row + x * a + core * b,
                            lambda x, c=out_start + col, a=col_x: c + x * a,
                            row_core != 0,
                            len(pieces) % CROSS_EVERY == CROSS_EVERY - 1,
                        )
                    )
            start += width
    return pieces


QUERY_BLOCK = 384
FIRST_TICKS = 8
LN_ROWS = 112
POINT_ROWS = 64


def back_kernel(pieces, sizes, fine, start, points, counts, *refs):
    replicas, given = counts
    (
        qkv,
        grad_mixed,
        segment,
        segment_row,
        normed_part,
        w_qkv,
        standard,
        inverse,
        grad_middle,
        gain,
        tokens,
        patches,
        fine_pairs,
        pos_fine,
        pos,
        rest,
    ) = refs[:16]
    early = refs[16 : 16 + given]
    refs = refs[16 + given :]
    outs, grad_embedded, refs = refs[:sizes], refs[sizes], refs[sizes + 1 :]
    (
        grad_qkv,
        grad_key,
        grad_value,
        partial,
        arrived,
        grad_w_qkv,
        grad_w_base,
        bundle,
        acc,
        land,
        land_right,
        land_left,
        sems,
        swap_sems,
        chunk_standard,
        chunk_middle,
        chunk_sems,
    ) = refs
    rows, width = standard.shape
    third = qkv.shape[1] // 3
    scale = 1.0 / math.sqrt(HD)
    low = lambda value: value.astype(jnp.bfloat16)
    blocks = range(0, rows, LN_ROWS)

    def prepare(core, place_x, sibling, remote):
        def back_rows(pair, here, keys, mask):
            column = lambda k: slice(k * third + pair * PAIR, k * third + (pair + 1) * PAIR)
            return attend_back_block(
                scale,
                qkv[here, column(0)],
                qkv[keys, column(1)],
                qkv[keys, column(2)],
                grad_mixed[here, column(0)],
                mask,
            )

        def store_qkv(pair, k, here, value):
            grad_qkv[here, k * third + pair * PAIR : k * third + (pair + 1) * PAIR] = low(value)

        def fine_job(pair, begin):
            def job():
                here = slice(begin, min(begin + QUERY_BLOCK, start))
                keys = slice(0, start)
                inside = lax.broadcasted_iota(jnp.int32, (start, here.stop - begin), 0) < fine
                grad_q, grad_k, grad_v = back_rows(pair, here, keys, inside)
                store_qkv(pair, 0, here, grad_q)
                if begin == 0:
                    grad_key[...] = grad_k
                    grad_value[...] = grad_v
                else:
                    grad_key[...] += grad_k
                    grad_value[...] += grad_v
                if here.stop == start:
                    store_qkv(pair, 1, keys, grad_key[...])
                    store_qkv(pair, 2, keys, grad_value[...])

            return job

        def coarse_job(pair):
            def job():
                here = slice(start, rows)
                same = segment[...] == segment_row[...]
                for k, value in enumerate(back_rows(pair, here, here, same)):
                    store_qkv(pair, k, here, value)

            return job

        def weight_job():
            grad_w_qkv[...] = tn(normed_part[...], grad_qkv[...])

        def partial_job():
            partial[...] = nt(grad_qkv[...], w_qkv[...])
            swap().start()

        def swap():
            return remote(partial, arrived, swap_sems.at[0], swap_sems.at[1], sibling)

        def chunk_copies(number):
            here = pl.ds(pl.multiple_of(number * LN_ROWS, 8), LN_ROWS)
            at = lax.rem(number, 2)
            return [
                pltpu.make_async_copy(standard.at[here], chunk_standard.at[at], chunk_sems.at[0, at]),
                pltpu.make_async_copy(
                    grad_middle.at[here], chunk_middle.at[at], chunk_sems.at[1, at]
                ),
            ]

        def norm_job():
            swap().wait()
            for copy in chunk_copies(0):
                copy.start()
            for k in range(3):
                bundle[points + k : points + k + 1, :] = jnp.zeros((1, width), jnp.float32)

            @pl.loop(0, len(blocks))
            def _(number):
                @pl.when(number + 1 < len(blocks))
                def _():
                    for copy in chunk_copies(number + 1):
                        copy.start()

                for copy in chunk_copies(number):
                    copy.wait()
                at = lax.rem(number, 2)
                here = pl.ds(pl.multiple_of(number * LN_ROWS, 16), LN_ROWS)
                grad = partial[here, :] + arrived[here, :]
                z = chunk_standard[at]
                up = grad * gain[...]
                mean = jnp.mean(up, axis=1, keepdims=True)
                along = jnp.mean(up * z, axis=1, keepdims=True)
                value = chunk_middle[at] + (up - mean - z * along) * inverse[here, :]
                grad_embedded[here, :] = value
                column = lambda v: jnp.sum(v, axis=0, keepdims=True)
                bundle[points : points + 1, :] += column(low(value).astype(jnp.float32))
                bundle[points + 1 : points + 2, :] += column(grad * z)
                bundle[points + 2 : points + 3, :] += column(grad)

        def base_job():
            half = grad_w_base.shape[0]
            channels = patches.shape[0]
            part = grad_w_base.shape[1] // channels
            area = 2 * part
            columns = pl.ds(pl.multiple_of(core * half, 128), half)
            stride = tokens.shape[1]
            some = low(grad_embedded[:fine, columns])
            wanted = fine_pairs[:, pl.ds(pl.multiple_of(place_x * part, 128), part)]
            for c in range(channels):
                gathered = low(tn(patches[c, :fine, :], some))
                total = tn(gathered, wanted)
                for k in range(3):
                    begin = start + k * stride
                    here = pl.ds(pl.multiple_of(c * area + place_x * part, 128), part)
                    total += tn(low(grad_embedded[begin : begin + stride, columns]), tokens[k, :, here])
                grad_w_base[:, c * part : (c + 1) * part] = total

        def bundle_job():
            gathered = tn(pos_fine[...], low(grad_embedded[:fine, :]))
            count = pos.shape[1]
            for k in range(3):
                begin = start + k * tokens.shape[1]
                gathered += tn(pos[k], low(grad_embedded[begin : begin + count, :]))
            bundle[:points, :] = gathered
            bundle[points + 3 : 2 * POINT_ROWS, :] = rest[points + 3 : 2 * POINT_ROWS, :]
            sums = jnp.sum(grad_qkv[...].astype(jnp.float32), axis=0, keepdims=True)
            bundle[points + 7 : points + 8, :third] = sums[:, :third]
            bundle[points + 7 : points + 8, third : 2 * third] = sums[:, 2 * third :]

        heads = []
        for pair in range(third // PAIR):
            heads += [fine_job(pair, begin) for begin in range(0, start, QUERY_BLOCK)]
            heads.append(coarse_job(pair))
        ticks = FIRST_TICKS
        parts = [heads[len(heads) * k // ticks : len(heads) * (k + 1) // ticks] for k in range(ticks)]
        parts[-1] = parts[-1] + [weight_job]
        return parts + [[partial_job], [norm_job], [base_job], [bundle_job]]

    move_pieces(
        pieces,
        1.0 / replicas,
        list(early) + [grad_w_qkv, grad_w_base, bundle],
        outs,
        acc,
        land,
        land_right,
        land_left,
        sems,
        prepare,
    )


def back_and_sync(
    qkv,
    grad_mixed,
    segment,
    segment_row,
    normed_part,
    w_qkv,
    standard,
    inverse,
    grad_middle,
    gain,
    tokens,
    patches,
    fine_pairs,
    pos_fine,
    pos,
    rest,
    early,
    out_shapes,
    grads,
    outs,
    fine,
    start,
    replicas,
):
    rows, width = standard.shape
    channels = patches.shape[0]
    pieces = sync_plan(grads, outs)
    count = len(pieces)
    high = max(p.rows for p in pieces)
    wide = max(p.cols for p in pieces)
    points = pos.shape[2]
    kernel = functools.partial(
        back_kernel, pieces, len(out_shapes), fine, start, points, (replicas, len(early))
    )
    f32 = lambda *dims: pltpu.VMEM(dims, jnp.float32)
    anywhere = pl.BlockSpec(memory_space=pl.ANY)
    results = pl.pallas_call(
        kernel,
        out_shape=[jax.ShapeDtypeStruct(s, jnp.float32) for s in out_shapes]
        + [jax.ShapeDtypeStruct((rows, width), jnp.float32)],
        in_specs=[VMEM] * 6
        + [anywhere, VMEM, anywhere]
        + [VMEM] * 7
        + [anywhere] * len(early),
        out_specs=[anywhere] * len(out_shapes) + [VMEM],
        scratch_shapes=[
            pltpu.VMEM(qkv.shape, jnp.bfloat16),
            f32(start, PAIR),
            f32(start, PAIR),
            f32(rows, width),
            f32(rows, width),
            f32(width // 2, qkv.shape[1]),
            f32(width // 2, channels * fine_pairs.shape[1] // 2),
            f32(2 * POINT_ROWS, width),
            f32(count, high // 2, wide),
            f32(count, high // 2, wide),
            f32(count, LINE - 1, high // 8, wide),
            f32(count, LINE - 1, high // 8, wide),
            pltpu.SemaphoreType.DMA((count, SEMS + 2)),
            pltpu.SemaphoreType.DMA((2,)),
            f32(2, LN_ROWS, width),
            f32(2, LN_ROWS, width),
            pltpu.SemaphoreType.DMA((2, 2)),
        ],
        compiler_params=pltpu.CompilerParams(
            collective_id=0, has_side_effects=True, vmem_limit_bytes=63 << 20
        ),
        name="back_and_sync",
    )(
        qkv,
        grad_mixed,
        segment,
        segment_row,
        normed_part,
        w_qkv,
        standard,
        inverse,
        grad_middle,
        gain,
        tokens,
        patches,
        fine_pairs,
        pos_fine,
        pos,
        rest,
        *early,
    )
    return results[:-1], results[-1]


def tensor_sum(partial):
    return partial + lax.ppermute(partial, "tensor", [(0, 1), (1, 0)])


def swap_cores(value):
    return lax.ppermute(value, "tensor", [(0, 1), (1, 0)])


def merged_rows(fine_rows, light_rows, second, counts, start, stride, rows):
    width = fine_rows.shape[1]
    keep = jnp.arange(stride, dtype=jnp.int32)[:, None]
    fine = fine_rows.shape[0]
    padded = jnp.pad(light_rows, ((0, stride), (0, 0)))
    third = padded[:stride]
    fourth = lax.dynamic_slice_in_dim(padded, counts[2], stride, axis=0)
    blocks = [
        jnp.pad(fine_rows, ((0, start - fine), (0, 0))),
        jnp.pad(second, ((0, stride - second.shape[0]), (0, 0))),
        jnp.where(keep < counts[2], third, 0.0),
        jnp.where(keep < counts[3], fourth, 0.0),
        jnp.zeros((rows - start - 3 * stride, width), fine_rows.dtype),
    ]
    return jnp.concatenate(blocks, axis=0)


def own_rows(merged, is_fine, counts, fine, start, stride, rows):
    width = merged.shape[1]
    coarse = counts[1]
    heavy = jnp.concatenate(
        [
            merged[:fine],
            merged[start : start + stride],
            jnp.zeros((rows - fine - stride, width), merged.dtype),
        ],
        axis=0,
    )
    row = jnp.arange(rows, dtype=jnp.int32)[:, None]
    third = jnp.pad(merged[start + stride : start + 2 * stride], ((0, rows - stride), (0, 0)))
    fourth = jnp.pad(merged[start + 2 * stride : start + 3 * stride], ((stride, rows), (0, 0)))
    fourth = lax.dynamic_slice_in_dim(fourth, stride - counts[2], rows, axis=0)
    light = jnp.where(row < counts[2], third, fourth)
    used = jnp.where(is_fine, fine + coarse, counts[2] + counts[3])
    return jnp.where(row < used, jnp.where(is_fine, heavy, light), jnp.zeros_like(heavy))


def local(
    pixels,
    patch_size,
    counts,
    offsets,
    resize_table,
    pos_table,
    w_base,
    patch_bias,
    pos_base,
    gain_one,
    shift_one,
    w_query,
    bias_query,
    w_key,
    w_value,
    bias_value,
    w_out,
    bias_out,
    gain_two,
    shift_two,
    w_up,
    bias_up,
    w_down,
    bias_down,
    cotangent,
):
    wide = lambda value: value.astype(jnp.float32)
    images, channels, res, _ = pixels.shape
    rows_total = cotangent.shape[0]
    replicas = lax.axis_size("dp")
    core = lax.axis_index("tensor")
    side_x = lax.rem(lax.axis_index("dp"), 2)
    fine = (res // FINE) ** 2
    small = (res // COARSE[0]) ** 2
    start = up_to(fine, 16)
    stride = up_to(small, 8)
    rows = up_to(start + 3 * stride, 16)

    there = [(i, i ^ 1) for i in range(replicas)]
    other_sizes = lax.ppermute(patch_size, "dp", there)
    own_pix = jnp.pad(wide(pixels), ((0, 0), (0, 0), (0, 0), (0, -res % 128)))
    direct = lax.ppermute(
        lax.dynamic_index_in_dim(own_pix, core, 0, keepdims=False), "dp", there
    )
    half_rows = rows_total // 2
    own_cotangent = wide(cotangent)
    cot_half = lax.dynamic_slice_in_dim(own_cotangent, core * half_rows, half_rows, axis=0)
    w_qkv = jnp.concatenate([w_query, w_key, w_value], axis=1)
    bias_qkv = jnp.concatenate([bias_query, jnp.zeros_like(bias_query), bias_value])
    pos_fine = pos_table[res // FINE, :fine]
    pos_coarse = pos_table[:, :stride]
    norm_rows = [wide(patch_bias)[None], wide(gain_one)[None], wide(shift_one)[None]]
    direct, other_sizes, cot_half, w_qkv, bias_qkv, pos_fine, pos_coarse, norm_rows = (
        lax.optimization_barrier(
            (direct, other_sizes, cot_half, w_qkv, bias_qkv, pos_fine, pos_coarse, norm_rows)
        )
    )
    across = swap_cores(direct)
    cot_direct = lax.ppermute(cot_half, "dp", there)
    is_fine = patch_size[0] == FINE
    fine_first = is_fine.astype(jnp.int32)
    sizes = jnp.where(
        is_fine,
        jnp.concatenate([patch_size, other_sizes]),
        jnp.concatenate([other_sizes, patch_size]),
    )
    slots = jnp.stack([0 * core, 0 * core + 1, core, 1 - core]) + 2 * jnp.stack(
        [1 - fine_first] * 2 + [fine_first] * 2
    )
    counts4 = (res // sizes) ** 2
    (
        embedded,
        standard_one,
        inverse_one,
        normed_one,
        tokens,
        patches,
        mixed_weight,
        fine_pairs,
        pos,
        segment,
        segment_row,
    ) = embed(
        sizes,
        slots,
        resize_table,
        pos_fine,
        pos_coarse,
        w_base,
        norm_rows,
        pos_base,
        [own_pix, direct, across],
        rows,
    )
    qkv = (
        jnp.dot(normed_one, w_qkv, preferred_element_type=jnp.float32) + wide(bias_qkv)
    ).astype(jnp.bfloat16)
    qkv, cot_direct = lax.optimization_barrier((qkv, cot_direct))
    cot_across = swap_cores(cot_direct)
    mixed = attend(qkv, segment, segment_row, fine, start)
    mixed, cot_across = lax.optimization_barrier((mixed, cot_across))
    attended = tensor_sum(jnp.dot(mixed, w_out, preferred_element_type=jnp.float32)) + wide(
        bias_out
    )
    middle = embedded + attended
    standard_two, standard_back_two = jax.vjp(standardize, middle)
    normed_two = (standard_two * wide(gain_two) + wide(shift_two)).astype(jnp.bfloat16)
    hidden = jnp.dot(normed_two, w_up, preferred_element_type=jnp.float32) + wide(bias_up)
    activated_wide, gelu_back = jax.vjp(jax.nn.gelu, hidden)
    activated = activated_wide.astype(jnp.bfloat16)
    branch = tensor_sum(jnp.dot(activated, w_down, preferred_element_type=jnp.float32)) + wide(
        bias_down
    )
    output = own_rows(
        (middle + branch).astype(jnp.bfloat16), is_fine, counts4, fine, start, stride, rows_total
    )
    other_cotangent = jnp.where(
        core == 0,
        jnp.concatenate([cot_direct, cot_across]),
        jnp.concatenate([cot_across, cot_direct]),
    )
    fine_cotangent = jnp.where(is_fine, own_cotangent, other_cotangent)
    light_cotangent = jnp.where(
        is_fine, other_cotangent[: 2 * stride], own_cotangent[: 2 * stride]
    )
    grad_out = (
        merged_rows(
            fine_cotangent[:fine],
            light_cotangent,
            fine_cotangent[fine : fine + small],
            counts4,
            start,
            stride,
            rows,
        )
    )
    grad_branch = grad_out.astype(jnp.bfloat16)
    own_part = lambda value: lax.dynamic_slice_in_dim(
        value, side_x * (value.shape[1] // 2), value.shape[1] // 2, axis=1
    )
    grad_w_down = jnp.einsum(
        "tf,td->fd", own_part(activated), grad_branch, preferred_element_type=jnp.float32
    )
    grad_activated = jnp.einsum(
        "td,fd->tf", grad_branch, w_down, preferred_element_type=jnp.float32
    )
    grad_hidden = gelu_back(grad_activated)[0].astype(jnp.bfloat16)
    grad_w_up = jnp.einsum(
        "td,tf->df", own_part(normed_two), grad_hidden, preferred_element_type=jnp.float32
    )
    grad_bias_up = jnp.dot(
        jnp.ones((8, rows), jnp.bfloat16), grad_hidden, preferred_element_type=jnp.float32
    )[0]
    grad_normed_two = tensor_sum(
        jnp.einsum("tf,df->td", grad_hidden, w_up, preferred_element_type=jnp.float32)
    )
    grad_middle = grad_out + standard_back_two(grad_normed_two * wide(gain_two))[0]
    grad_attended = grad_middle.astype(jnp.bfloat16)
    grad_w_out = jnp.einsum(
        "te,td->ed", own_part(mixed), grad_attended, preferred_element_type=jnp.float32
    )
    grad_mixed = jnp.einsum(
        "td,ed->te", grad_attended, w_out, preferred_element_type=jnp.float32
    ).astype(jnp.bfloat16)
    points = pos.shape[2]
    width = grad_attended.shape[1]
    bundle = jnp.concatenate(
        [
            jnp.zeros((points + 3, width), jnp.float32),
            jnp.sum(grad_attended, axis=0, dtype=jnp.float32)[None],
            jnp.sum(grad_normed_two * standard_two, axis=0)[None],
            jnp.sum(grad_normed_two, axis=0)[None],
            jnp.sum(grad_branch, axis=0, dtype=jnp.float32)[None],
            jnp.zeros((1, width), jnp.float32),
            grad_bias_up.reshape(-1, width),
        ],
        axis=0,
    )
    used = bundle.shape[0]
    bundle = jnp.pad(bundle, ((0, 2 * POINT_ROWS - used), (0, 0)))
    early = [grad_w_down, grad_w_up, grad_w_out]
    area = w_base.shape[1] // channels
    ff = w_down.shape[0]
    deep = w_up.shape[0]
    cut = bias_query.shape[0]
    out_shapes = [
        w_base.shape,
        w_down.shape,
        w_up.shape,
        w_query.shape,
        w_key.shape,
        w_value.shape,
        w_out.shape,
        bundle.shape,
    ]
    grads = [
        (ff // 2, width, 0),
        (deep // 2, ff, 0),
        (cut // 2, width, 0),
        (deep // 2, 3 * cut, 0),
        (width // 2, w_base.shape[1] // 2, 0),
        (POINT_ROWS, width, POINT_ROWS),
    ]
    outs = [
        [(1, width, ff // 2, 0, 0, 0)],
        [(2, ff, deep // 2, 0, 0, 0)],
        [(6, width, cut // 2, 0, 0, 0)],
        [(3 + k, cut, deep // 2, 0, 0, 0) for k in range(3)],
        [(0, area // 2, 0, width // 2, area // 2, area * c) for c in range(channels)],
        [(7, width, POINT_ROWS, 0, 0, 0)],
    ]
    synced, grad_embedded = back_and_sync(
        qkv,
        grad_mixed,
        segment,
        segment_row,
        own_part(normed_one),
        w_qkv,
        standard_one,
        inverse_one,
        grad_middle,
        wide(gain_one)[None],
        tokens,
        patches,
        fine_pairs,
        pos_fine,
        pos,
        bundle,
        early,
        out_shapes,
        grads,
        outs,
        fine,
        start,
        replicas,
    )
    beyond = replicas // 16
    step = 1
    while step < beyond:
        swap = [(i, (i // 16 ^ step) * 16 + i % 16) for i in range(replicas)]
        synced = [part + lax.ppermute(part, "dp", swap) for part in synced]
        step *= 2
    pixel_grad = pixel_back(
        sizes,
        is_fine.astype(jnp.int32)[None],
        grad_embedded,
        resize_table,
        w_base,
        mixed_weight,
        pixels.shape,
    )
    base_s, down_s, up_s, query_s, key_s, value_s, out_s, small_s = synced
    line = lambda k: small_s[points + k]
    return (
        output,
        pixel_grad,
        base_s,
        line(0),
        small_s[:points].T,
        line(1),
        line(2),
        query_s,
        line(7)[:cut],
        key_s,
        value_s,
        line(7)[cut:],
        out_s,
        line(3),
        line(4),
        line(5),
        up_s,
        small_s[points + 8 : used].reshape(-1),
        down_s,
        line(6),
    )


def solution(mesh):
    in_specs = (
        P("dp", None, None, None),
        P("dp"),
        P("dp"),
        P("dp"),
        P(),
        P(),
        P(),
        P(),
        P(),
        P(),
        P(),
        P(None, "tensor"),
        P("tensor"),
        P(None, "tensor"),
        P(None, "tensor"),
        P("tensor"),
        P("tensor", None),
        P(),
        P(),
        P(),
        P(None, "tensor"),
        P("tensor"),
        P("tensor", None),
        P(),
        P("dp", None),
    )
    out_specs = (
        P("dp", None),
        P("dp", None, None, None),
        P(),
        P(),
        P(),
        P(),
        P(),
        P(None, "tensor"),
        P("tensor"),
        P(None, "tensor"),
        P(None, "tensor"),
        P("tensor"),
        P("tensor", None),
        P(),
        P(),
        P(),
        P(None, "tensor"),
        P("tensor"),
        P("tensor", None),
        P(),
    )
    return jax.shard_map(local, mesh=mesh, in_specs=in_specs, out_specs=out_specs, check_vma=False)
```
